512 devices in a mesh: role: 2 (over z_lo), seq: 64 (over y, x, core), head: 4 (over z_hi).
Axes of the slice: x: 4, y: 8, z: 8 (z_hi: 4, z_lo: 2; z = z_hi * 2 + z_lo), core: 2. Of those that a mesh axis runs over, the one named last changes fastest.
Arguments:
- query_heads: bfloat16 [8192, 16, 128], P('seq', ('role', 'head')), may hold values from -16 to 16
- key_heads: bfloat16 [8192, 8, 128], P('seq', ('role', 'head')), may hold values from -16 to 16
- value_heads: bfloat16 [8192, 8, 128], P('seq', ('role', 'head')), may hold values from -6 to 6
- distill_proj: bfloat16 [16, 128, 1024], P(('role', 'head')), may hold values from -6 to 6
- conv_input: bfloat16 [1024, 8192], P(('role', 'head'), 'seq'), may hold values from -6 to 6
- gate_input: bfloat16 [1024, 8192], P(('role', 'head'), 'seq'), may hold values from -6 to 6
- filter_taps: float32 [1024, 8192], P(('role', 'head'), 'seq'), may hold values from -0.0625 to 0.0625
- skip_gain: float32 [1024], P(('role', 'head')), may hold values from -4 to 4
Outputs:
- grad_input: float32 [1024, 8192], P(('role', 'head'), 'seq')
- filter_step: float32 [1024, 8192], P(('role', 'head'), 'seq')
The draws below stay inside these ranges and needn't reach their ends.
All inputs are finite; a program needn't handle non-finite values.
Results may differ from the reference program's by a relative error of at most 0.005.
Values may be sent and summed in bfloat16 or wider, within the bound.
No kernel may reach another device: no remote copies, remote signals or barrier semaphores. Data moves between devices by JAX's collectives and lax.ppermute only.
A program may use at most 64 MiB of HBM per device.

```python
import math
import jax
import jax.numpy as jnp
from jax import lax

SEQ = 8192
QHEADS = 16
KV_HEADS = 8
HEAD_DIM = 128
WINDOW = 4096
CHANNELS = 1024


def draw_query_heads(key, part):
    normal_part = jnp.clip(jax.random.normal(jax.random.fold_in(key, 21), (SEQ, QHEADS, HEAD_DIM), jnp.float32), -6.0, 6.0)
    return normal_part.astype(jnp.bfloat16)


def draw_key_heads(key, part):
    normal_part = jnp.clip(jax.random.normal(jax.random.fold_in(key, 22), (SEQ, KV_HEADS, HEAD_DIM), jnp.float32), -6.0, 6.0)
    return normal_part.astype(jnp.bfloat16)


def raised(entries, own_key, source, target, shards_of, factor):
    owner, partner = [(jnp.arange(entries.shape[axis_at]) // (entries.shape[axis_at] // shards_of)).reshape([-1 if axis == axis_at else 1 for axis in range(entries.ndim)]) for axis_at in (source, target)]
    chosen = jax.random.permutation(own_key, shards_of)[partner]
    strong = (owner == chosen) | (owner == (partner + shards_of // 2) % shards_of)
    return jnp.where(strong, factor * entries, entries)


def block_levels(stream_key, dims, pieces, smallest, top_value):
    factor_of = 1.0
    for dim, shards_of in pieces:
        steps = jax.random.uniform(jax.random.fold_in(jax.random.fold_in(stream_key, 6), dim), (shards_of,), jnp.float32, smallest / len(pieces), top_value / len(pieces))
        factor_of = factor_of * jnp.repeat(jnp.exp(steps), dims[dim] // shards_of).reshape((-1,) + (1,) * (len(dims) - 1 - dim))
    return factor_of


def bell_draw(own_key, shape, scale, reach, split=(), kind=jnp.bfloat16):
    level = block_levels(own_key, shape, split, -0.22, 0.18) if split else 1.0
    drawn = jax.random.normal(own_key, shape, jnp.float32) * scale * level
    return jnp.minimum(jnp.maximum(drawn, -reach), reach).astype(kind)


def noise_with(rng, extent, scale, most, split, heavy, kind=jnp.bfloat16):
    drawn = scale * jax.random.normal(rng, extent, jnp.float32)
    if split:
        drawn = drawn * block_levels(rng, extent, split, -0.22, 0.18)
    return jnp.clip(raised(drawn, jax.random.fold_in(rng, 3), *heavy), -most, most).astype(kind)


def setup_inputs(seed: int = 0) -> dict:
    splits = jax.random.split(jax.random.key(seed), 9)
    return {
        "query_heads": draw_query_heads(jax.random.fold_in(splits[8], 71), 0),
        "key_heads": draw_key_heads(jax.random.fold_in(splits[8], 71), 0),
        "value_heads": bell_draw(splits[2], (SEQ, KV_HEADS, HEAD_DIM), 1.0, 6.0, ((0, 64), (1, 8))),
        "distill_proj": noise_with(splits[3], (QHEADS, HEAD_DIM, CHANNELS), 1.0, 6.0, ((0, 8),), (0, 2, 8, 2.0)),
        "conv_input": bell_draw(splits[4], (CHANNELS, SEQ), 1.0, 6.0, ((0, 8), (1, 64))),
        "gate_input": bell_draw(splits[5], (CHANNELS, SEQ), 1.0, 6.0, ((0, 8), (1, 64))),
        "filter_taps": bell_draw(splits[6], (CHANNELS, SEQ), SEQ ** -0.5, 0.0625, ((0, 8), (1, 64)), jnp.float32),
        "skip_gain": bell_draw(splits[7], (CHANNELS,), 1.0, 4.0, ((0, 8),), jnp.float32),
    }


def teacher_target(query_heads, key_heads, value_heads, distill_proj):
    per_group = QHEADS // KV_HEADS
    query_span = math.gcd(SEQ, 512)
    score_scale = HEAD_DIM ** -0.5
    key_pad = jnp.pad(key_heads, ((WINDOW, 0), (0, 0), (0, 0)))
    value_pad = jnp.pad(value_heads, ((WINDOW, 0), (0, 0), (0, 0)))

    def one_block(offset):
        queries = lax.dynamic_slice_in_dim(query_heads, offset, query_span, 0).astype(jnp.float32)
        queries = queries.reshape(query_span, KV_HEADS, per_group, HEAD_DIM)
        key_block = lax.dynamic_slice_in_dim(key_pad, offset, WINDOW + query_span, 0).astype(jnp.float32)
        value_block = lax.dynamic_slice_in_dim(value_pad, offset, WINDOW + query_span, 0).astype(jnp.float32)
        scores = jnp.einsum("qgae,kge->gaqk", queries, key_block) * score_scale
        query_pos = offset + jnp.arange(query_span, dtype=jnp.int32)
        key_pos = offset - WINDOW + jnp.arange(WINDOW + query_span, dtype=jnp.int32)
        in_window = (key_pos[None, :] <= query_pos[:, None]) & (key_pos[None, :] > query_pos[:, None] - WINDOW) & (key_pos[None, :] >= 0)
        row_max = jnp.max(jnp.where(in_window, scores, -jnp.inf), axis=-1, keepdims=True)
        weight = jnp.where(in_window, jnp.exp(scores - row_max), 0.0)
        row_sum = jnp.sum(weight, axis=-1)
        rounded = lax.optimization_barrier(weight.astype(jnp.bfloat16)).astype(jnp.float32)
        weighted = jnp.einsum("gaqk,kge->qgae", rounded, value_block)
        attended = weighted / jnp.transpose(row_sum, (2, 0, 1))[..., None]
        return attended.reshape(query_span, QHEADS, HEAD_DIM).astype(jnp.bfloat16)

    offsets = jnp.arange(SEQ // query_span, dtype=jnp.int32) * query_span
    attended = lax.map(one_block, offsets).reshape(SEQ, QHEADS, HEAD_DIM)
    attended = lax.optimization_barrier(attended).astype(jnp.float32)
    return jnp.einsum("the,hec->ct", attended, distill_proj.astype(jnp.float32))


def student_grads(conv_input, gate_input, filter_taps, skip_gain, target):
    full_len = 2 * SEQ

    def one_group(packed):
        signal, gate_part, taps, skip_part, aimed = packed
        signal = signal.astype(jnp.float32)
        gate_part = gate_part.astype(jnp.float32)
        input_spec = jnp.fft.rfft(signal, n=full_len, axis=-1)
        taps_spec = jnp.fft.rfft(taps, n=full_len, axis=-1)
        convolved = jnp.fft.irfft(input_spec * taps_spec, n=full_len, axis=-1)[:, :SEQ]
        output = gate_part * (convolved + skip_part[:, None] * signal)
        backed = gate_part * (output - aimed)
        back_spec = jnp.fft.rfft(backed, n=full_len, axis=-1)
        corr_input = jnp.fft.irfft(jnp.conj(taps_spec) * back_spec, n=full_len, axis=-1)[:, :SEQ]
        corr_taps = jnp.fft.irfft(jnp.conj(input_spec) * back_spec, n=full_len, axis=-1)[:, :SEQ]
        return skip_part[:, None] * backed + corr_input, corr_taps * (SEQ ** -0.5)

    chan_block = math.gcd(CHANNELS, 64)

    def folded(array):
        return array.reshape((CHANNELS // chan_block, chan_block) + array.shape[1:])

    gradients, updates = lax.map(one_group, (folded(conv_input), folded(gate_input), folded(filter_taps), folded(skip_gain), folded(target)))
    return gradients.reshape(CHANNELS, SEQ), updates.reshape(CHANNELS, SEQ)


def reference(query_heads, key_heads, value_heads, distill_proj, conv_input, gate_input, filter_taps, skip_gain):
    target = teacher_target(query_heads, key_heads, value_heads, distill_proj)
    grad_input, filter_step = student_grads(conv_input, gate_input, filter_taps, skip_gain, target)
    return (grad_input, filter_step)
```

```python
import math

import jax
import jax.numpy as jnp
import numpy as np
from jax import lax
from jax.experimental import pallas as pl
from jax.experimental.pallas import tpu as pltpu
from jax.sharding import PartitionSpec as P

WINDOW = 4096
SHARD = 128
ROW = 8
BACK = WINDOW // (ROW * SHARD)
SHARDS = 64
HALF = 72
NEG = -1e30
highest = lax.Precision.HIGHEST


def transform_tables():
    length = 2 * SHARDS * SHARD
    k1 = np.arange(HALF)[:, None]
    live = (k1 <= SHARDS).astype(np.float64)
    a = np.arange(SHARDS)[None, :]
    angle = 2.0 * np.pi * ((k1 * a) % 128) / 128
    first = np.concatenate([live * np.cos(angle), -live * np.sin(angle)], 0)
    weight = live * np.where((k1 == 0) | (k1 == SHARDS), 1.0, 2.0) / length
    last = np.concatenate([weight * np.cos(angle), -weight * np.sin(angle)], 0).T
    b = np.arange(128)[None, :]
    turn = 2.0 * np.pi * (k1 * b) / length
    b2 = np.arange(128)[:, None]
    grid = 2.0 * np.pi * ((b2 * b) % 128) / 128
    cosine, sine = np.cos(grid), np.sin(grid)
    forward = np.block([[cosine, -sine], [sine, cosine]])
    backward = np.block([[cosine, sine], [-sine, cosine]])
    return [np.asarray(t, np.float32) for t in (first, last, np.cos(turn), np.sin(turn), forward, backward)]


def mul(a, b):
    return jnp.dot(a, b, precision=highest, preferred_element_type=jnp.float32)


def to_spectra(signals, first, turn_cos, turn_sin, forward):
    stacked = mul(first, jnp.concatenate(signals, 1))
    rows = []
    for n in range(len(signals)):
        re = stacked[:HALF, n * 128 : (n + 1) * 128]
        im = stacked[HALF:, n * 128 : (n + 1) * 128]
        rows.append(jnp.concatenate([re * turn_cos + im * turn_sin, im * turn_cos - re * turn_sin], 1))
    spectra = mul(jnp.concatenate(rows, 0), forward)
    return [spectra[n * HALF : (n + 1) * HALF] for n in range(len(signals))]


def to_signals(spectra, last, turn_cos, turn_sin, backward):
    rows = mul(jnp.concatenate(spectra, 0), backward)
    columns = []
    for n in range(len(spectra)):
        re = rows[n * HALF : (n + 1) * HALF, :128]
        im = rows[n * HALF : (n + 1) * HALF, 128:]
        columns.append(jnp.concatenate([re * turn_cos - im * turn_sin, re * turn_sin + im * turn_cos], 0))
    return mul(last, jnp.concatenate(columns, 1))


def product(a, b):
    ar, ai, br, bi = a[:, :128], a[:, 128:], b[:, :128], b[:, 128:]
    return jnp.concatenate([ar * br - ai * bi, ar * bi + ai * br], 1)


def product_conj(a, b):
    ar, ai, br, bi = a[:, :128], a[:, 128:], b[:, :128], b[:, 128:]
    return jnp.concatenate([ar * br + ai * bi, ar * bi - ai * br], 1)


def before_kernel(skip_ref, in_ref, first, last, tc, ts, fwd, bwd, spec_ref, pre_ref, gate_ref):
    x = [in_ref[:, c, :] for c in (0, 1)]
    gate = [in_ref[:, c, :] for c in (2, 3)]
    taps = [in_ref[:, c, :] for c in (4, 5)]
    spectra = to_spectra(x + taps, first[...], tc[...], ts[...], fwd[...])
    for n in range(4):
        spec_ref[n] = spectra[n]
    conv = to_signals(
        [product(spectra[c], spectra[2 + c]) for c in (0, 1)], last[...], tc[...], ts[...], bwd[...]
    )
    for c in (0, 1):
        pre_ref[c] = gate[c] * (conv[:, c * 128 : (c + 1) * 128] + skip_ref[c] * x[c])
        gate_ref[c] = gate[c]


def after_kernel(skip_ref, target_ref, spec_ref, pre_ref, gate_ref, first, last, tc, ts, fwd, bwd, out_ref):
    back = [gate_ref[c] * (pre_ref[c] - target_ref[:, c, :]) for c in (0, 1)]
    spectra = to_spectra(back, first[...], tc[...], ts[...], fwd[...])
    mixed = [product_conj(spec_ref[2 + c], spectra[c]) for c in (0, 1)]
    mixed += [product_conj(spec_ref[c], spectra[c]) for c in (0, 1)]
    signals = to_signals(mixed, last[...], tc[...], ts[...], bwd[...])
    scale = (SHARDS * SHARD) ** -0.5
    for c in (0, 1):
        out_ref[:, c, :] = skip_ref[c] * back[c] + signals[:, c * 128 : (c + 1) * 128]
        out_ref[:, 2 + c, :] = scale * signals[:, (2 + c) * 128 : (3 + c) * 128]


def attend_kernel(place_ref, q_ref, kv0, kv1, kv2, kv3, kv4, out_ref):
    row, mine = place_ref[0], place_ref[1]
    theirs = pl.program_id(0)
    scale = 128 ** -0.5
    q = q_ref[0].reshape(2 * SHARD, 128)

    def scores(ref):
        return lax.dot_general(ref[0], q, (((1,), (1,)), ((), ())), preferred_element_type=jnp.float32)

    def gathered(ref, weight):
        return lax.dot_general(ref[1], weight, (((0,), (0,)), ((), ())), preferred_element_type=jnp.float32)

    key = lax.broadcasted_iota(jnp.int32, (SHARD, 2 * SHARD), 0)
    query = lax.broadcasted_iota(jnp.int32, (SHARD, 2 * SHARD), 1) % SHARD
    newest = (theirs - mine) * SHARD + query - key >= 0
    oldest = jnp.where(row >= BACK, scores(kv0), NEG)
    blocks = [jnp.where(newest, scores(kv4), oldest)]
    for r, ref in ((1, kv1), (2, kv2), (3, kv3)):
        blocks.append(jnp.where(row >= BACK - r, scores(ref), NEG))
    top = jnp.maximum(jnp.maximum(blocks[0], blocks[1]), jnp.maximum(blocks[2], blocks[3]))
    top = jnp.maximum(jnp.max(top, axis=0, keepdims=True), 0.5 * NEG)
    weights = [jnp.exp((b - top) * scale) for b in blocks]
    total = jnp.sum(weights[0] + weights[1] + weights[2] + weights[3], axis=0, keepdims=True)
    zero = jnp.zeros_like(weights[0])
    out = gathered(kv4, jnp.where(newest, weights[0], zero).astype(jnp.bfloat16))
    out += gathered(kv0, jnp.where(newest, zero, weights[0]).astype(jnp.bfloat16))
    for ref, w in zip((kv1, kv2, kv3), weights[1:]):
        out += gathered(ref, w.astype(jnp.bfloat16))
    out = out / jnp.maximum(total, 1e-30)
    log_sum = jnp.where(total > 0.0, top * scale + jnp.log(jnp.maximum(total, 1e-30)), NEG)
    high = log_sum.astype(jnp.bfloat16).astype(jnp.float32)
    rest = log_sum - high
    middle = rest.astype(jnp.bfloat16).astype(jnp.float32)
    low = rest - middle
    stats = []
    for h in (0, 1):
        out_ref[0, h * 128 : (h + 1) * 128, :] = out[:, h * 128 : (h + 1) * 128].astype(jnp.bfloat16)
        stats += [part[:, h * 128 : (h + 1) * 128] for part in (high, middle, low)]
    stats.append(jnp.zeros((10, 128), jnp.float32))
    out_ref[0, 256:272, :] = jnp.concatenate(stats, 0).astype(jnp.bfloat16)


def merge_kernel(parts_ref, proj_ref, out_ref):
    heads = []
    for h in (0, 1):
        sums = []
        for p in range(ROW):
            stats = parts_ref[p, 256:272, :].astype(jnp.float32)
            sums.append(stats[3 * h : 3 * h + 1] + stats[3 * h + 1 : 3 * h + 2] + stats[3 * h + 2 : 3 * h + 3])
        top = sums[0]
        for p in range(1, ROW):
            top = jnp.maximum(top, sums[p])
        shares = [jnp.exp(s - top) for s in sums]
        total = shares[0]
        merged = shares[0] * parts_ref[0, h * 128 : (h + 1) * 128, :].astype(jnp.float32)
        for p in range(1, ROW):
            total += shares[p]
            merged += shares[p] * parts_ref[p, h * 128 : (h + 1) * 128, :].astype(jnp.float32)
        heads.append((merged / total).astype(jnp.bfloat16))
    target = jnp.dot(proj_ref[...], jnp.concatenate(heads, 0), preferred_element_type=jnp.float32)
    out_ref[...] = target.reshape(8, 128, 128).astype(jnp.bfloat16)


VMEM = pl.BlockSpec(memory_space=pltpu.VMEM)
SMEM = pl.BlockSpec(memory_space=pltpu.SMEM)


def call_before(skip, packed, tables):
    return pl.pallas_call(
        before_kernel,
        out_shape=(
            jax.ShapeDtypeStruct((4, HALF, 256), jnp.float32),
            jax.ShapeDtypeStruct((2, SHARDS, 128), jnp.float32),
            jax.ShapeDtypeStruct((2, SHARDS, 128), jnp.float32),
        ),
        in_specs=[SMEM] + [VMEM] * 7,
        out_specs=(VMEM,) * 3,
    )(skip, packed, *tables)


def call_after(skip, target, spectra, pre, gate, tables):
    return pl.pallas_call(
        after_kernel,
        out_shape=jax.ShapeDtypeStruct((SHARDS, 4, 128), jnp.float32),
        in_specs=[SMEM] + [VMEM] * 10,
        out_specs=VMEM,
    )(skip, target, spectra, pre, gate, *tables)


def call_attend(place, queries, blocks):
    fixed = pl.BlockSpec((2, SHARD, 128), lambda p: (0, 0, 0))
    return pl.pallas_call(
        attend_kernel,
        out_shape=jax.ShapeDtypeStruct((ROW, 272, 128), jnp.bfloat16),
        grid=(ROW,),
        in_specs=[SMEM, pl.BlockSpec((1, 2, SHARD, 128), lambda p: (p, 0, 0, 0))] + [fixed] * 5,
        out_specs=pl.BlockSpec((1, 272, 128), lambda p: (p, 0, 0)),
    )(place, queries, *blocks)


def call_merge(parts, proj):
    return pl.pallas_call(
        merge_kernel,
        out_shape=jax.ShapeDtypeStruct((8, 128, 128), jnp.bfloat16),
        in_specs=[VMEM] * 2,
        out_specs=VMEM,
    )(parts, proj)


def body(
    query_heads,
    key_heads,
    value_heads,
    distill_proj,
    conv_input,
    gate_input,
    filter_taps,
    skip_gain,
):
    tables = [jnp.asarray(t) for t in transform_tables()]
    rank = lax.axis_index("seq")
    rows = [[y * ROW + p for p in range(ROW)] for y in range(SHARDS // ROW)]
    place = jnp.stack([rank // ROW, rank % ROW]).astype(jnp.int32)

    own = jnp.stack([key_heads[:, 0], value_heads[:, 0]])
    blocks = [
        lax.ppermute(own, "seq", [(i, i + ROW * k) for i in range(SHARDS - ROW * k)])
        for k in range(BACK, 0, -1)
    ] + [own]
    queries = lax.all_gather(jnp.transpose(query_heads, (1, 0, 2)), "seq", axis_index_groups=rows)

    packed = jnp.concatenate(
        [
            part.astype(jnp.float32).reshape(SHARDS, 2, 128)
            for part in (conv_input, gate_input, filter_taps)
        ],
        axis=1,
    )
    packed = lax.all_to_all(packed, "seq", 0, 0)
    skip = lax.dynamic_slice(skip_gain, (2 * rank,), (2,))
    spectra, pre, gate = call_before(skip, packed, tables)

    proj = distill_proj.reshape(256, 1024).T
    parts = call_attend(place, queries, blocks)
    parts = lax.all_to_all(parts, "seq", 0, 0, axis_index_groups=rows)
    target = call_merge(parts, proj)
    target = lax.all_to_all(target, ("role", "head"), 0, 0)
    target = jnp.sum(target.astype(jnp.float32), axis=0).reshape(SHARDS, 2, 128)
    target = lax.all_to_all(target, "seq", 0, 0)
    out = call_after(skip, target, spectra, pre, gate, tables)
    out = lax.all_to_all(out, "seq", 0, 0)
    return out[:, :2].reshape(128, 128), out[:, 2:].reshape(128, 128)


def solution(mesh):
    in_specs = (
        P("seq", ("role", "head"), None),
        P("seq", ("role", "head"), None),
        P("seq", ("role", "head"), None),
        P(("role", "head"), None, None),
        P(("role", "head"), "seq"),
        P(("role", "head"), "seq"),
        P(("role", "head"), "seq"),
        P(("role", "head")),
    )
    out_specs = (P(("role", "head"), "seq"), P(("role", "head"), "seq"))
    return jax.shard_map(body, mesh=mesh, in_specs=in_specs, out_specs=out_specs, check_vma=False)
```

```python
import math

import jax
import jax.numpy as jnp
import numpy as np
from jax import lax
from jax.experimental import pallas as pl
from jax.experimental.pallas import tpu as pltpu
from jax.sharding import PartitionSpec as P

WINDOW = 4096
SHARD = 128
ROW = 8
BACK = WINDOW // (ROW * SHARD)
SHARDS = 64
HALF = 72
NEG = -1e30
highest = lax.Precision.HIGHEST


def transform_tables():
    length = 2 * SHARDS * SHARD
    k1 = np.arange(HALF)[:, None]
    live = (k1 <= SHARDS).astype(np.float64)
    a = np.arange(SHARDS)[None, :]
    angle = 2.0 * np.pi * ((k1 * a) % 128) / 128
    first = np.concatenate([live * np.cos(angle), -live * np.sin(angle)], 0)
    weight = live * np.where((k1 == 0) | (k1 == SHARDS), 1.0, 2.0) / length
    last = np.concatenate([weight * np.cos(angle), -weight * np.sin(angle)], 0).T
    b = np.arange(128)[None, :]
    turn = 2.0 * np.pi * (k1 * b) / length
    b2 = np.arange(128)[:, None]
    grid = 2.0 * np.pi * ((b2 * b) % 128) / 128
    cosine, sine = np.cos(grid), np.sin(grid)
    forward = np.block([[cosine, -sine], [sine, cosine]])
    backward = np.block([[cosine, sine], [-sine, cosine]])
    return [np.asarray(t, np.float32) for t in (first, last, np.cos(turn), np.sin(turn), forward, backward)]


def mul(a, b):
    return jnp.dot(a, b, precision=highest, preferred_element_type=jnp.float32)


def to_spectra(signals, first, turn_cos, turn_sin, forward):
    stacked = mul(first, jnp.concatenate(signals, 1))
    rows = []
    for n in range(len(signals)):
        re = stacked[:HALF, n * 128 : (n + 1) * 128]
        im = stacked[HALF:, n * 128 : (n + 1) * 128]
        rows.append(jnp.concatenate([re * turn_cos + im * turn_sin, im * turn_cos - re * turn_sin], 1))
    spectra = mul(jnp.concatenate(rows, 0), forward)
    return [spectra[n * HALF : (n + 1) * HALF] for n in range(len(signals))]


def to_signals(spectra, last, turn_cos, turn_sin, backward):
    rows = mul(jnp.concatenate(spectra, 0), backward)
    columns = []
    for n in range(len(spectra)):
        re = rows[n * HALF : (n + 1) * HALF, :128]
        im = rows[n * HALF : (n + 1) * HALF, 128:]
        columns.append(jnp.concatenate([re * turn_cos - im * turn_sin, re * turn_sin + im * turn_cos], 0))
    return mul(last, jnp.concatenate(columns, 1))


def product(a, b):
    ar, ai, br, bi = a[:, :128], a[:, 128:], b[:, :128], b[:, 128:]
    return jnp.concatenate([ar * br - ai * bi, ar * bi + ai * br], 1)


def product_conj(a, b):
    ar, ai, br, bi = a[:, :128], a[:, 128:], b[:, :128], b[:, 128:]
    return jnp.concatenate([ar * br + ai * bi, ar * bi - ai * br], 1)


def before_kernel(skip_ref, in_ref, first, last, tc, ts, fwd, bwd, spec_ref, pre_ref, gate_ref):
    first_channel = 2 * lax.axis_index("seq")
    x = [in_ref[:, c, :] for c in (0, 1)]
    gate = [in_ref[:, c, :] for c in (2, 3)]
    taps = [in_ref[:, c, :] for c in (4, 5)]
    spectra = to_spectra(x + taps, first[...], tc[...], ts[...], fwd[...])
    for n in range(4):
        spec_ref[n] = spectra[n]
    conv = to_signals(
        [product(spectra[c], spectra[2 + c]) for c in (0, 1)], last[...], tc[...], ts[...], bwd[...]
    )
    for c in (0, 1):
        pre_ref[c] = gate[c] * (conv[:, c * 128 : (c + 1) * 128] + skip_ref[first_channel + c] * x[c])
        gate_ref[c] = gate[c]


def after_kernel(skip_ref, target_ref, spec_ref, pre_ref, gate_ref, first, last, tc, ts, fwd, bwd, out_ref):
    first_channel = 2 * lax.axis_index("seq")
    back = [gate_ref[c] * (pre_ref[c] - target_ref[:, c, :]) for c in (0, 1)]
    spectra = to_spectra(back, first[...], tc[...], ts[...], fwd[...])
    mixed = [product_conj(spec_ref[2 + c], spectra[c]) for c in (0, 1)]
    mixed += [product_conj(spec_ref[c], spectra[c]) for c in (0, 1)]
    signals = to_signals(mixed, last[...], tc[...], ts[...], bwd[...])
    scale = (SHARDS * SHARD) ** -0.5
    for c in (0, 1):
        out_ref[:, c, :] = skip_ref[first_channel + c] * back[c] + signals[:, c * 128 : (c + 1) * 128]
        out_ref[:, 2 + c, :] = scale * signals[:, (2 + c) * 128 : (3 + c) * 128]


def attend_kernel(q_ref, kv0, kv1, kv2, kv3, kv4, out_ref):
    rank = lax.axis_index("seq")
    row, mine = rank // ROW, rank % ROW
    scale = 128 ** -0.5
    keys = jnp.concatenate([ref[0] for ref in (kv4, kv0, kv1, kv2, kv3)], 0)
    ones = jnp.ones((5 * SHARD, 128), jnp.bfloat16)
    values = jnp.concatenate([jnp.concatenate([ref[1] for ref in (kv4, kv0, kv1, kv2, kv3)], 0), ones], 1)
    lag = lax.broadcasted_iota(jnp.int32, (SHARD, SHARD), 0) - lax.broadcasted_iota(jnp.int32, (SHARD, SHARD), 1)
    diagonal = lag == 0
    zero = jnp.zeros((SHARD, SHARD), jnp.float32)
    for theirs in range(ROW):
        newest = lag >= (mine - theirs) * SHARD
        stats = []
        for h in (0, 1):
            scores = lax.dot_general(
                q_ref[theirs, h], keys, (((1,), (1,)), ((), ())), preferred_element_type=jnp.float32
            )
            parts = [scores[:, n * SHARD : (n + 1) * SHARD] for n in range(5)]
            blocks = [jnp.where(newest, parts[0], jnp.where(row >= BACK, parts[1], NEG))]
            blocks += [jnp.where(row >= BACK - r, parts[1 + r], NEG) for r in (1, 2, 3)]
            top = jnp.maximum(jnp.maximum(blocks[0], blocks[1]), jnp.maximum(blocks[2], blocks[3]))
            top = jnp.maximum(jnp.max(top, axis=1, keepdims=True), 0.5 * NEG)
            weights = [jnp.exp((b - top) * scale) for b in blocks]
            spread = [jnp.where(newest, weights[0], zero), jnp.where(newest, zero, weights[0])] + weights[1:]
            spread = jnp.concatenate([w.astype(jnp.bfloat16) for w in spread], 1)
            sums = jnp.dot(spread, values, preferred_element_type=jnp.float32)
            total = sums[:, 128:]
            safe = jnp.maximum(total, 1e-30)
            out_ref[theirs, h * 128 : (h + 1) * 128, :] = (sums[:, :128] / safe).astype(jnp.bfloat16)
            log_sum = jnp.where(total > 0.0, top * scale + jnp.log(safe), NEG)
            log_sum = jnp.sum(jnp.where(diagonal, log_sum, 0.0), axis=0, keepdims=True)
            high = log_sum.astype(jnp.bfloat16).astype(jnp.float32)
            rest = log_sum - high
            middle = rest.astype(jnp.bfloat16).astype(jnp.float32)
            stats += [high, middle, rest - middle]
        stats.append(jnp.zeros((10, 128), jnp.float32))
        out_ref[theirs, 256:272, :] = jnp.concatenate(stats, 0).astype(jnp.bfloat16)


def merge_kernel(parts_ref, proj_ref, out_ref):
    shares = []
    for h in (0, 1):
        sums = []
        for p in range(ROW):
            stats = parts_ref[p, 256:272, :].astype(jnp.float32)
            sums.append(stats[3 * h : 3 * h + 1] + stats[3 * h + 1 : 3 * h + 2] + stats[3 * h + 2 : 3 * h + 3])
        sums = jnp.concatenate(sums, 0)
        share = jnp.exp(sums - jnp.max(sums, axis=0, keepdims=True))
        shares.append(share / jnp.sum(share, axis=0, keepdims=True))
    shares.append(jnp.zeros((112, 128), jnp.float32))
    shares = jnp.concatenate(shares, 0).T
    heads = []
    for h in (0, 1):
        merged = None
        for p in range(ROW):
            part = parts_ref[p, h * 128 : (h + 1) * 128, :].astype(jnp.float32)
            part = shares[:, h * ROW + p : h * ROW + p + 1] * part
            merged = part if merged is None else merged + part
        heads.append(merged.astype(jnp.bfloat16))
    attended = jnp.concatenate(heads, 1)
    target = lax.dot_general(
        proj_ref[...], attended, (((1,), (1,)), ((), ())), preferred_element_type=jnp.float32
    )
    out_ref[...] = target.reshape(8, 128, 128).astype(jnp.bfloat16)


VMEM = pl.BlockSpec(memory_space=pltpu.VMEM)
SMEM = pl.BlockSpec(memory_space=pltpu.SMEM)


def near(x):
    return pltpu.with_memory_space_constraint(x, pltpu.VMEM)


def call_before(skip, packed, tables):
    return pl.pallas_call(
        before_kernel,
        out_shape=(
            pltpu.VMEM((4, HALF, 256), jnp.float32),
            pltpu.VMEM((2, SHARDS, 128), jnp.float32),
            pltpu.VMEM((2, SHARDS, 128), jnp.float32),
        ),
        in_specs=[SMEM] + [VMEM] * 7,
        out_specs=(VMEM,) * 3,
    )(skip, near(packed), *tables)


def call_after(skip, target, spectra, pre, gate, tables):
    return pl.pallas_call(
        after_kernel,
        out_shape=pltpu.VMEM((SHARDS, 4, 128), jnp.float32),
        in_specs=[SMEM] + [VMEM] * 10,
        out_specs=VMEM,
    )(skip, near(target), near(spectra), near(pre), near(gate), *tables)


def call_attend(queries, blocks):
    return pl.pallas_call(
        attend_kernel,
        out_shape=pltpu.VMEM((ROW, 272, 128), jnp.bfloat16),
        in_specs=[VMEM] * 6,
        out_specs=VMEM,
    )(near(queries), *[near(b) for b in blocks])


def call_merge(parts, proj):
    return pl.pallas_call(
        merge_kernel,
        out_shape=pltpu.VMEM((8, 128, 128), jnp.bfloat16),
        in_specs=[VMEM] * 2,
        out_specs=VMEM,
    )(near(parts), near(proj))


def body(
    query_heads,
    key_heads,
    value_heads,
    distill_proj,
    conv_input,
    gate_input,
    filter_taps,
    skip_gain,
):
    tables = [near(jnp.asarray(t)) for t in transform_tables()]
    rows = [[y * ROW + p for p in range(ROW)] for y in range(SHARDS // ROW)]

    packed = jnp.concatenate(
        [
            part.astype(jnp.float32).reshape(SHARDS, 2, 128)
            for part in (conv_input, gate_input, filter_taps)
        ],
        axis=1,
    )
    packed = lax.all_to_all(packed, "seq", 0, 0)
    own = jnp.stack([key_heads[:, 0], value_heads[:, 0]])
    blocks = [
        lax.ppermute(own, "seq", [(i, i + ROW * k) for i in range(SHARDS - ROW * k)])
        for k in range(BACK, 0, -1)
    ] + [own]
    packed, queries = lax.optimization_barrier((packed, jnp.transpose(query_heads, (1, 0, 2))))
    queries = lax.all_gather(queries, "seq", axis_index_groups=rows)
    spectra, pre, gate = call_before(skip_gain, packed, tables)

    proj = distill_proj.reshape(256, 1024).T
    parts = call_attend(queries, blocks)
    parts = lax.all_to_all(parts, "seq", 0, 0, axis_index_groups=rows)
    target = call_merge(parts, proj)
    target = lax.all_to_all(target, ("role", "head"), 0, 0)
    target = jnp.sum(target.astype(jnp.float32), axis=0).reshape(SHARDS, 2, 128)
    target = lax.all_to_all(target, "seq", 0, 0)
    out = call_after(skip_gain, target, spectra, pre, gate, tables)
    out = lax.all_to_all(out, "seq", 0, 0)
    return out[:, :2].reshape(128, 128), out[:, 2:].reshape(128, 128)


def solution(mesh):
    in_specs = (
        P("seq", ("role", "head"), None),
        P("seq", ("role", "head"), None),
        P("seq", ("role", "head"), None),
        P(("role", "head"), None, None),
        P(("role", "head"), "seq"),
        P(("role", "head"), "seq"),
        P(("role", "head"), "seq"),
        P(("role", "head")),
    )
    out_specs = (P(("role", "head"), "seq"), P(("role", "head"), "seq"))
    return jax.shard_map(body, mesh=mesh, in_specs=in_specs, out_specs=out_specs, check_vma=False)
```

```python
import jax
import jax.numpy as jnp
import ml_dtypes
import numpy as np
from jax import lax
from jax.experimental import pallas as pl
from jax.experimental.pallas import tpu as pltpu
from jax.sharding import PartitionSpec as P

WINDOW = 4096
SHARD = 128
ROW = 8
BACK = WINDOW // (ROW * SHARD)
SHARDS = 64
HALF = 72
NEG = -1e30


def transform_tables():
    length = 2 * SHARDS * SHARD
    k1 = np.arange(HALF)[:, None]
    live = (k1 <= SHARDS).astype(np.float64)
    a = np.arange(SHARDS)[None, :]
    angle = 2.0 * np.pi * ((k1 * a) % 128) / 128
    first = np.concatenate([live * np.cos(angle), -live * np.sin(angle)], 0)
    weight = live * np.where((k1 == 0) | (k1 == SHARDS), 1.0, 2.0) / length
    last = np.concatenate([weight * np.cos(angle), -weight * np.sin(angle)], 0).T
    b = np.arange(128)[None, :]
    turn = 2.0 * np.pi * (k1 * b) / length
    b2 = np.arange(128)[:, None]
    grid = 2.0 * np.pi * ((b2 * b) % 128) / 128
    cosine, sine = np.cos(grid), np.sin(grid)
    forward = np.block([[cosine, -sine], [sine, cosine]])
    backward = np.block([[cosine, sine], [-sine, cosine]])
    tables = [np.asarray(t, np.float32) for t in (np.cos(turn), np.sin(turn))]
    for table in (first, last, forward, backward):
        high = np.asarray(table, ml_dtypes.bfloat16)
        tables += [high, np.asarray(table - high.astype(np.float64), ml_dtypes.bfloat16)]
    return tables


def halves(x):
    high = x.astype(jnp.bfloat16)
    return high, (x - high.astype(jnp.float32)).astype(jnp.bfloat16)


def dot32(a, b):
    return jnp.dot(a, b, preferred_element_type=jnp.float32)


def table_times(table, x):
    high, low = halves(x)
    return dot32(table[0], high) + (dot32(table[0], low) + dot32(table[1], high))


def times_table(x, table):
    high, low = halves(x)
    return dot32(high, table[0]) + (dot32(low, table[0]) + dot32(high, table[1]))


def to_spectra(signals, first, turn_cos, turn_sin, forward):
    stacked = table_times(first, jnp.concatenate(signals, 1))
    rows = []
    for n in range(len(signals)):
        re = stacked[:HALF, n * 128 : (n + 1) * 128]
        im = stacked[HALF:, n * 128 : (n + 1) * 128]
        rows.append(jnp.concatenate([re * turn_cos + im * turn_sin, im * turn_cos - re * turn_sin], 1))
    spectra = times_table(jnp.concatenate(rows, 0), forward)
    return [spectra[n * HALF : (n + 1) * HALF] for n in range(len(signals))]


def to_signals(spectra, last, turn_cos, turn_sin, backward):
    rows = times_table(jnp.concatenate(spectra, 0), backward)
    columns = []
    for n in range(len(spectra)):
        re = rows[n * HALF : (n + 1) * HALF, :128]
        im = rows[n * HALF : (n + 1) * HALF, 128:]
        columns.append(jnp.concatenate([re * turn_cos - im * turn_sin, re * turn_sin + im * turn_cos], 0))
    return table_times(last, jnp.concatenate(columns, 1))


def product(a, b):
    ar, ai, br, bi = a[:, :128], a[:, 128:], b[:, :128], b[:, 128:]
    return jnp.concatenate([ar * br - ai * bi, ar * bi + ai * br], 1)


def product_conj(a, b):
    ar, ai, br, bi = a[:, :128], a[:, 128:], b[:, :128], b[:, 128:]
    return jnp.concatenate([ar * br + ai * bi, ar * bi - ai * br], 1)


def pack_kernel(parts_ref, input_ref, gate_ref, taps_ref, out_ref):
    target = parts_ref[0].astype(jnp.float32)
    for n in range(1, 8):
        target += parts_ref[n].astype(jnp.float32)
    arrays = (target, input_ref[...], gate_ref[...], taps_ref[...])
    for n, array in enumerate(arrays):
        array = array.astype(jnp.float32)
        out_ref[:, 2 * n, :] = array[:SHARDS]
        out_ref[:, 2 * n + 1, :] = array[SHARDS:]


def student_kernel(skip_ref, in_ref, tc, ts, f0, f1, l0, l1, w0, w1, b0, b1, out_ref):
    rank = lax.axis_index("seq")
    skip = [skip_ref[rank], skip_ref[rank + SHARDS]]
    target, signal, gate, taps = [[in_ref[:, 2 * n + c, :] for c in (0, 1)] for n in range(4)]
    turn = tc[...], ts[...]
    ahead = (f0[...], f1[...]), *turn, (w0[...], w1[...])
    behind = (l0[...], l1[...]), *turn, (b0[...], b1[...])
    spectra = to_spectra(signal + taps, *ahead)
    conv = to_signals([product(spectra[c], spectra[2 + c]) for c in (0, 1)], *behind)
    back = []
    for c in (0, 1):
        output = gate[c] * (conv[:, c * 128 : (c + 1) * 128] + skip[c] * signal[c])
        back.append(gate[c] * (output - target[c]))
    gradient = to_spectra(back, *ahead)
    mixed = [product_conj(spectra[2 + c], gradient[c]) for c in (0, 1)]
    mixed += [product_conj(spectra[c], gradient[c]) for c in (0, 1)]
    signals = to_signals(mixed, *behind)
    scale = (SHARDS * SHARD) ** -0.5
    for c in (0, 1):
        out_ref[:, c, :] = skip[c] * back[c] + signals[:, c * 128 : (c + 1) * 128]
        out_ref[:, 2 + c, :] = scale * signals[:, (2 + c) * 128 : (3 + c) * 128]


def unpack_kernel(in_ref, grad_ref, step_ref):
    for c in (0, 1):
        grad_ref[c * SHARDS : (c + 1) * SHARDS, :] = in_ref[:, c, :]
        step_ref[c * SHARDS : (c + 1) * SHARDS, :] = in_ref[:, 2 + c, :]


def attend_kernel(q_ref, kv0, kv1, kv2, kv3, kv4, out_ref):
    rank = lax.axis_index("seq")
    row, mine = rank // ROW, rank % ROW
    scale = 128 ** -0.5
    keys = jnp.concatenate([ref[0] for ref in (kv4, kv0, kv1, kv2, kv3)], 0)
    ones = jnp.ones((5 * SHARD, 128), jnp.bfloat16)
    values = jnp.concatenate([jnp.concatenate([ref[1] for ref in (kv4, kv0, kv1, kv2, kv3)], 0), ones], 1)
    lag = lax.broadcasted_iota(jnp.int32, (SHARD, SHARD), 0) - lax.broadcasted_iota(jnp.int32, (SHARD, SHARD), 1)
    diagonal = lag == 0
    zero = jnp.zeros((SHARD, SHARD), jnp.float32)
    for theirs in range(ROW):
        newest = lag >= (mine - theirs) * SHARD
        stats = []
        for h in (0, 1):
            scores = lax.dot_general(
                q_ref[theirs, h], keys, (((1,), (1,)), ((), ())), preferred_element_type=jnp.float32
            )
            parts = [scores[:, n * SHARD : (n + 1) * SHARD] for n in range(5)]
            blocks = [jnp.where(newest, parts[0], jnp.where(row >= BACK, parts[1], NEG))]
            blocks += [jnp.where(row >= BACK - r, parts[1 + r], NEG) for r in (1, 2, 3)]
            top = jnp.maximum(jnp.maximum(blocks[0], blocks[1]), jnp.maximum(blocks[2], blocks[3]))
            top = jnp.maximum(jnp.max(top, axis=1, keepdims=True), 0.5 * NEG)
            weights = [jnp.exp((b - top) * scale) for b in blocks]
            spread = [jnp.where(newest, weights[0], zero), jnp.where(newest, zero, weights[0])] + weights[1:]
            spread = jnp.concatenate([w.astype(jnp.bfloat16) for w in spread], 1)
            sums = jnp.dot(spread, values, preferred_element_type=jnp.float32)
            total = sums[:, 128:]
            safe = jnp.maximum(total, 1e-30)
            out_ref[theirs, h * 128 : (h + 1) * 128, :] = (sums[:, :128] / safe).astype(jnp.bfloat16)
            log_sum = jnp.where(total > 0.0, top * scale + jnp.log(safe), NEG)
            log_sum = jnp.sum(jnp.where(diagonal, log_sum, 0.0), axis=0, keepdims=True)
            high = log_sum.astype(jnp.bfloat16).astype(jnp.float32)
            rest = log_sum - high
            middle = rest.astype(jnp.bfloat16).astype(jnp.float32)
            stats += [high, middle, rest - middle]
        stats.append(jnp.zeros((10, 128), jnp.float32))
        out_ref[theirs, 256:272, :] = jnp.concatenate(stats, 0).astype(jnp.bfloat16)


def merge_kernel(parts_ref, proj_ref, out_ref):
    shares = []
    for h in (0, 1):
        sums = []
        for p in range(ROW):
            stats = parts_ref[p, 256:272, :].astype(jnp.float32)
            sums.append(stats[3 * h : 3 * h + 1] + stats[3 * h + 1 : 3 * h + 2] + stats[3 * h + 2 : 3 * h + 3])
        sums = jnp.concatenate(sums, 0)
        share = jnp.exp(sums - jnp.max(sums, axis=0, keepdims=True))
        shares.append(share / jnp.sum(share, axis=0, keepdims=True))
    shares.append(jnp.zeros((112, 128), jnp.float32))
    shares = jnp.concatenate(shares, 0).T
    heads = []
    for h in (0, 1):
        merged = None
        for p in range(ROW):
            part = parts_ref[p, h * 128 : (h + 1) * 128, :].astype(jnp.float32)
            part = shares[:, h * ROW + p : h * ROW + p + 1] * part
            merged = part if merged is None else merged + part
        heads.append(merged.astype(jnp.bfloat16))
    attended = jnp.concatenate(heads, 1)
    target = lax.dot_general(
        proj_ref[...], attended, (((1,), (1,)), ((), ())), preferred_element_type=jnp.float32
    )
    out_ref[...] = target.reshape(8, 128, 128).astype(jnp.bfloat16)


VMEM = pl.BlockSpec(memory_space=pltpu.VMEM)
SMEM = pl.BlockSpec(memory_space=pltpu.SMEM)


def near(x):
    return pltpu.with_memory_space_constraint(x, pltpu.VMEM)


def call_pack(parts, *inputs):
    return pl.pallas_call(
        pack_kernel,
        out_shape=pltpu.VMEM((SHARDS, 8, 128), jnp.float32),
        in_specs=[VMEM] * 4,
        out_specs=VMEM,
    )(near(parts), *[near(x) for x in inputs])


def call_student(skip, packed, tables):
    return pl.pallas_call(
        student_kernel,
        out_shape=pltpu.VMEM((SHARDS, 4, 128), jnp.float32),
        in_specs=[SMEM] + [VMEM] * 11,
        out_specs=VMEM,
    )(skip, near(packed), *tables)


def call_unpack(out):
    return pl.pallas_call(
        unpack_kernel,
        out_shape=(jax.ShapeDtypeStruct((128, 128), jnp.float32),) * 2,
        in_specs=[VMEM],
        out_specs=(VMEM,) * 2,
    )(near(out))


def call_attend(queries, blocks):
    return pl.pallas_call(
        attend_kernel,
        out_shape=pltpu.VMEM((ROW, 272, 128), jnp.bfloat16),
        in_specs=[VMEM] * 6,
        out_specs=VMEM,
    )(near(queries), *[near(b) for b in blocks])


def call_merge(parts, proj):
    return pl.pallas_call(
        merge_kernel,
        out_shape=pltpu.VMEM((8, 128, 128), jnp.bfloat16),
        in_specs=[VMEM] * 2,
        out_specs=VMEM,
    )(near(parts), near(proj))


def body(
    query_heads,
    key_heads,
    value_heads,
    distill_proj,
    conv_input,
    gate_input,
    filter_taps,
    skip_gain,
):
    tables = [near(jnp.asarray(t)) for t in transform_tables()]
    rows = [[y * ROW + p for p in range(ROW)] for y in range(SHARDS // ROW)]

    own = jnp.stack([key_heads[:, 0], value_heads[:, 0]])
    blocks = [
        lax.ppermute(own, "seq", [(i, i + ROW * k) for i in range(SHARDS - ROW * k)])
        for k in range(BACK, 0, -1)
    ] + [own]
    queries = lax.all_gather(jnp.transpose(query_heads, (1, 0, 2)), "seq", axis_index_groups=rows)
    proj = distill_proj.reshape(256, 1024).T
    parts = call_attend(queries, blocks)
    parts = lax.all_to_all(parts, "seq", 0, 0, axis_index_groups=rows)
    target = call_merge(parts, proj)
    target = lax.all_to_all(target, ("role", "head"), 0, 0)
    packed = call_pack(target, conv_input, gate_input, filter_taps)
    packed = lax.all_to_all(packed, "seq", 0, 0)
    out = call_student(skip_gain, packed, tables)
    out = lax.all_to_all(out, "seq", 0, 0)
    return call_unpack(out)


def solution(mesh):
    in_specs = (
        P("seq", ("role", "head"), None),
        P("seq", ("role", "head"), None),
        P("seq", ("role", "head"), None),
        P(("role", "head"), None, None),
        P(("role", "head"), "seq"),
        P(("role", "head"), "seq"),
        P(("role", "head"), "seq"),
        P(("role", "head")),
    )
    out_specs = (P(("role", "head"), "seq"), P(("role", "head"), "seq"))
    return jax.shard_map(body, mesh=mesh, in_specs=in_specs, out_specs=out_specs, check_vma=False)
```

```python
import jax
import jax.numpy as jnp
import ml_dtypes
import numpy as np
from jax import lax
from jax.experimental import pallas as pl
from jax.experimental.pallas import tpu as pltpu
from jax.sharding import PartitionSpec as P

WINDOW = 4096
SHARD = 128
ROW = 8
BACK = WINDOW // (ROW * SHARD)
SHARDS = 64
HALF = 72
NEG = -1e30


def transform_tables():
    length = 2 * SHARDS * SHARD
    k1 = np.arange(HALF)[:, None]
    live = (k1 <= SHARDS).astype(np.float64)
    a = np.arange(SHARDS)[None, :]
    angle = 2.0 * np.pi * ((k1 * a) % 128) / 128
    first = np.concatenate([live * np.cos(angle), -live * np.sin(angle)], 0)
    weight = live * np.where((k1 == 0) | (k1 == SHARDS), 1.0, 2.0) / length
    last = np.concatenate([weight * np.cos(angle), -weight * np.sin(angle)], 0).T
    b = np.arange(128)[None, :]
    turn = 2.0 * np.pi * (k1 * b) / length
    b2 = np.arange(128)[:, None]
    grid = 2.0 * np.pi * ((b2 * b) % 128) / 128
    cosine, sine = np.cos(grid), np.sin(grid)
    forward = np.block([[cosine, -sine], [sine, cosine]])
    backward = np.block([[cosine, sine], [-sine, cosine]])
    tables = [np.asarray(t, np.float32) for t in (np.cos(turn), np.sin(turn))]
    for table in (first, last, forward, backward):
        high = np.asarray(table, ml_dtypes.bfloat16)
        tables += [high, np.asarray(table - high.astype(np.float64), ml_dtypes.bfloat16)]
    return tables


def halves(x):
    high = x.astype(jnp.bfloat16)
    return high, (x - high.astype(jnp.float32)).astype(jnp.bfloat16)


def dot32(a, b):
    return jnp.dot(a, b, preferred_element_type=jnp.float32)


def table_times(table, x):
    high, low = halves(x)
    return dot32(table[0], high) + (dot32(table[0], low) + dot32(table[1], high))


def times_table(x, table):
    high, low = halves(x)
    return dot32(high, table[0]) + (dot32(low, table[0]) + dot32(high, table[1]))


def to_spectra(signals, first, turn_cos, turn_sin, forward):
    stacked = table_times(first, jnp.concatenate(signals, 1))
    rows = []
    for n in range(len(signals)):
        re = stacked[:HALF, n * 128 : (n + 1) * 128]
        im = stacked[HALF:, n * 128 : (n + 1) * 128]
        rows.append(jnp.concatenate([re * turn_cos + im * turn_sin, im * turn_cos - re * turn_sin], 1))
    spectra = times_table(jnp.concatenate(rows, 0), forward)
    return [spectra[n * HALF : (n + 1) * HALF] for n in range(len(signals))]


def to_signals(spectra, last, turn_cos, turn_sin, backward):
    rows = times_table(jnp.concatenate(spectra, 0), backward)
    columns = []
    for n in range(len(spectra)):
        re = rows[n * HALF : (n + 1) * HALF, :128]
        im = rows[n * HALF : (n + 1) * HALF, 128:]
        columns.append(jnp.concatenate([re * turn_cos - im * turn_sin, re * turn_sin + im * turn_cos], 0))
    return table_times(last, jnp.concatenate(columns, 1))


def product(a, b):
    ar, ai, br, bi = a[:, :128], a[:, 128:], b[:, :128], b[:, 128:]
    return jnp.concatenate([ar * br - ai * bi, ar * bi + ai * br], 1)


def product_conj(a, b):
    ar, ai, br, bi = a[:, :128], a[:, 128:], b[:, :128], b[:, 128:]
    return jnp.concatenate([ar * br + ai * bi, ar * bi - ai * br], 1)


def pack_kernel(parts_ref, input_ref, gate_ref, taps_ref, out_ref):
    target = parts_ref[0].astype(jnp.float32)
    for n in range(1, 8):
        target += parts_ref[n].astype(jnp.float32)
    arrays = (target, input_ref[...], gate_ref[...], taps_ref[...])
    for n, array in enumerate(arrays):
        array = array.astype(jnp.float32)
        out_ref[:, 2 * n, :] = array[:SHARDS]
        out_ref[:, 2 * n + 1, :] = array[SHARDS:]


def student_kernel(skip_ref, in_ref, tc, ts, f0, f1, l0, l1, w0, w1, b0, b1, out_ref):
    rank = lax.axis_index("seq")
    skip = [skip_ref[rank], skip_ref[rank + SHARDS]]
    target, signal, gate, taps = [[in_ref[:, 2 * n + c, :] for c in (0, 1)] for n in range(4)]
    turn = tc[...], ts[...]
    ahead = (f0[...], f1[...]), *turn, (w0[...], w1[...])
    behind = (l0[...], l1[...]), *turn, (b0[...], b1[...])
    spectra = to_spectra(signal + taps, *ahead)
    conv = to_signals([product(spectra[c], spectra[2 + c]) for c in (0, 1)], *behind)
    back = []
    for c in (0, 1):
        output = gate[c] * (conv[:, c * 128 : (c + 1) * 128] + skip[c] * signal[c])
        back.append(gate[c] * (output - target[c]))
    gradient = to_spectra(back, *ahead)
    mixed = [product_conj(spectra[2 + c], gradient[c]) for c in (0, 1)]
    mixed += [product_conj(spectra[c], gradient[c]) for c in (0, 1)]
    signals = to_signals(mixed, *behind)
    scale = (SHARDS * SHARD) ** -0.5
    for c in (0, 1):
        out_ref[:, c, :] = skip[c] * back[c] + signals[:, c * 128 : (c + 1) * 128]
        out_ref[:, 2 + c, :] = scale * signals[:, (2 + c) * 128 : (3 + c) * 128]


def unpack_kernel(in_ref, grad_ref, step_ref):
    for c in (0, 1):
        grad_ref[c * SHARDS : (c + 1) * SHARDS, :] = in_ref[:, c, :]
        step_ref[c * SHARDS : (c + 1) * SHARDS, :] = in_ref[:, 2 + c, :]


def attend_kernel(q_ref, kv_ref, out_ref):
    rank = lax.axis_index("seq")
    row, mine = rank // ROW, rank % ROW
    scale = 128 ** -0.5
    order = [row] + [jnp.maximum(row - BACK + r, 0) for r in range(BACK)]
    keys = jnp.concatenate([kv_ref[n, 0] for n in order], 0)
    ones = jnp.ones((5 * SHARD, 128), jnp.bfloat16)
    values = jnp.concatenate([jnp.concatenate([kv_ref[n, 1] for n in order], 0), ones], 1)
    lag = lax.broadcasted_iota(jnp.int32, (SHARD, SHARD), 0) - lax.broadcasted_iota(jnp.int32, (SHARD, SHARD), 1)
    diagonal = lag == 0
    zero = jnp.zeros((SHARD, SHARD), jnp.float32)
    for theirs in range(ROW):
        newest = lag >= (mine - theirs) * SHARD
        stats = []
        for h in (0, 1):
            scores = lax.dot_general(
                q_ref[theirs, h], keys, (((1,), (1,)), ((), ())), preferred_element_type=jnp.float32
            )
            parts = [scores[:, n * SHARD : (n + 1) * SHARD] for n in range(5)]
            blocks = [jnp.where(newest, parts[0], jnp.where(row >= BACK, parts[1], NEG))]
            blocks += [jnp.where(row >= BACK - r, parts[1 + r], NEG) for r in (1, 2, 3)]
            top = jnp.maximum(jnp.maximum(blocks[0], blocks[1]), jnp.maximum(blocks[2], blocks[3]))
            top = jnp.maximum(jnp.max(top, axis=1, keepdims=True), 0.5 * NEG)
            weights = [jnp.exp((b - top) * scale) for b in blocks]
            spread = [jnp.where(newest, weights[0], zero), jnp.where(newest, zero, weights[0])] + weights[1:]
            spread = jnp.concatenate([w.astype(jnp.bfloat16) for w in spread], 1)
            sums = jnp.dot(spread, values, preferred_element_type=jnp.float32)
            total = sums[:, 128:]
            safe = jnp.maximum(total, 1e-30)
            out_ref[theirs, h * 128 : (h + 1) * 128, :] = (sums[:, :128] / safe).astype(jnp.bfloat16)
            log_sum = jnp.where(total > 0.0, top * scale + jnp.log(safe), NEG)
            log_sum = jnp.sum(jnp.where(diagonal, log_sum, 0.0), axis=0, keepdims=True)
            high = log_sum.astype(jnp.bfloat16).astype(jnp.float32)
            rest = log_sum - high
            middle = rest.astype(jnp.bfloat16).astype(jnp.float32)
            stats += [high, middle, rest - middle]
        stats.append(jnp.zeros((10, 128), jnp.float32))
        out_ref[theirs, 256:272, :] = jnp.concatenate(stats, 0).astype(jnp.bfloat16)


def merge_kernel(parts_ref, proj_ref, out_ref):
    shares = []
    for h in (0, 1):
        sums = []
        for p in range(ROW):
            stats = parts_ref[p, 256:272, :].astype(jnp.float32)
            sums.append(stats[3 * h : 3 * h + 1] + stats[3 * h + 1 : 3 * h + 2] + stats[3 * h + 2 : 3 * h + 3])
        sums = jnp.concatenate(sums, 0)
        share = jnp.exp(sums - jnp.max(sums, axis=0, keepdims=True))
        shares.append(share / jnp.sum(share, axis=0, keepdims=True))
    shares.append(jnp.zeros((112, 128), jnp.float32))
    shares = jnp.concatenate(shares, 0).T
    heads = []
    for h in (0, 1):
        merged = None
        for p in range(ROW):
            part = parts_ref[p, h * 128 : (h + 1) * 128, :].astype(jnp.float32)
            part = shares[:, h * ROW + p : h * ROW + p + 1] * part
            merged = part if merged is None else merged + part
        heads.append(merged.astype(jnp.bfloat16))
    attended = jnp.concatenate(heads, 1)
    target = lax.dot_general(
        proj_ref[...], attended, (((1,), (1,)), ((), ())), preferred_element_type=jnp.float32
    )
    out_ref[...] = target.reshape(8, 128, 128).astype(jnp.bfloat16)


VMEM = pl.BlockSpec(memory_space=pltpu.VMEM)
SMEM = pl.BlockSpec(memory_space=pltpu.SMEM)


def near(x):
    return pltpu.with_memory_space_constraint(x, pltpu.VMEM)


def call_pack(parts, *inputs):
    return pl.pallas_call(
        pack_kernel,
        out_shape=pltpu.VMEM((SHARDS, 8, 128), jnp.float32),
        in_specs=[VMEM] * 4,
        out_specs=VMEM,
    )(near(parts), *[near(x) for x in inputs])


def call_student(skip, packed, tables):
    return pl.pallas_call(
        student_kernel,
        out_shape=pltpu.VMEM((SHARDS, 4, 128), jnp.float32),
        in_specs=[SMEM] + [VMEM] * 11,
        out_specs=VMEM,
    )(skip, near(packed), *tables)


def call_unpack(out):
    return pl.pallas_call(
        unpack_kernel,
        out_shape=(jax.ShapeDtypeStruct((128, 128), jnp.float32),) * 2,
        in_specs=[VMEM],
        out_specs=(VMEM,) * 2,
    )(near(out))


def call_attend(queries, pairs):
    return pl.pallas_call(
        attend_kernel,
        out_shape=pltpu.VMEM((ROW, 272, 128), jnp.bfloat16),
        in_specs=[VMEM] * 2,
        out_specs=VMEM,
    )(near(queries), near(pairs))


def call_merge(parts, proj):
    return pl.pallas_call(
        merge_kernel,
        out_shape=pltpu.VMEM((8, 128, 128), jnp.bfloat16),
        in_specs=[VMEM] * 2,
        out_specs=VMEM,
    )(near(parts), near(proj))


def body(
    query_heads,
    key_heads,
    value_heads,
    distill_proj,
    conv_input,
    gate_input,
    filter_taps,
    skip_gain,
):
    tables = [near(jnp.asarray(t)) for t in transform_tables()]
    rows = [[y * ROW + p for p in range(ROW)] for y in range(SHARDS // ROW)]

    columns = [[y * ROW + p for y in range(SHARDS // ROW)] for p in range(ROW)]
    own = jnp.stack([key_heads[:, 0], value_heads[:, 0]])
    pairs = jnp.broadcast_to(own, (SHARDS // ROW,) + own.shape)
    pairs = lax.all_to_all(pairs, "seq", 0, 0, axis_index_groups=columns)
    queries = lax.all_gather(jnp.transpose(query_heads, (1, 0, 2)), "seq", axis_index_groups=rows)
    proj = distill_proj.reshape(256, 1024).T
    parts = call_attend(queries, pairs)
    parts = lax.all_to_all(parts, "seq", 0, 0, axis_index_groups=rows)
    target = call_merge(parts, proj)
    target = lax.all_to_all(target, ("role", "head"), 0, 0)
    packed = call_pack(target, conv_input, gate_input, filter_taps)
    packed = lax.all_to_all(packed, "seq", 0, 0)
    out = call_student(skip_gain, packed, tables)
    out = lax.all_to_all(out, "seq", 0, 0)
    return call_unpack(out)


def solution(mesh):
    in_specs = (
        P("seq", ("role", "head"), None),
        P("seq", ("role", "head"), None),
        P("seq", ("role", "head"), None),
        P(("role", "head"), None, None),
        P(("role", "head"), "seq"),
        P(("role", "head"), "seq"),
        P(("role", "head"), "seq"),
        P(("role", "head")),
    )
    out_specs = (P(("role", "head"), "seq"), P(("role", "head"), "seq"))
    return jax.shard_map(body, mesh=mesh, in_specs=in_specs, out_specs=out_specs, check_vma=False)
```

```python
import jax
import jax.numpy as jnp
import ml_dtypes
import numpy as np
from jax import lax
from jax.experimental import pallas as pl
from jax.experimental.pallas import tpu as pltpu
from jax.sharding import PartitionSpec as P

WINDOW = 4096
SHARD = 128
ROW = 8
BACK = WINDOW // (ROW * SHARD)
SHARDS = 64
HALF = 72
NEG = -1e30


def transform_tables():
    length = 2 * SHARDS * SHARD
    k1 = np.arange(HALF)[:, None]
    live = (k1 <= SHARDS).astype(np.float64)
    a = np.arange(SHARDS)[None, :]
    angle = 2.0 * np.pi * ((k1 * a) % 128) / 128
    first = np.concatenate([live * np.cos(angle), -live * np.sin(angle)], 0)
    weight = live * np.where((k1 == 0) | (k1 == SHARDS), 1.0, 2.0) / length
    last = np.concatenate([weight * np.cos(angle), -weight * np.sin(angle)], 0).T
    b = np.arange(128)[None, :]
    turn = 2.0 * np.pi * (k1 * b) / length
    b2 = np.arange(128)[:, None]
    grid = 2.0 * np.pi * ((b2 * b) % 128) / 128
    cosine, sine = np.cos(grid), np.sin(grid)
    forward = np.block([[cosine, -sine], [sine, cosine]])
    backward = np.block([[cosine, sine], [-sine, cosine]])
    tables = [np.asarray(t, np.float32) for t in (np.cos(turn), np.sin(turn))]
    for table in (first, last, forward, backward):
        high = np.asarray(table, ml_dtypes.bfloat16)
        tables += [high, np.asarray(table - high.astype(np.float64), ml_dtypes.bfloat16)]
    return tables


def halves(x):
    high = x.astype(jnp.bfloat16)
    return high, (x - high.astype(jnp.float32)).astype(jnp.bfloat16)


def dot32(a, b):
    return jnp.dot(a, b, preferred_element_type=jnp.float32)


def table_times(table, x):
    high, low = halves(x)
    return dot32(table[0], high) + (dot32(table[0], low) + dot32(table[1], high))


def times_table(x, table):
    high, low = halves(x)
    return dot32(high, table[0]) + (dot32(low, table[0]) + dot32(high, table[1]))


def to_spectra(signals, first, turn_cos, turn_sin, forward):
    stacked = table_times(first, jnp.concatenate(signals, 1))
    rows = []
    for n in range(len(signals)):
        re = stacked[:HALF, n * 128 : (n + 1) * 128]
        im = stacked[HALF:, n * 128 : (n + 1) * 128]
        rows.append(jnp.concatenate([re * turn_cos + im * turn_sin, im * turn_cos - re * turn_sin], 1))
    spectra = times_table(jnp.concatenate(rows, 0), forward)
    return [spectra[n * HALF : (n + 1) * HALF] for n in range(len(signals))]


def to_signals(spectra, last, turn_cos, turn_sin, backward):
    rows = times_table(jnp.concatenate(spectra, 0), backward)
    columns = []
    for n in range(len(spectra)):
        re = rows[n * HALF : (n + 1) * HALF, :128]
        im = rows[n * HALF : (n + 1) * HALF, 128:]
        columns.append(jnp.concatenate([re * turn_cos - im * turn_sin, re * turn_sin + im * turn_cos], 0))
    return table_times(last, jnp.concatenate(columns, 1))


def product(a, b):
    ar, ai, br, bi = a[:, :128], a[:, 128:], b[:, :128], b[:, 128:]
    return jnp.concatenate([ar * br - ai * bi, ar * bi + ai * br], 1)


def product_conj(a, b):
    ar, ai, br, bi = a[:, :128], a[:, 128:], b[:, :128], b[:, 128:]
    return jnp.concatenate([ar * br + ai * bi, ar * bi - ai * br], 1)


def repeat_kernel(key_ref, value_ref, out_ref):
    for n in range(SHARDS // ROW):
        out_ref[n, 0] = key_ref[...]
        out_ref[n, 1] = value_ref[...]


def pack_kernel(parts_ref, input_ref, gate_ref, taps_ref, out_ref, wide_ref):
    target = parts_ref[0].astype(jnp.float32)
    for n in range(1, 8):
        target += parts_ref[n].astype(jnp.float32)
    arrays = (target, input_ref[...], gate_ref[...], taps_ref[...])
    for n, array in enumerate(arrays):
        array = array.astype(jnp.float32)
        wide_ref[:, 2 * n, :] = array[:SHARDS]
        wide_ref[:, 2 * n + 1, :] = array[SHARDS:]
    out_ref[...] = wide_ref[...].astype(jnp.bfloat16)


def student_kernel(skip_ref, in_ref, tc, ts, f0, f1, l0, l1, w0, w1, b0, b1, out_ref, wide_in, wide_out):
    wide_in[...] = in_ref[...].astype(jnp.float32)
    rank = lax.axis_index("seq")
    skip = [skip_ref[rank], skip_ref[rank + SHARDS]]
    target, signal, gate, taps = [[wide_in[:, 2 * n + c, :] for c in (0, 1)] for n in range(4)]
    turn = tc[...], ts[...]
    ahead = (f0[...], f1[...]), *turn, (w0[...], w1[...])
    behind = (l0[...], l1[...]), *turn, (b0[...], b1[...])
    spectra = to_spectra(signal + taps, *ahead)
    conv = to_signals([product(spectra[c], spectra[2 + c]) for c in (0, 1)], *behind)
    back = []
    for c in (0, 1):
        output = gate[c] * (conv[:, c * 128 : (c + 1) * 128] + skip[c] * signal[c])
        back.append(gate[c] * (output - target[c]))
    gradient = to_spectra(back, *ahead)
    mixed = [product_conj(spectra[2 + c], gradient[c]) for c in (0, 1)]
    mixed += [product_conj(spectra[c], gradient[c]) for c in (0, 1)]
    signals = to_signals(mixed, *behind)
    scale = (SHARDS * SHARD) ** -0.5
    for c in (0, 1):
        wide_out[:, c, :] = skip[c] * back[c] + signals[:, c * 128 : (c + 1) * 128]
        wide_out[:, 2 + c, :] = scale * signals[:, (2 + c) * 128 : (3 + c) * 128]
    out_ref[...] = wide_out[...].astype(jnp.bfloat16)


def unpack_kernel(in_ref, grad_ref, step_ref, wide_ref):
    wide_ref[...] = in_ref[...].astype(jnp.float32)
    for c in (0, 1):
        grad_ref[c * SHARDS : (c + 1) * SHARDS, :] = wide_ref[:, c, :]
        step_ref[c * SHARDS : (c + 1) * SHARDS, :] = wide_ref[:, 2 + c, :]


def attend_kernel(q_ref, kv_ref, out_ref):
    rank = lax.axis_index("seq")
    row, mine = rank // ROW, rank % ROW
    scale = 128 ** -0.5
    order = [row] + [jnp.maximum(row - BACK + r, 0) for r in range(BACK)]
    keys = jnp.concatenate([kv_ref[n, 0] for n in order], 0)
    ones = jnp.ones((5 * SHARD, 128), jnp.bfloat16)
    values = jnp.concatenate([jnp.concatenate([kv_ref[n, 1] for n in order], 0), ones], 1)
    lag = lax.broadcasted_iota(jnp.int32, (SHARD, SHARD), 0) - lax.broadcasted_iota(jnp.int32, (SHARD, SHARD), 1)
    diagonal = lag == 0
    zero = jnp.zeros((SHARD, SHARD), jnp.float32)
    for theirs in range(ROW):
        newest = lag >= (mine - theirs) * SHARD
        stats = []
        for h in (0, 1):
            scores = lax.dot_general(
                q_ref[theirs, h], keys, (((1,), (1,)), ((), ())), preferred_element_type=jnp.float32
            )
            parts = [scores[:, n * SHARD : (n + 1) * SHARD] for n in range(5)]
            blocks = [jnp.where(newest, parts[0], jnp.where(row >= BACK, parts[1], NEG))]
            blocks += [jnp.where(row >= BACK - r, parts[1 + r], NEG) for r in (1, 2, 3)]
            top = jnp.maximum(jnp.maximum(blocks[0], blocks[1]), jnp.maximum(blocks[2], blocks[3]))
            top = jnp.maximum(jnp.max(top, axis=1, keepdims=True), 0.5 * NEG)
            weights = [jnp.exp((b - top) * scale) for b in blocks]
            spread = [jnp.where(newest, weights[0], zero), jnp.where(newest, zero, weights[0])] + weights[1:]
            spread = jnp.concatenate([w.astype(jnp.bfloat16) for w in spread], 1)
            sums = jnp.dot(spread, values, preferred_element_type=jnp.float32)
            total = sums[:, 128:]
            safe = jnp.maximum(total, 1e-30)
            out_ref[theirs, h * 128 : (h + 1) * 128, :] = (sums[:, :128] / safe).astype(jnp.bfloat16)
            log_sum = jnp.where(total > 0.0, top * scale + jnp.log(safe), NEG)
            log_sum = jnp.sum(jnp.where(diagonal, log_sum, 0.0), axis=0, keepdims=True)
            high = log_sum.astype(jnp.bfloat16).astype(jnp.float32)
            rest = log_sum - high
            middle = rest.astype(jnp.bfloat16).astype(jnp.float32)
            stats += [high, middle, rest - middle]
        stats.append(jnp.zeros((10, 128), jnp.float32))
        out_ref[theirs, 256:272, :] = jnp.concatenate(stats, 0).astype(jnp.bfloat16)


def merge_kernel(parts_ref, proj_ref, out_ref):
    shares = []
    for h in (0, 1):
        sums = []
        for p in range(ROW):
            stats = parts_ref[p, 256:272, :].astype(jnp.float32)
            sums.append(stats[3 * h : 3 * h + 1] + stats[3 * h + 1 : 3 * h + 2] + stats[3 * h + 2 : 3 * h + 3])
        sums = jnp.concatenate(sums, 0)
        share = jnp.exp(sums - jnp.max(sums, axis=0, keepdims=True))
        shares.append(share / jnp.sum(share, axis=0, keepdims=True))
    shares.append(jnp.zeros((112, 128), jnp.float32))
    shares = jnp.concatenate(shares, 0).T
    heads = []
    for h in (0, 1):
        merged = None
        for p in range(ROW):
            part = parts_ref[p, h * 128 : (h + 1) * 128, :].astype(jnp.float32)
            part = shares[:, h * ROW + p : h * ROW + p + 1] * part
            merged = part if merged is None else merged + part
        heads.append(merged.astype(jnp.bfloat16))
    attended = jnp.concatenate(heads, 1)
    target = lax.dot_general(
        proj_ref[...], attended, (((1,), (1,)), ((), ())), preferred_element_type=jnp.float32
    )
    out_ref[...] = target.reshape(8, 128, 128).astype(jnp.bfloat16)


VMEM = pl.BlockSpec(memory_space=pltpu.VMEM)
SMEM = pl.BlockSpec(memory_space=pltpu.SMEM)


def near(x):
    return pltpu.with_memory_space_constraint(x, pltpu.VMEM)


def call_repeat(key, value):
    return pl.pallas_call(
        repeat_kernel,
        out_shape=pltpu.VMEM((SHARDS // ROW, 2, SHARD, 128), jnp.bfloat16),
        in_specs=[VMEM] * 2,
        out_specs=VMEM,
    )(key, value)


def call_pack(parts, *inputs):
    return pl.pallas_call(
        pack_kernel,
        out_shape=pltpu.VMEM((SHARDS, 8, 128), jnp.bfloat16),
        in_specs=[VMEM] * 4,
        out_specs=VMEM,
        scratch_shapes=[pltpu.VMEM((SHARDS, 8, 128), jnp.float32)],
    )(near(parts), *[near(x) for x in inputs])


def call_student(skip, packed, tables):
    return pl.pallas_call(
        student_kernel,
        out_shape=pltpu.VMEM((SHARDS, 4, 128), jnp.bfloat16),
        in_specs=[SMEM] + [VMEM] * 11,
        out_specs=VMEM,
        scratch_shapes=[pltpu.VMEM((SHARDS, 8, 128), jnp.float32), pltpu.VMEM((SHARDS, 4, 128), jnp.float32)],
    )(skip, near(packed), *tables)


def call_unpack(out):
    return pl.pallas_call(
        unpack_kernel,
        out_shape=(jax.ShapeDtypeStruct((128, 128), jnp.float32),) * 2,
        in_specs=[VMEM],
        out_specs=(VMEM,) * 2,
        scratch_shapes=[pltpu.VMEM((SHARDS, 4, 128), jnp.float32)],
    )(near(out))


def call_attend(queries, pairs):
    return pl.pallas_call(
        attend_kernel,
        out_shape=pltpu.VMEM((ROW, 272, 128), jnp.bfloat16),
        in_specs=[VMEM] * 2,
        out_specs=VMEM,
    )(near(queries), near(pairs))


def call_merge(parts, proj):
    return pl.pallas_call(
        merge_kernel,
        out_shape=pltpu.VMEM((8, 128, 128), jnp.bfloat16),
        in_specs=[VMEM] * 2,
        out_specs=VMEM,
    )(near(parts), near(proj))


def body(
    query_heads,
    key_heads,
    value_heads,
    distill_proj,
    conv_input,
    gate_input,
    filter_taps,
    skip_gain,
):
    tables = [near(jnp.asarray(t)) for t in transform_tables()]
    rows = [[y * ROW + p for p in range(ROW)] for y in range(SHARDS // ROW)]

    columns = [[y * ROW + p for y in range(SHARDS // ROW)] for p in range(ROW)]
    pairs = call_repeat(key_heads[:, 0], value_heads[:, 0])
    pairs = lax.all_to_all(pairs, "seq", 0, 0, axis_index_groups=columns)
    queries = lax.all_gather(jnp.transpose(query_heads, (1, 0, 2)), "seq", axis_index_groups=rows)
    proj = distill_proj.reshape(256, 1024).T
    parts = call_attend(queries, pairs)
    parts = lax.all_to_all(parts, "seq", 0, 0, axis_index_groups=rows)
    target = call_merge(parts, proj)
    target = lax.all_to_all(target, ("role", "head"), 0, 0)
    packed = call_pack(target, conv_input, gate_input, filter_taps)
    packed = lax.all_to_all(packed, "seq", 0, 0)
    out = call_student(skip_gain, packed, tables)
    out = lax.all_to_all(out, "seq", 0, 0)
    return call_unpack(out)


def solution(mesh):
    in_specs = (
        P("seq", ("role", "head"), None),
        P("seq", ("role", "head"), None),
        P("seq", ("role", "head"), None),
        P(("role", "head"), None, None),
        P(("role", "head"), "seq"),
        P(("role", "head"), "seq"),
        P(("role", "head"), "seq"),
        P(("role", "head")),
    )
    out_specs = (P(("role", "head"), "seq"), P(("role", "head"), "seq"))
    return jax.shard_map(body, mesh=mesh, in_specs=in_specs, out_specs=out_specs, check_vma=False)
```

```python
import jax
import jax.numpy as jnp
import ml_dtypes
import numpy as np
from jax import lax
from jax.experimental import pallas as pl
from jax.experimental.pallas import tpu as pltpu
from jax.sharding import PartitionSpec as P

WINDOW = 4096
SHARD = 128
ROW = 8
GROUP = 4
BACK = WINDOW // (ROW * SHARD)
SHARDS = 64
HALF = 72
NEG = -1e30


def transform_tables():
    length = 2 * SHARDS * SHARD
    k1 = np.arange(HALF)[:, None]
    live = (k1 <= SHARDS).astype(np.float64)
    a = np.arange(SHARDS)[None, :]
    angle = 2.0 * np.pi * ((k1 * a) % 128) / 128
    first = np.concatenate([live * np.cos(angle), -live * np.sin(angle)], 0)
    weight = live * np.where((k1 == 0) | (k1 == SHARDS), 1.0, 2.0) / length
    last = np.concatenate([weight * np.cos(angle), -weight * np.sin(angle)], 0).T
    b = np.arange(128)[None, :]
    turn = 2.0 * np.pi * (k1 * b) / length
    b2 = np.arange(128)[:, None]
    grid = 2.0 * np.pi * ((b2 * b) % 128) / 128
    cosine, sine = np.cos(grid), np.sin(grid)
    forward = np.block([[cosine, -sine], [sine, cosine]])
    backward = np.block([[cosine, sine], [-sine, cosine]])
    tables = [np.asarray(t, np.float32) for t in (np.cos(turn), np.sin(turn))]
    for table in (first, last, forward, backward):
        high = np.asarray(table, ml_dtypes.bfloat16)
        tables += [high, np.asarray(table - high.astype(np.float64), ml_dtypes.bfloat16)]
    return tables


def halves(x):
    high = x.astype(jnp.bfloat16)
    return high, (x - high.astype(jnp.float32)).astype(jnp.bfloat16)


def dot32(a, b):
    return jnp.dot(a, b, preferred_element_type=jnp.float32)


def table_times(table, x):
    high, low = halves(x)
    return dot32(table[0], high) + (dot32(table[0], low) + dot32(table[1], high))


def times_table(x, table):
    high, low = halves(x)
    return dot32(high, table[0]) + (dot32(low, table[0]) + dot32(high, table[1]))


def to_spectra(signals, first, turn_cos, turn_sin, forward):
    stacked = table_times(first, jnp.concatenate(signals, 1))
    rows = []
    for n in range(len(signals)):
        re = stacked[:HALF, n * 128 : (n + 1) * 128]
        im = stacked[HALF:, n * 128 : (n + 1) * 128]
        rows.append(jnp.concatenate([re * turn_cos + im * turn_sin, im * turn_cos - re * turn_sin], 1))
    spectra = times_table(jnp.concatenate(rows, 0), forward)
    return [spectra[n * HALF : (n + 1) * HALF] for n in range(len(signals))]


def to_signals(spectra, last, turn_cos, turn_sin, backward):
    rows = times_table(jnp.concatenate(spectra, 0), backward)
    columns = []
    for n in range(len(spectra)):
        re = rows[n * HALF : (n + 1) * HALF, :128]
        im = rows[n * HALF : (n + 1) * HALF, 128:]
        columns.append(jnp.concatenate([re * turn_cos - im * turn_sin, re * turn_sin + im * turn_cos], 0))
    return table_times(last, jnp.concatenate(columns, 1))


def product(a, b):
    ar, ai, br, bi = a[:, :128], a[:, 128:], b[:, :128], b[:, 128:]
    return jnp.concatenate([ar * br - ai * bi, ar * bi + ai * br], 1)


def product_conj(a, b):
    ar, ai, br, bi = a[:, :128], a[:, 128:], b[:, :128], b[:, 128:]
    return jnp.concatenate([ar * br + ai * bi, ar * bi - ai * br], 1)


def repeat_kernel(key_ref, value_ref, out_ref):
    for n in range(SHARDS // ROW):
        out_ref[n, 0] = key_ref[...]
        out_ref[n, 1] = value_ref[...]


def pack_kernel(parts_ref, input_ref, gate_ref, taps_ref, out_ref, wide_ref):
    target = parts_ref[0].astype(jnp.float32)
    for n in range(1, 8):
        target += parts_ref[n].astype(jnp.float32)
    arrays = (target, input_ref[...], gate_ref[...], taps_ref[...])
    for n, array in enumerate(arrays):
        array = array.astype(jnp.float32)
        wide_ref[:, 2 * n, :] = array[:SHARDS]
        wide_ref[:, 2 * n + 1, :] = array[SHARDS:]
    out_ref[...] = wide_ref[...].astype(jnp.bfloat16)


def student_kernel(skip_ref, in_ref, tc, ts, f0, f1, l0, l1, w0, w1, b0, b1, out_ref, wide_in, wide_out):
    wide_in[...] = in_ref[...].astype(jnp.float32)
    rank = lax.axis_index("seq")
    skip = [skip_ref[rank], skip_ref[rank + SHARDS]]
    target, signal, gate, taps = [[wide_in[:, 2 * n + c, :] for c in (0, 1)] for n in range(4)]
    turn = tc[...], ts[...]
    ahead = (f0[...], f1[...]), *turn, (w0[...], w1[...])
    behind = (l0[...], l1[...]), *turn, (b0[...], b1[...])
    spectra = to_spectra(signal + taps, *ahead)
    conv = to_signals([product(spectra[c], spectra[2 + c]) for c in (0, 1)], *behind)
    back = []
    for c in (0, 1):
        output = gate[c] * (conv[:, c * 128 : (c + 1) * 128] + skip[c] * signal[c])
        back.append(gate[c] * (output - target[c]))
    gradient = to_spectra(back, *ahead)
    mixed = [product_conj(spectra[2 + c], gradient[c]) for c in (0, 1)]
    mixed += [product_conj(spectra[c], gradient[c]) for c in (0, 1)]
    signals = to_signals(mixed, *behind)
    scale = (SHARDS * SHARD) ** -0.5
    for c in (0, 1):
        wide_out[:, c, :] = skip[c] * back[c] + signals[:, c * 128 : (c + 1) * 128]
        wide_out[:, 2 + c, :] = scale * signals[:, (2 + c) * 128 : (3 + c) * 128]
    out_ref[...] = wide_out[...].astype(jnp.bfloat16)


def unpack_kernel(in_ref, grad_ref, step_ref, wide_ref):
    wide_ref[...] = in_ref[...].astype(jnp.float32)
    for c in (0, 1):
        grad_ref[c * SHARDS : (c + 1) * SHARDS, :] = wide_ref[:, c, :]
        step_ref[c * SHARDS : (c + 1) * SHARDS, :] = wide_ref[:, 2 + c, :]


def attend_kernel(q_ref, own_ref, sibling_ref, out_ref):
    rank = lax.axis_index("seq")
    row, mine, core = rank // ROW, rank % ROW // 2, rank % 2
    scale = 128 ** -0.5
    order = [row] + [jnp.maximum(row - BACK + r, 0) for r in range(BACK)]
    sources = (own_ref, sibling_ref)
    keys = jnp.concatenate([ref[n, 0] for ref in sources for n in order], 0)
    ones = jnp.ones((10 * SHARD, 128), jnp.bfloat16)
    values = jnp.concatenate([jnp.concatenate([ref[n, 1] for ref in sources for n in order], 0), ones], 1)
    lag = lax.broadcasted_iota(jnp.int32, (SHARD, SHARD), 0) - lax.broadcasted_iota(jnp.int32, (SHARD, SHARD), 1)
    diagonal = lag == 0
    zero = jnp.zeros((SHARD, SHARD), jnp.float32)
    for theirs in range(GROUP):
        ahead = 2 * (mine - theirs) * SHARD
        newest = [lag >= ahead, lag >= ahead + (1 - 2 * core) * SHARD]
        stats = []
        for h in (0, 1):
            scores = lax.dot_general(
                q_ref[theirs, h], keys, (((1,), (1,)), ((), ())), preferred_element_type=jnp.float32
            )
            parts = [scores[:, n * SHARD : (n + 1) * SHARD] for n in range(10)]
            blocks = []
            for source in (0, 1):
                part = parts[5 * source : 5 * source + 5]
                blocks.append(jnp.where(newest[source], part[0], jnp.where(row >= BACK, part[1], NEG)))
                blocks += [jnp.where(row >= BACK - r, part[1 + r], NEG) for r in (1, 2, 3)]
            top = blocks[0]
            for block in blocks[1:]:
                top = jnp.maximum(top, block)
            top = jnp.maximum(jnp.max(top, axis=1, keepdims=True), 0.5 * NEG)
            weights = [jnp.exp((b - top) * scale) for b in blocks]
            spread = []
            for source in (0, 1):
                part = weights[4 * source : 4 * source + 4]
                spread += [jnp.where(newest[source], part[0], zero), jnp.where(newest[source], zero, part[0])]
                spread += part[1:]
            spread = jnp.concatenate([w.astype(jnp.bfloat16) for w in spread], 1)
            sums = jnp.dot(spread, values, preferred_element_type=jnp.float32)
            total = sums[:, 128:]
            safe = jnp.maximum(total, 1e-30)
            out_ref[theirs, h * 128 : (h + 1) * 128, :] = (sums[:, :128] / safe).astype(jnp.bfloat16)
            log_sum = jnp.where(total > 0.0, top * scale + jnp.log(safe), NEG)
            log_sum = jnp.sum(jnp.where(diagonal, log_sum, 0.0), axis=0, keepdims=True)
            high = log_sum.astype(jnp.bfloat16).astype(jnp.float32)
            rest = log_sum - high
            middle = rest.astype(jnp.bfloat16).astype(jnp.float32)
            stats += [high, middle, rest - middle]
        stats.append(jnp.zeros((10, 128), jnp.float32))
        out_ref[theirs, 256:272, :] = jnp.concatenate(stats, 0).astype(jnp.bfloat16)


def merge_kernel(parts_ref, proj_ref, out_ref):
    shares = []
    for h in (0, 1):
        sums = []
        for p in range(GROUP):
            stats = parts_ref[p, 256:272, :].astype(jnp.float32)
            sums.append(stats[3 * h : 3 * h + 1] + stats[3 * h + 1 : 3 * h + 2] + stats[3 * h + 2 : 3 * h + 3])
        sums = jnp.concatenate(sums, 0)
        share = jnp.exp(sums - jnp.max(sums, axis=0, keepdims=True))
        shares.append(share / jnp.sum(share, axis=0, keepdims=True))
    shares.append(jnp.zeros((128 - 2 * GROUP, 128), jnp.float32))
    shares = jnp.concatenate(shares, 0).T
    heads = []
    for h in (0, 1):
        merged = None
        for p in range(GROUP):
            part = parts_ref[p, h * 128 : (h + 1) * 128, :].astype(jnp.float32)
            part = shares[:, h * GROUP + p : h * GROUP + p + 1] * part
            merged = part if merged is None else merged + part
        heads.append(merged.astype(jnp.bfloat16))
    attended = jnp.concatenate(heads, 1)
    target = lax.dot_general(
        proj_ref[...], attended, (((1,), (1,)), ((), ())), preferred_element_type=jnp.float32
    )
    out_ref[...] = target.reshape(8, 128, 128).astype(jnp.bfloat16)


VMEM = pl.BlockSpec(memory_space=pltpu.VMEM)
SMEM = pl.BlockSpec(memory_space=pltpu.SMEM)


def near(x):
    return pltpu.with_memory_space_constraint(x, pltpu.VMEM)


def call_repeat(key, value):
    return pl.pallas_call(
        repeat_kernel,
        out_shape=pltpu.VMEM((SHARDS // ROW, 2, SHARD, 128), jnp.bfloat16),
        in_specs=[VMEM] * 2,
        out_specs=VMEM,
    )(key, value)


def call_pack(parts, *inputs):
    return pl.pallas_call(
        pack_kernel,
        out_shape=pltpu.VMEM((SHARDS, 8, 128), jnp.bfloat16),
        in_specs=[VMEM] * 4,
        out_specs=VMEM,
        scratch_shapes=[pltpu.VMEM((SHARDS, 8, 128), jnp.float32)],
    )(near(parts), *[near(x) for x in inputs])


def call_student(skip, packed, tables):
    return pl.pallas_call(
        student_kernel,
        out_shape=pltpu.VMEM((SHARDS, 4, 128), jnp.bfloat16),
        in_specs=[SMEM] + [VMEM] * 11,
        out_specs=VMEM,
        scratch_shapes=[pltpu.VMEM((SHARDS, 8, 128), jnp.float32), pltpu.VMEM((SHARDS, 4, 128), jnp.float32)],
    )(skip, near(packed), *tables)


def call_unpack(out):
    return pl.pallas_call(
        unpack_kernel,
        out_shape=(jax.ShapeDtypeStruct((128, 128), jnp.float32),) * 2,
        in_specs=[VMEM],
        out_specs=(VMEM,) * 2,
        scratch_shapes=[pltpu.VMEM((SHARDS, 4, 128), jnp.float32)],
    )(near(out))


def call_attend(queries, own, sibling):
    return pl.pallas_call(
        attend_kernel,
        out_shape=pltpu.VMEM((GROUP, 272, 128), jnp.bfloat16),
        in_specs=[VMEM] * 3,
        out_specs=VMEM,
    )(near(queries), near(own), near(sibling))


def call_merge(parts, proj):
    return pl.pallas_call(
        merge_kernel,
        out_shape=pltpu.VMEM((8, 128, 128), jnp.bfloat16),
        in_specs=[VMEM] * 2,
        out_specs=VMEM,
    )(near(parts), near(proj))


def body(
    query_heads,
    key_heads,
    value_heads,
    distill_proj,
    conv_input,
    gate_input,
    filter_taps,
    skip_gain,
):
    tables = [near(jnp.asarray(t)) for t in transform_tables()]
    lines = range(SHARDS // ROW)
    groups = [[y * ROW + 2 * x + core for x in range(GROUP)] for y in lines for core in (0, 1)]
    columns = [[y * ROW + p for y in lines] for p in range(ROW)]
    pairs = call_repeat(key_heads[:, 0], value_heads[:, 0])
    own = lax.all_to_all(pairs, "seq", 0, 0, axis_index_groups=columns)
    queries = lax.all_gather(jnp.transpose(query_heads, (1, 0, 2)), "seq", axis_index_groups=groups)
    own, queries = lax.optimization_barrier((own, queries))
    sibling = lax.ppermute(own, "seq", [(i, i ^ 1) for i in range(SHARDS)])
    proj = distill_proj.reshape(256, 1024).T
    parts = call_attend(queries, own, sibling)
    parts = lax.all_to_all(parts, "seq", 0, 0, axis_index_groups=groups)
    target = call_merge(parts, proj)
    target = lax.all_to_all(target, ("role", "head"), 0, 0)
    packed = call_pack(target, conv_input, gate_input, filter_taps)
    packed = lax.all_to_all(packed, "seq", 0, 0)
    out = call_student(skip_gain, packed, tables)
    out = lax.all_to_all(out, "seq", 0, 0)
    return call_unpack(out)


def solution(mesh):
    in_specs = (
        P("seq", ("role", "head"), None),
        P("seq", ("role", "head"), None),
        P("seq", ("role", "head"), None),
        P(("role", "head"), None, None),
        P(("role", "head"), "seq"),
        P(("role", "head"), "seq"),
        P(("role", "head"), "seq"),
        P(("role", "head")),
    )
    out_specs = (P(("role", "head"), "seq"), P(("role", "head"), "seq"))
    return jax.shard_map(body, mesh=mesh, in_specs=in_specs, out_specs=out_specs, check_vma=False)
```

```python
import jax
import jax.numpy as jnp
import ml_dtypes
import numpy as np
from jax import lax
from jax.experimental import pallas as pl
from jax.experimental.pallas import tpu as pltpu
from jax.sharding import PartitionSpec as P

WINDOW = 4096
SHARD = 128
ROW = 8
GROUP = 4
BACK = WINDOW // (ROW * SHARD)
SHARDS = 64
HALF = 72
NEG = -1e30


def transform_tables():
    length = 2 * SHARDS * SHARD
    k1 = np.arange(HALF)[:, None]
    live = (k1 <= SHARDS).astype(np.float64)
    a = np.arange(SHARDS)[None, :]
    angle = 2.0 * np.pi * ((k1 * a) % 128) / 128
    first = np.concatenate([live * np.cos(angle), -live * np.sin(angle)], 0)
    weight = live * np.where((k1 == 0) | (k1 == SHARDS), 1.0, 2.0) / length
    last = np.concatenate([weight * np.cos(angle), -weight * np.sin(angle)], 0).T
    b = np.arange(128)[None, :]
    turn = 2.0 * np.pi * (k1 * b) / length
    b2 = np.arange(128)[:, None]
    grid = 2.0 * np.pi * ((b2 * b) % 128) / 128
    cosine, sine = np.cos(grid), np.sin(grid)
    forward = np.block([[cosine, -sine], [sine, cosine]])
    backward = np.block([[cosine, sine], [-sine, cosine]])
    tables = [np.asarray(t, np.float32) for t in (np.cos(turn), np.sin(turn))]
    for table in (first, last, forward, backward):
        high = np.asarray(table, ml_dtypes.bfloat16)
        tables += [high, np.asarray(table - high.astype(np.float64), ml_dtypes.bfloat16)]
    return tables


def halves(x):
    high = x.astype(jnp.bfloat16)
    return high, (x - high.astype(jnp.float32)).astype(jnp.bfloat16)


def dot32(a, b):
    return jnp.dot(a, b, preferred_element_type=jnp.float32)


def table_times(table, x):
    high, low = halves(x)
    return dot32(table[0], high) + (dot32(table[0], low) + dot32(table[1], high))


def times_table(x, table):
    high, low = halves(x)
    return dot32(high, table[0]) + (dot32(low, table[0]) + dot32(high, table[1]))


def to_spectra(signals, first, turn_cos, turn_sin, forward):
    stacked = table_times(first, jnp.concatenate(signals, 1))
    rows = []
    for n in range(len(signals)):
        re = stacked[:HALF, n * 128 : (n + 1) * 128]
        im = stacked[HALF:, n * 128 : (n + 1) * 128]
        rows.append(jnp.concatenate([re * turn_cos + im * turn_sin, im * turn_cos - re * turn_sin], 1))
    spectra = times_table(jnp.concatenate(rows, 0), forward)
    return [spectra[n * HALF : (n + 1) * HALF] for n in range(len(signals))]


def to_signals(spectra, last, turn_cos, turn_sin, backward):
    rows = times_table(jnp.concatenate(spectra, 0), backward)
    columns = []
    for n in range(len(spectra)):
        re = rows[n * HALF : (n + 1) * HALF, :128]
        im = rows[n * HALF : (n + 1) * HALF, 128:]
        columns.append(jnp.concatenate([re * turn_cos - im * turn_sin, re * turn_sin + im * turn_cos], 0))
    return table_times(last, jnp.concatenate(columns, 1))


def product(a, b):
    ar, ai, br, bi = a[:, :128], a[:, 128:], b[:, :128], b[:, 128:]
    return jnp.concatenate([ar * br - ai * bi, ar * bi + ai * br], 1)


def product_conj(a, b):
    ar, ai, br, bi = a[:, :128], a[:, 128:], b[:, :128], b[:, 128:]
    return jnp.concatenate([ar * br + ai * bi, ar * bi - ai * br], 1)


def repeat_kernel(key_ref, value_ref, out_ref, done):
    copies = []
    for n in range(SHARDS // ROW):
        for m, ref in enumerate((key_ref, value_ref)):
            copies.append(pltpu.make_async_copy(ref, out_ref.at[n, m], done.at[n, m]))
    for copy in copies:
        copy.start()
    for copy in copies:
        copy.wait()


def pack_kernel(parts_ref, input_ref, gate_ref, taps_ref, out_ref, wide_ref):
    target = parts_ref[0].astype(jnp.float32)
    for n in range(1, 8):
        target += parts_ref[n].astype(jnp.float32)
    arrays = (target, input_ref[...], gate_ref[...], taps_ref[...])
    for n, array in enumerate(arrays):
        array = array.astype(jnp.float32)
        wide_ref[:, 2 * n, :] = array[:SHARDS]
        wide_ref[:, 2 * n + 1, :] = array[SHARDS:]
    out_ref[...] = wide_ref[...].astype(jnp.bfloat16)


def student_kernel(skip_ref, in_ref, tc, ts, f0, f1, l0, l1, w0, w1, b0, b1, out_ref, wide_in, wide_out):
    wide_in[...] = in_ref[...].astype(jnp.float32)
    rank = lax.axis_index("seq")
    skip = [skip_ref[rank], skip_ref[rank + SHARDS]]
    target, signal, gate, taps = [[wide_in[:, 2 * n + c, :] for c in (0, 1)] for n in range(4)]
    turn = tc[...], ts[...]
    ahead = (f0[...], f1[...]), *turn, (w0[...], w1[...])
    behind = (l0[...], l1[...]), *turn, (b0[...], b1[...])
    spectra = to_spectra(signal + taps, *ahead)
    conv = to_signals([product(spectra[c], spectra[2 + c]) for c in (0, 1)], *behind)
    back = []
    for c in (0, 1):
        output = gate[c] * (conv[:, c * 128 : (c + 1) * 128] + skip[c] * signal[c])
        back.append(gate[c] * (output - target[c]))
    gradient = to_spectra(back, *ahead)
    mixed = [product_conj(spectra[2 + c], gradient[c]) for c in (0, 1)]
    mixed += [product_conj(spectra[c], gradient[c]) for c in (0, 1)]
    signals = to_signals(mixed, *behind)
    scale = (SHARDS * SHARD) ** -0.5
    for c in (0, 1):
        wide_out[:, c, :] = skip[c] * back[c] + signals[:, c * 128 : (c + 1) * 128]
        wide_out[:, 2 + c, :] = scale * signals[:, (2 + c) * 128 : (3 + c) * 128]
    out_ref[...] = wide_out[...].astype(jnp.bfloat16)


def unpack_kernel(in_ref, grad_ref, step_ref, wide_ref):
    wide_ref[...] = in_ref[...].astype(jnp.float32)
    for c in (0, 1):
        grad_ref[c * SHARDS : (c + 1) * SHARDS, :] = wide_ref[:, c, :]
        step_ref[c * SHARDS : (c + 1) * SHARDS, :] = wide_ref[:, 2 + c, :]


def attend_kernel(q_ref, own_ref, sibling_ref, out_ref):
    rank = lax.axis_index("seq")
    row, mine, core = rank // ROW, rank % ROW // 2, rank % 2
    scale = 128 ** -0.5
    order = [row] + [jnp.maximum(row - BACK + r, 0) for r in range(BACK)]
    sources = (own_ref, sibling_ref)
    keys = jnp.concatenate([ref[n, 0] for ref in sources for n in order], 0)
    ones = jnp.ones((10 * SHARD, 128), jnp.bfloat16)
    values = jnp.concatenate([jnp.concatenate([ref[n, 1] for ref in sources for n in order], 0), ones], 1)
    lag = lax.broadcasted_iota(jnp.int32, (SHARD, SHARD), 0) - lax.broadcasted_iota(jnp.int32, (SHARD, SHARD), 1)
    diagonal = lag == 0
    zero = jnp.zeros((SHARD, SHARD), jnp.float32)
    for theirs in range(GROUP):
        ahead = 2 * (mine - theirs) * SHARD
        newest = [lag >= ahead, lag >= ahead + (1 - 2 * core) * SHARD]
        stats = []
        for h in (0, 1):
            scores = lax.dot_general(
                q_ref[theirs, h], keys, (((1,), (1,)), ((), ())), preferred_element_type=jnp.float32
            )
            parts = [scores[:, n * SHARD : (n + 1) * SHARD] for n in range(10)]
            blocks = []
            for source in (0, 1):
                part = parts[5 * source : 5 * source + 5]
                blocks.append(jnp.where(newest[source], part[0], jnp.where(row >= BACK, part[1], NEG)))
                blocks += [jnp.where(row >= BACK - r, part[1 + r], NEG) for r in (1, 2, 3)]
            top = blocks[0]
            for block in blocks[1:]:
                top = jnp.maximum(top, block)
            top = jnp.maximum(jnp.max(top, axis=1, keepdims=True), 0.5 * NEG)
            weights = [jnp.exp((b - top) * scale) for b in blocks]
            spread = []
            for source in (0, 1):
                part = weights[4 * source : 4 * source + 4]
                spread += [jnp.where(newest[source], part[0], zero), jnp.where(newest[source], zero, part[0])]
                spread += part[1:]
            spread = jnp.concatenate([w.astype(jnp.bfloat16) for w in spread], 1)
            sums = jnp.dot(spread, values, preferred_element_type=jnp.float32)
            total = sums[:, 128:]
            safe = jnp.maximum(total, 1e-30)
            out_ref[theirs, h * 128 : (h + 1) * 128, :] = (sums[:, :128] / safe).astype(jnp.bfloat16)
            log_sum = jnp.where(total > 0.0, top * scale + jnp.log(safe), NEG)
            log_sum = jnp.sum(jnp.where(diagonal, log_sum, 0.0), axis=0, keepdims=True)
            high = log_sum.astype(jnp.bfloat16).astype(jnp.float32)
            rest = log_sum - high
            middle = rest.astype(jnp.bfloat16).astype(jnp.float32)
            stats += [high, middle, rest - middle]
        stats.append(jnp.zeros((10, 128), jnp.float32))
        out_ref[theirs, 256:272, :] = jnp.concatenate(stats, 0).astype(jnp.bfloat16)


def merge_kernel(parts_ref, proj_ref, out_ref):
    shares = []
    for h in (0, 1):
        sums = []
        for p in range(GROUP):
            stats = parts_ref[p, 256:272, :].astype(jnp.float32)
            sums.append(stats[3 * h : 3 * h + 1] + stats[3 * h + 1 : 3 * h + 2] + stats[3 * h + 2 : 3 * h + 3])
        sums = jnp.concatenate(sums, 0)
        share = jnp.exp(sums - jnp.max(sums, axis=0, keepdims=True))
        shares.append(share / jnp.sum(share, axis=0, keepdims=True))
    shares.append(jnp.zeros((128 - 2 * GROUP, 128), jnp.float32))
    shares = jnp.concatenate(shares, 0).T
    heads = []
    for h in (0, 1):
        merged = None
        for p in range(GROUP):
            part = parts_ref[p, h * 128 : (h + 1) * 128, :].astype(jnp.float32)
            part = shares[:, h * GROUP + p : h * GROUP + p + 1] * part
            merged = part if merged is None else merged + part
        heads.append(merged.astype(jnp.bfloat16))
    attended = jnp.concatenate(heads, 1)
    target = lax.dot_general(
        proj_ref[...], attended, (((1,), (1,)), ((), ())), preferred_element_type=jnp.float32
    )
    out_ref[...] = target.reshape(8, 128, 128).astype(jnp.bfloat16)


VMEM = pl.BlockSpec(memory_space=pltpu.VMEM)
SMEM = pl.BlockSpec(memory_space=pltpu.SMEM)


def near(x):
    return pltpu.with_memory_space_constraint(x, pltpu.VMEM)


def call_repeat(key, value):
    anywhere = pl.BlockSpec(memory_space=pl.ANY)
    return pl.pallas_call(
        repeat_kernel,
        out_shape=jax.ShapeDtypeStruct((SHARDS // ROW, 2, SHARD, 128), jnp.bfloat16),
        in_specs=[anywhere] * 2,
        out_specs=anywhere,
        scratch_shapes=[pltpu.SemaphoreType.DMA((SHARDS // ROW, 2))],
    )(key, value)


def call_pack(parts, *inputs):
    return pl.pallas_call(
        pack_kernel,
        out_shape=pltpu.VMEM((SHARDS, 8, 128), jnp.bfloat16),
        in_specs=[VMEM] * 4,
        out_specs=VMEM,
        scratch_shapes=[pltpu.VMEM((SHARDS, 8, 128), jnp.float32)],
    )(near(parts), *[near(x) for x in inputs])


def call_student(skip, packed, tables):
    return pl.pallas_call(
        student_kernel,
        out_shape=pltpu.VMEM((SHARDS, 4, 128), jnp.bfloat16),
        in_specs=[SMEM] + [VMEM] * 11,
        out_specs=VMEM,
        scratch_shapes=[pltpu.VMEM((SHARDS, 8, 128), jnp.float32), pltpu.VMEM((SHARDS, 4, 128), jnp.float32)],
    )(skip, near(packed), *tables)


def call_unpack(out):
    return pl.pallas_call(
        unpack_kernel,
        out_shape=(jax.ShapeDtypeStruct((128, 128), jnp.float32),) * 2,
        in_specs=[VMEM],
        out_specs=(VMEM,) * 2,
        scratch_shapes=[pltpu.VMEM((SHARDS, 4, 128), jnp.float32)],
    )(near(out))


def call_attend(queries, own, sibling):
    return pl.pallas_call(
        attend_kernel,
        out_shape=pltpu.VMEM((GROUP, 272, 128), jnp.bfloat16),
        in_specs=[VMEM] * 3,
        out_specs=VMEM,
    )(near(queries), near(own), near(sibling))


def call_merge(parts, proj):
    return pl.pallas_call(
        merge_kernel,
        out_shape=pltpu.VMEM((8, 128, 128), jnp.bfloat16),
        in_specs=[VMEM] * 2,
        out_specs=VMEM,
    )(near(parts), near(proj))


def body(
    query_heads,
    key_heads,
    value_heads,
    distill_proj,
    conv_input,
    gate_input,
    filter_taps,
    skip_gain,
):
    tables = [near(jnp.asarray(t)) for t in transform_tables()]
    lines = range(SHARDS // ROW)
    groups = [[y * ROW + 2 * x + core for x in range(GROUP)] for y in lines for core in (0, 1)]
    columns = [[y * ROW + p for y in lines] for p in range(ROW)]
    pairs = call_repeat(key_heads[:, 0], value_heads[:, 0])
    own = lax.all_to_all(pairs, "seq", 0, 0, axis_index_groups=columns)
    queries = lax.all_gather(jnp.transpose(query_heads, (1, 0, 2)), "seq", axis_index_groups=groups)
    proj = distill_proj.reshape(256, 1024).T
    own, queries, proj = lax.optimization_barrier((own, queries, proj))
    sibling = lax.ppermute(own, "seq", [(i, i ^ 1) for i in range(SHARDS)])
    parts = call_attend(queries, own, sibling)
    parts = lax.all_to_all(parts, "seq", 0, 0, axis_index_groups=groups)
    target = call_merge(parts, proj)
    target = lax.all_to_all(target, ("role", "head"), 0, 0)
    packed = call_pack(target, conv_input, gate_input, filter_taps)
    packed = lax.all_to_all(packed, "seq", 0, 0)
    out = call_student(skip_gain, packed, tables)
    out = lax.all_to_all(out, "seq", 0, 0)
    return call_unpack(out)


def solution(mesh):
    in_specs = (
        P("seq", ("role", "head"), None),
        P("seq", ("role", "head"), None),
        P("seq", ("role", "head"), None),
        P(("role", "head"), None, None),
        P(("role", "head"), "seq"),
        P(("role", "head"), "seq"),
        P(("role", "head"), "seq"),
        P(("role", "head")),
    )
    out_specs = (P(("role", "head"), "seq"), P(("role", "head"), "seq"))
    return jax.shard_map(body, mesh=mesh, in_specs=in_specs, out_specs=out_specs, check_vma=False)
```

```python
import jax
import jax.numpy as jnp
import ml_dtypes
import numpy as np
from jax import lax
from jax.experimental import pallas as pl
from jax.experimental.pallas import tpu as pltpu
from jax.sharding import PartitionSpec as P

WINDOW = 4096
SHARD = 128
ROW = 8
GROUP = 4
BACK = WINDOW // (ROW * SHARD)
SHARDS = 64
HALF = 72
NEG = -1e30


def transform_tables():
    length = 2 * SHARDS * SHARD
    k1 = np.arange(HALF)[:, None]
    live = (k1 <= SHARDS).astype(np.float64)
    a = np.arange(SHARDS)[None, :]
    angle = 2.0 * np.pi * ((k1 * a) % 128) / 128
    first = np.concatenate([live * np.cos(angle), -live * np.sin(angle)], 0)
    weight = live * np.where((k1 == 0) | (k1 == SHARDS), 1.0, 2.0) / length
    last = np.concatenate([weight * np.cos(angle), -weight * np.sin(angle)], 0).T
    b = np.arange(128)[None, :]
    turn = 2.0 * np.pi * (k1 * b) / length
    b2 = np.arange(128)[:, None]
    grid = 2.0 * np.pi * ((b2 * b) % 128) / 128
    cosine, sine = np.cos(grid), np.sin(grid)
    forward = np.block([[cosine, -sine], [sine, cosine]])
    backward = np.block([[cosine, sine], [-sine, cosine]])
    tables = [np.asarray(t, np.float32) for t in (np.cos(turn), np.sin(turn))]
    for table, axis in ((first, 1), (last, 1), (forward, 0), (backward, 0)):
        high = np.asarray(table, ml_dtypes.bfloat16)
        low = np.asarray(table - high.astype(np.float64), ml_dtypes.bfloat16)
        tables.append(np.concatenate([high, high, low], axis))
    return tables


def triple(x, axis):
    high = x.astype(jnp.bfloat16)
    low = (x - high.astype(jnp.float32)).astype(jnp.bfloat16)
    return jnp.concatenate([high, low, high], axis)


def table_times(table, x):
    return jnp.dot(table, triple(x, 0), preferred_element_type=jnp.float32)


def times_table(x, table):
    return jnp.dot(triple(x, 1), table, preferred_element_type=jnp.float32)


def to_spectra(signals, first, turn_cos, turn_sin, forward):
    stacked = table_times(first, jnp.concatenate(signals, 1))
    rows = []
    for n in range(len(signals)):
        re = stacked[:HALF, n * 128 : (n + 1) * 128]
        im = stacked[HALF:, n * 128 : (n + 1) * 128]
        rows.append(jnp.concatenate([re * turn_cos + im * turn_sin, im * turn_cos - re * turn_sin], 1))
    spectra = times_table(jnp.concatenate(rows, 0), forward)
    return [spectra[n * HALF : (n + 1) * HALF] for n in range(len(signals))]


def to_signals(spectra, last, turn_cos, turn_sin, backward):
    rows = times_table(jnp.concatenate(spectra, 0), backward)
    columns = []
    for n in range(len(spectra)):
        re = rows[n * HALF : (n + 1) * HALF, :128]
        im = rows[n * HALF : (n + 1) * HALF, 128:]
        columns.append(jnp.concatenate([re * turn_cos - im * turn_sin, re * turn_sin + im * turn_cos], 0))
    return table_times(last, jnp.concatenate(columns, 1))


def product(a, b):
    ar, ai, br, bi = a[:, :128], a[:, 128:], b[:, :128], b[:, 128:]
    return jnp.concatenate([ar * br - ai * bi, ar * bi + ai * br], 1)


def product_conj(a, b):
    ar, ai, br, bi = a[:, :128], a[:, 128:], b[:, :128], b[:, 128:]
    return jnp.concatenate([ar * br + ai * bi, ar * bi - ai * br], 1)


def repeat_kernel(key_ref, value_ref, out_ref, held, arrived, done):
    loads = []
    for m, ref in enumerate((key_ref, value_ref)):
        loads.append(pltpu.make_async_copy(ref, held.at[m], arrived.at[m]))
        loads[m].start()
    copies = []
    for m in (0, 1):
        loads[m].wait()
        for n in range(SHARDS // ROW):
            copies.append(pltpu.make_async_copy(held.at[m], out_ref.at[n, m], done.at[n, m]))
            copies[-1].start()
    for copy in copies:
        copy.wait()


def pack_kernel(parts_ref, input_ref, gate_ref, taps_ref, out_ref, wide_ref):
    target = parts_ref[0].astype(jnp.float32)
    for n in range(1, 8):
        target += parts_ref[n].astype(jnp.float32)
    arrays = (target, input_ref[...], gate_ref[...], taps_ref[...])
    for n, array in enumerate(arrays):
        array = array.astype(jnp.float32)
        wide_ref[:, 2 * n, :] = array[:SHARDS]
        wide_ref[:, 2 * n + 1, :] = array[SHARDS:]
    out_ref[...] = wide_ref[...].astype(jnp.bfloat16)


def student_kernel(skip_ref, in_ref, tc, ts, first, last, forward, backward, out_ref, wide_in, wide_out):
    wide_in[...] = in_ref[...].astype(jnp.float32)
    rank = lax.axis_index("seq")
    skip = [skip_ref[rank], skip_ref[rank + SHARDS]]
    target, signal, gate, taps = [[wide_in[:, 2 * n + c, :] for c in (0, 1)] for n in range(4)]
    turn = tc[...], ts[...]
    ahead = first[...], *turn, forward[...]
    behind = last[...], *turn, backward[...]
    spectra = to_spectra(signal + taps, *ahead)
    conv = to_signals([product(spectra[c], spectra[2 + c]) for c in (0, 1)], *behind)
    back = []
    for c in (0, 1):
        output = gate[c] * (conv[:, c * 128 : (c + 1) * 128] + skip[c] * signal[c])
        back.append(gate[c] * (output - target[c]))
    gradient = to_spectra(back, *ahead)
    mixed = [product_conj(spectra[2 + c], gradient[c]) for c in (0, 1)]
    mixed += [product_conj(spectra[c], gradient[c]) for c in (0, 1)]
    signals = to_signals(mixed, *behind)
    scale = (SHARDS * SHARD) ** -0.5
    for c in (0, 1):
        wide_out[:, c, :] = skip[c] * back[c] + signals[:, c * 128 : (c + 1) * 128]
        wide_out[:, 2 + c, :] = scale * signals[:, (2 + c) * 128 : (3 + c) * 128]
    out_ref[...] = wide_out[...].astype(jnp.bfloat16)


def unpack_kernel(in_ref, grad_ref, step_ref, wide_ref):
    wide_ref[...] = in_ref[...].astype(jnp.float32)
    for c in (0, 1):
        grad_ref[c * SHARDS : (c + 1) * SHARDS, :] = wide_ref[:, c, :]
        step_ref[c * SHARDS : (c + 1) * SHARDS, :] = wide_ref[:, 2 + c, :]


def attend_kernel(q_ref, own_ref, sibling_ref, out_ref):
    rank = lax.axis_index("seq")
    row, mine, core = rank // ROW, rank % ROW // 2, rank % 2
    scale = 128 ** -0.5
    order = [row] + [jnp.maximum(row - BACK + r, 0) for r in range(BACK)]
    sources = (own_ref, sibling_ref)
    keys = jnp.concatenate([ref[n, 0] for ref in sources for n in order], 0)
    ones = jnp.ones((10 * SHARD, 128), jnp.bfloat16)
    values = jnp.concatenate([jnp.concatenate([ref[n, 1] for ref in sources for n in order], 0), ones], 1)
    lag = lax.broadcasted_iota(jnp.int32, (SHARD, SHARD), 0) - lax.broadcasted_iota(jnp.int32, (SHARD, SHARD), 1)
    diagonal = lag == 0
    zero = jnp.zeros((SHARD, SHARD), jnp.float32)
    for theirs in range(GROUP):
        ahead = 2 * (mine - theirs) * SHARD
        newest = [lag >= ahead, lag >= ahead + (1 - 2 * core) * SHARD]
        stats = []
        for h in (0, 1):
            scores = lax.dot_general(
                q_ref[theirs, h], keys, (((1,), (1,)), ((), ())), preferred_element_type=jnp.float32
            )
            parts = [scores[:, n * SHARD : (n + 1) * SHARD] for n in range(10)]
            blocks = []
            for source in (0, 1):
                part = parts[5 * source : 5 * source + 5]
                blocks.append(jnp.where(newest[source], part[0], jnp.where(row >= BACK, part[1], NEG)))
                blocks += [jnp.where(row >= BACK - r, part[1 + r], NEG) for r in (1, 2, 3)]
            top = blocks[0]
            for block in blocks[1:]:
                top = jnp.maximum(top, block)
            top = jnp.maximum(jnp.max(top, axis=1, keepdims=True), 0.5 * NEG)
            weights = [jnp.exp((b - top) * scale) for b in blocks]
            spread = []
            for source in (0, 1):
                part = weights[4 * source : 4 * source + 4]
                spread += [jnp.where(newest[source], part[0], zero), jnp.where(newest[source], zero, part[0])]
                spread += part[1:]
            spread = jnp.concatenate([w.astype(jnp.bfloat16) for w in spread], 1)
            sums = jnp.dot(spread, values, preferred_element_type=jnp.float32)
            total = sums[:, 128:]
            safe = jnp.maximum(total, 1e-30)
            out_ref[theirs, h * 128 : (h + 1) * 128, :] = (sums[:, :128] / safe).astype(jnp.bfloat16)
            log_sum = jnp.where(total > 0.0, top * scale + jnp.log(safe), NEG)
            log_sum = jnp.sum(jnp.where(diagonal, log_sum, 0.0), axis=0, keepdims=True)
            high = log_sum.astype(jnp.bfloat16).astype(jnp.float32)
            rest = log_sum - high
            middle = rest.astype(jnp.bfloat16).astype(jnp.float32)
            stats += [high, middle, rest - middle]
        stats.append(jnp.zeros((10, 128), jnp.float32))
        out_ref[theirs, 256:272, :] = jnp.concatenate(stats, 0).astype(jnp.bfloat16)


def merge_kernel(parts_ref, proj_ref, out_ref):
    shares = []
    for h in (0, 1):
        sums = []
        for p in range(GROUP):
            stats = parts_ref[p, 256:272, :].astype(jnp.float32)
            sums.append(stats[3 * h : 3 * h + 1] + stats[3 * h + 1 : 3 * h + 2] + stats[3 * h + 2 : 3 * h + 3])
        sums = jnp.concatenate(sums, 0)
        share = jnp.exp(sums - jnp.max(sums, axis=0, keepdims=True))
        shares.append(share / jnp.sum(share, axis=0, keepdims=True))
    shares.append(jnp.zeros((128 - 2 * GROUP, 128), jnp.float32))
    shares = jnp.concatenate(shares, 0).T
    heads = []
    for h in (0, 1):
        merged = None
        for p in range(GROUP):
            part = parts_ref[p, h * 128 : (h + 1) * 128, :].astype(jnp.float32)
            part = shares[:, h * GROUP + p : h * GROUP + p + 1] * part
            merged = part if merged is None else merged + part
        heads.append(merged.astype(jnp.bfloat16))
    attended = jnp.concatenate(heads, 1)
    target = lax.dot_general(
        proj_ref[...], attended, (((1,), (1,)), ((), ())), preferred_element_type=jnp.float32
    )
    out_ref[...] = target.reshape(8, 128, 128).astype(jnp.bfloat16)


VMEM = pl.BlockSpec(memory_space=pltpu.VMEM)
SMEM = pl.BlockSpec(memory_space=pltpu.SMEM)


def near(x):
    return pltpu.with_memory_space_constraint(x, pltpu.VMEM)


def call_repeat(key, value):
    anywhere = pl.BlockSpec(memory_space=pl.ANY)
    return pl.pallas_call(
        repeat_kernel,
        out_shape=jax.ShapeDtypeStruct((SHARDS // ROW, 2, SHARD, 128), jnp.bfloat16),
        in_specs=[anywhere] * 2,
        out_specs=anywhere,
        scratch_shapes=[
            pltpu.VMEM((2, SHARD, 128), jnp.bfloat16),
            pltpu.SemaphoreType.DMA((2,)),
            pltpu.SemaphoreType.DMA((SHARDS // ROW, 2)),
        ],
    )(key, value)


def call_pack(parts, *inputs):
    return pl.pallas_call(
        pack_kernel,
        out_shape=pltpu.VMEM((SHARDS, 8, 128), jnp.bfloat16),
        in_specs=[VMEM] * 4,
        out_specs=VMEM,
        scratch_shapes=[pltpu.VMEM((SHARDS, 8, 128), jnp.float32)],
    )(near(parts), *[near(x) for x in inputs])


def call_student(skip, packed, tables):
    return pl.pallas_call(
        student_kernel,
        out_shape=pltpu.VMEM((SHARDS, 4, 128), jnp.bfloat16),
        in_specs=[SMEM] + [VMEM] * 7,
        out_specs=VMEM,
        scratch_shapes=[pltpu.VMEM((SHARDS, 8, 128), jnp.float32), pltpu.VMEM((SHARDS, 4, 128), jnp.float32)],
    )(skip, near(packed), *tables)


def call_unpack(out):
    return pl.pallas_call(
        unpack_kernel,
        out_shape=(jax.ShapeDtypeStruct((128, 128), jnp.float32),) * 2,
        in_specs=[VMEM],
        out_specs=(VMEM,) * 2,
        scratch_shapes=[pltpu.VMEM((SHARDS, 4, 128), jnp.float32)],
    )(near(out))


def call_attend(queries, own, sibling):
    return pl.pallas_call(
        attend_kernel,
        out_shape=pltpu.VMEM((GROUP, 272, 128), jnp.bfloat16),
        in_specs=[VMEM] * 3,
        out_specs=VMEM,
    )(near(queries), near(own), near(sibling))


def call_merge(parts, proj):
    return pl.pallas_call(
        merge_kernel,
        out_shape=pltpu.VMEM((8, 128, 128), jnp.bfloat16),
        in_specs=[VMEM] * 2,
        out_specs=VMEM,
    )(near(parts), near(proj))


def body(
    query_heads,
    key_heads,
    value_heads,
    distill_proj,
    conv_input,
    gate_input,
    filter_taps,
    skip_gain,
):
    tables = [near(jnp.asarray(t)) for t in transform_tables()]
    lines = range(SHARDS // ROW)
    groups = [[y * ROW + 2 * x + core for x in range(GROUP)] for y in lines for core in (0, 1)]
    columns = [[y * ROW + p for y in lines] for p in range(ROW)]
    pairs = call_repeat(key_heads[:, 0], value_heads[:, 0])
    own = lax.all_to_all(pairs, "seq", 0, 0, axis_index_groups=columns)
    queries = lax.all_gather(jnp.transpose(query_heads, (1, 0, 2)), "seq", axis_index_groups=groups)
    proj = distill_proj.reshape(256, 1024).T
    own, queries, proj = lax.optimization_barrier((own, queries, proj))
    sibling = lax.ppermute(own, "seq", [(i, i ^ 1) for i in range(SHARDS)])
    parts = call_attend(queries, own, sibling)
    parts = lax.all_to_all(parts, "seq", 0, 0, axis_index_groups=groups)
    target = call_merge(parts, proj)
    target = lax.all_to_all(target, ("role", "head"), 0, 0)
    packed = call_pack(target, conv_input, gate_input, filter_taps)
    packed = lax.all_to_all(packed, "seq", 0, 0)
    out = call_student(skip_gain, packed, tables)
    out = lax.all_to_all(out, "seq", 0, 0)
    return call_unpack(out)


def solution(mesh):
    in_specs = (
        P("seq", ("role", "head"), None),
        P("seq", ("role", "head"), None),
        P("seq", ("role", "head"), None),
        P(("role", "head"), None, None),
        P(("role", "head"), "seq"),
        P(("role", "head"), "seq"),
        P(("role", "head"), "seq"),
        P(("role", "head")),
    )
    out_specs = (P(("role", "head"), "seq"), P(("role", "head"), "seq"))
    return jax.shard_map(body, mesh=mesh, in_specs=in_specs, out_specs=out_specs, check_vma=False)
```

```python
import jax
import jax.numpy as jnp
import ml_dtypes
import numpy as np
from jax import lax
from jax.experimental import pallas as pl
from jax.experimental.pallas import tpu as pltpu
from jax.sharding import PartitionSpec as P

WINDOW = 4096
SHARD = 128
ROW = 8
GROUP = 4
BACK = WINDOW // (ROW * SHARD)
SHARDS = 64
HALF = 72
NEG = -1e30


def transform_tables():
    length = 2 * SHARDS * SHARD
    k1 = np.arange(HALF)[:, None]
    live = (k1 <= SHARDS).astype(np.float64)
    a = np.arange(SHARDS)[None, :]
    angle = 2.0 * np.pi * ((k1 * a) % 128) / 128
    first = np.concatenate([live * np.cos(angle), -live * np.sin(angle)], 0)
    weight = live * np.where((k1 == 0) | (k1 == SHARDS), 1.0, 2.0) / length
    last = np.concatenate([weight * np.cos(angle), -weight * np.sin(angle)], 0).T
    b = np.arange(128)[None, :]
    turn = 2.0 * np.pi * (k1 * b) / length
    b2 = np.arange(128)[:, None]
    grid = 2.0 * np.pi * ((b2 * b) % 128) / 128
    cosine, sine = np.cos(grid), np.sin(grid)
    forward = np.block([[cosine, -sine], [sine, cosine]])
    backward = np.block([[cosine, sine], [-sine, cosine]])
    tables = [np.asarray(t, np.float32) for t in (np.cos(turn), np.sin(turn))]
    for table, axis in ((first, 1), (last, 1), (forward, 0), (backward, 0)):
        high = np.asarray(table, ml_dtypes.bfloat16)
        low = np.asarray(table - high.astype(np.float64), ml_dtypes.bfloat16)
        tables.append(np.concatenate([high, high, low], axis))
    return tables


def triple(x, axis):
    high = x.astype(jnp.bfloat16)
    low = (x - high.astype(jnp.float32)).astype(jnp.bfloat16)
    return jnp.concatenate([high, low, high], axis)


def table_times(table, x):
    return jnp.dot(table, triple(x, 0), preferred_element_type=jnp.float32)


def times_table(x, table):
    return jnp.dot(triple(x, 1), table, preferred_element_type=jnp.float32)


def to_spectra(signals, first, turn_cos, turn_sin, forward):
    stacked = table_times(first, jnp.concatenate(signals, 1))
    rows = []
    for n in range(len(signals)):
        re = stacked[:HALF, n * 128 : (n + 1) * 128]
        im = stacked[HALF:, n * 128 : (n + 1) * 128]
        rows.append(jnp.concatenate([re * turn_cos + im * turn_sin, im * turn_cos - re * turn_sin], 1))
    spectra = times_table(jnp.concatenate(rows, 0), forward)
    return [spectra[n * HALF : (n + 1) * HALF] for n in range(len(signals))]


def to_signals(spectra, last, turn_cos, turn_sin, backward):
    rows = times_table(jnp.concatenate(spectra, 0), backward)
    columns = []
    for n in range(len(spectra)):
        re = rows[n * HALF : (n + 1) * HALF, :128]
        im = rows[n * HALF : (n + 1) * HALF, 128:]
        columns.append(jnp.concatenate([re * turn_cos - im * turn_sin, re * turn_sin + im * turn_cos], 0))
    return table_times(last, jnp.concatenate(columns, 1))


def product(a, b):
    ar, ai, br, bi = a[:, :128], a[:, 128:], b[:, :128], b[:, 128:]
    return jnp.concatenate([ar * br - ai * bi, ar * bi + ai * br], 1)


def product_conj(a, b):
    ar, ai, br, bi = a[:, :128], a[:, 128:], b[:, :128], b[:, 128:]
    return jnp.concatenate([ar * br + ai * bi, ar * bi - ai * br], 1)


def join_kernel(*refs):
    for n in range(BACK + 1):
        refs[-1][n] = refs[n][...]


def pack_kernel(parts_ref, input_ref, gate_ref, taps_ref, out_ref, wide_ref):
    target = parts_ref[0].astype(jnp.float32)
    for n in range(1, 8):
        target += parts_ref[n].astype(jnp.float32)
    arrays = (target, input_ref[...], gate_ref[...], taps_ref[...])
    for n, array in enumerate(arrays):
        array = array.astype(jnp.float32)
        wide_ref[:, 2 * n, :] = array[:SHARDS]
        wide_ref[:, 2 * n + 1, :] = array[SHARDS:]
    out_ref[...] = wide_ref[...].astype(jnp.bfloat16)


def student_kernel(skip_ref, in_ref, tc, ts, first, last, forward, backward, out_ref, wide_in, wide_out):
    wide_in[...] = in_ref[...].astype(jnp.float32)
    rank = lax.axis_index("seq")
    skip = [skip_ref[rank], skip_ref[rank + SHARDS]]
    target, signal, gate, taps = [[wide_in[:, 2 * n + c, :] for c in (0, 1)] for n in range(4)]
    turn = tc[...], ts[...]
    ahead = first[...], *turn, forward[...]
    behind = last[...], *turn, backward[...]
    spectra = to_spectra(signal + taps, *ahead)
    conv = to_signals([product(spectra[c], spectra[2 + c]) for c in (0, 1)], *behind)
    back = []
    for c in (0, 1):
        output = gate[c] * (conv[:, c * 128 : (c + 1) * 128] + skip[c] * signal[c])
        back.append(gate[c] * (output - target[c]))
    gradient = to_spectra(back, *ahead)
    mixed = [product_conj(spectra[2 + c], gradient[c]) for c in (0, 1)]
    mixed += [product_conj(spectra[c], gradient[c]) for c in (0, 1)]
    signals = to_signals(mixed, *behind)
    scale = (SHARDS * SHARD) ** -0.5
    for c in (0, 1):
        wide_out[:, c, :] = skip[c] * back[c] + signals[:, c * 128 : (c + 1) * 128]
        wide_out[:, 2 + c, :] = scale * signals[:, (2 + c) * 128 : (3 + c) * 128]
    out_ref[...] = wide_out[...].astype(jnp.bfloat16)


def unpack_kernel(in_ref, grad_ref, step_ref, wide_ref):
    wide_ref[...] = in_ref[...].astype(jnp.float32)
    for c in (0, 1):
        grad_ref[c * SHARDS : (c + 1) * SHARDS, :] = wide_ref[:, c, :]
        step_ref[c * SHARDS : (c + 1) * SHARDS, :] = wide_ref[:, 2 + c, :]


def attend_kernel(q_ref, own_ref, sibling_ref, out_ref):
    rank = lax.axis_index("seq")
    row, mine, core = rank // ROW, rank % ROW // 2, rank % 2
    scale = 128 ** -0.5
    sources = (own_ref, sibling_ref)
    keys = jnp.concatenate([ref[n, 0] for ref in sources for n in range(BACK + 1)], 0)
    ones = jnp.ones((10 * SHARD, 128), jnp.bfloat16)
    values = [ref[n, 1] for ref in sources for n in range(BACK + 1)]
    values = jnp.concatenate([jnp.concatenate(values, 0), ones], 1)
    lag = lax.broadcasted_iota(jnp.int32, (SHARD, SHARD), 0) - lax.broadcasted_iota(jnp.int32, (SHARD, SHARD), 1)
    diagonal = lag == 0
    zero = jnp.zeros((SHARD, SHARD), jnp.float32)
    for theirs in range(GROUP):
        ahead = 2 * (mine - theirs) * SHARD
        newest = [lag >= ahead, lag >= ahead + (1 - 2 * core) * SHARD]
        stats = []
        for h in (0, 1):
            scores = lax.dot_general(
                q_ref[theirs, h], keys, (((1,), (1,)), ((), ())), preferred_element_type=jnp.float32
            )
            parts = [scores[:, n * SHARD : (n + 1) * SHARD] for n in range(10)]
            blocks = []
            for source in (0, 1):
                part = parts[5 * source : 5 * source + 5]
                blocks.append(jnp.where(newest[source], part[0], jnp.where(row >= BACK, part[1], NEG)))
                blocks += [jnp.where(row >= BACK - r, part[1 + r], NEG) for r in (1, 2, 3)]
            top = blocks[0]
            for block in blocks[1:]:
                top = jnp.maximum(top, block)
            top = jnp.maximum(jnp.max(top, axis=1, keepdims=True), 0.5 * NEG)
            weights = [jnp.exp((b - top) * scale) for b in blocks]
            spread = []
            for source in (0, 1):
                part = weights[4 * source : 4 * source + 4]
                spread += [jnp.where(newest[source], part[0], zero), jnp.where(newest[source], zero, part[0])]
                spread += part[1:]
            spread = jnp.concatenate([w.astype(jnp.bfloat16) for w in spread], 1)
            sums = jnp.dot(spread, values, preferred_element_type=jnp.float32)
            total = sums[:, 128:]
            safe = jnp.maximum(total, 1e-30)
            out_ref[theirs, h * 128 : (h + 1) * 128, :] = (sums[:, :128] / safe).astype(jnp.bfloat16)
            log_sum = jnp.where(total > 0.0, top * scale + jnp.log(safe), NEG)
            log_sum = jnp.sum(jnp.where(diagonal, log_sum, 0.0), axis=0, keepdims=True)
            high = log_sum.astype(jnp.bfloat16).astype(jnp.float32)
            rest = log_sum - high
            middle = rest.astype(jnp.bfloat16).astype(jnp.float32)
            stats += [high, middle, rest - middle]
        stats.append(jnp.zeros((10, 128), jnp.float32))
        out_ref[theirs, 256:272, :] = jnp.concatenate(stats, 0).astype(jnp.bfloat16)


def merge_kernel(parts_ref, proj_ref, out_ref):
    shares = []
    for h in (0, 1):
        sums = []
        for p in range(GROUP):
            stats = parts_ref[p, 256:272, :].astype(jnp.float32)
            sums.append(stats[3 * h : 3 * h + 1] + stats[3 * h + 1 : 3 * h + 2] + stats[3 * h + 2 : 3 * h + 3])
        sums = jnp.concatenate(sums, 0)
        share = jnp.exp(sums - jnp.max(sums, axis=0, keepdims=True))
        shares.append(share / jnp.sum(share, axis=0, keepdims=True))
    shares.append(jnp.zeros((128 - 2 * GROUP, 128), jnp.float32))
    shares = jnp.concatenate(shares, 0).T
    heads = []
    for h in (0, 1):
        merged = None
        for p in range(GROUP):
            part = parts_ref[p, h * 128 : (h + 1) * 128, :].astype(jnp.float32)
            part = shares[:, h * GROUP + p : h * GROUP + p + 1] * part
            merged = part if merged is None else merged + part
        heads.append(merged.astype(jnp.bfloat16))
    attended = jnp.concatenate(heads, 1)
    target = lax.dot_general(
        proj_ref[...], attended, (((1,), (1,)), ((), ())), preferred_element_type=jnp.float32
    )
    out_ref[...] = target.reshape(8, 128, 128).astype(jnp.bfloat16)


VMEM = pl.BlockSpec(memory_space=pltpu.VMEM)
SMEM = pl.BlockSpec(memory_space=pltpu.SMEM)


def near(x):
    return pltpu.with_memory_space_constraint(x, pltpu.VMEM)


def call_join(blocks):
    return pl.pallas_call(
        join_kernel,
        out_shape=pltpu.VMEM((BACK + 1, 2, SHARD, 128), jnp.bfloat16),
        in_specs=[VMEM] * (BACK + 1),
        out_specs=VMEM,
    )(*[near(block) for block in blocks])


def call_pack(parts, *inputs):
    return pl.pallas_call(
        pack_kernel,
        out_shape=pltpu.VMEM((SHARDS, 8, 128), jnp.bfloat16),
        in_specs=[VMEM] * 4,
        out_specs=VMEM,
        scratch_shapes=[pltpu.VMEM((SHARDS, 8, 128), jnp.float32)],
    )(near(parts), *[near(x) for x in inputs])


def call_student(skip, packed, tables):
    return pl.pallas_call(
        student_kernel,
        out_shape=pltpu.VMEM((SHARDS, 4, 128), jnp.bfloat16),
        in_specs=[SMEM] + [VMEM] * 7,
        out_specs=VMEM,
        scratch_shapes=[pltpu.VMEM((SHARDS, 8, 128), jnp.float32), pltpu.VMEM((SHARDS, 4, 128), jnp.float32)],
    )(skip, near(packed), *tables)


def call_unpack(out):
    return pl.pallas_call(
        unpack_kernel,
        out_shape=(jax.ShapeDtypeStruct((128, 128), jnp.float32),) * 2,
        in_specs=[VMEM],
        out_specs=(VMEM,) * 2,
        scratch_shapes=[pltpu.VMEM((SHARDS, 4, 128), jnp.float32)],
    )(near(out))


def call_attend(queries, own, sibling):
    return pl.pallas_call(
        attend_kernel,
        out_shape=pltpu.VMEM((GROUP, 272, 128), jnp.bfloat16),
        in_specs=[VMEM] * 3,
        out_specs=VMEM,
    )(near(queries), near(own), near(sibling))


def call_merge(parts, proj):
    return pl.pallas_call(
        merge_kernel,
        out_shape=pltpu.VMEM((8, 128, 128), jnp.bfloat16),
        in_specs=[VMEM] * 2,
        out_specs=VMEM,
    )(near(parts), near(proj))


def body(
    query_heads,
    key_heads,
    value_heads,
    distill_proj,
    conv_input,
    gate_input,
    filter_taps,
    skip_gain,
):
    tables = [near(jnp.asarray(t)) for t in transform_tables()]
    lines = range(SHARDS // ROW)
    groups = [[y * ROW + 2 * x + core for x in range(GROUP)] for y in lines for core in (0, 1)]
    queries = jnp.transpose(query_heads, (1, 0, 2))
    queries = lax.all_to_all(
        jnp.broadcast_to(queries, (GROUP,) + queries.shape), "seq", 0, 0, axis_index_groups=groups
    )
    block = jnp.stack([key_heads[:, 0], value_heads[:, 0]])
    blocks = [
        lax.ppermute(block, "seq", [(i, i + ROW * k) for i in range(SHARDS - ROW * k)])
        for k in range(1, BACK + 1)
    ]
    proj = distill_proj.reshape(256, 1024).T
    own = call_join([block] + blocks[::-1])
    queries, proj, own = lax.optimization_barrier((queries, proj, own))
    sibling = lax.ppermute(own, "seq", [(i, i ^ 1) for i in range(SHARDS)])
    parts = call_attend(queries, own, sibling)
    parts = lax.all_to_all(parts, "seq", 0, 0, axis_index_groups=groups)
    target = call_merge(parts, proj)
    target = lax.all_to_all(target, ("role", "head"), 0, 0)
    packed = call_pack(target, conv_input, gate_input, filter_taps)
    packed = lax.all_to_all(packed, "seq", 0, 0)
    out = call_student(skip_gain, packed, tables)
    out = lax.all_to_all(out, "seq", 0, 0)
    return call_unpack(out)


def solution(mesh):
    in_specs = (
        P("seq", ("role", "head"), None),
        P("seq", ("role", "head"), None),
        P("seq", ("role", "head"), None),
        P(("role", "head"), None, None),
        P(("role", "head"), "seq"),
        P(("role", "head"), "seq"),
        P(("role", "head"), "seq"),
        P(("role", "head")),
    )
    out_specs = (P(("role", "head"), "seq"), P(("role", "head"), "seq"))
    return jax.shard_map(body, mesh=mesh, in_specs=in_specs, out_specs=out_specs, check_vma=False)
```

```python
import jax
import jax.numpy as jnp
import ml_dtypes
import numpy as np
from jax import lax
from jax.experimental import pallas as pl
from jax.experimental.pallas import tpu as pltpu
from jax.sharding import PartitionSpec as P

WINDOW = 4096
SHARD = 128
ROW = 8
GROUP = 4
BACK = WINDOW // (ROW * SHARD)
SHARDS = 64
HALF = 72
NEG = -1e30


def transform_tables():
    length = 2 * SHARDS * SHARD
    k1 = np.arange(HALF)[:, None]
    live = (k1 <= SHARDS).astype(np.float64)
    a = np.arange(SHARDS)[None, :]
    angle = 2.0 * np.pi * ((k1 * a) % 128) / 128
    first = np.concatenate([live * np.cos(angle), -live * np.sin(angle)], 0)
    weight = live * np.where((k1 == 0) | (k1 == SHARDS), 1.0, 2.0) / length
    last = np.concatenate([weight * np.cos(angle), -weight * np.sin(angle)], 0).T
    b = np.arange(128)[None, :]
    turn = 2.0 * np.pi * (k1 * b) / length
    b2 = np.arange(128)[:, None]
    grid = 2.0 * np.pi * ((b2 * b) % 128) / 128
    cosine, sine = np.cos(grid), np.sin(grid)
    forward = np.block([[cosine, -sine], [sine, cosine]])
    backward = np.block([[cosine, sine], [-sine, cosine]])
    tables = [np.asarray(t, np.float32) for t in (np.cos(turn), np.sin(turn))]
    for table, axis in ((first, 1), (last, 1), (forward, 0), (backward, 0)):
        high = np.asarray(table, ml_dtypes.bfloat16)
        low = np.asarray(table - high.astype(np.float64), ml_dtypes.bfloat16)
        tables.append(np.concatenate([high, high, low], axis))
    return tables


def triple(x, axis):
    high = x.astype(jnp.bfloat16)
    low = (x - high.astype(jnp.float32)).astype(jnp.bfloat16)
    return jnp.concatenate([high, low, high], axis)


def table_times(table, x):
    return jnp.dot(table, triple(x, 0), preferred_element_type=jnp.float32)


def times_table(x, table):
    return jnp.dot(triple(x, 1), table, preferred_element_type=jnp.float32)


def to_spectra(signals, first, turn_cos, turn_sin, forward):
    stacked = table_times(first, jnp.concatenate(signals, 1))
    rows = []
    for n in range(len(signals)):
        re = stacked[:HALF, n * 128 : (n + 1) * 128]
        im = stacked[HALF:, n * 128 : (n + 1) * 128]
        rows.append(jnp.concatenate([re * turn_cos + im * turn_sin, im * turn_cos - re * turn_sin], 1))
    spectra = times_table(jnp.concatenate(rows, 0), forward)
    return [spectra[n * HALF : (n + 1) * HALF] for n in range(len(signals))]


def to_signals(spectra, last, turn_cos, turn_sin, backward):
    rows = times_table(jnp.concatenate(spectra, 0), backward)
    columns = []
    for n in range(len(spectra)):
        re = rows[n * HALF : (n + 1) * HALF, :128]
        im = rows[n * HALF : (n + 1) * HALF, 128:]
        columns.append(jnp.concatenate([re * turn_cos - im * turn_sin, re * turn_sin + im * turn_cos], 0))
    return table_times(last, jnp.concatenate(columns, 1))


def product(a, b):
    ar, ai, br, bi = a[:, :128], a[:, 128:], b[:, :128], b[:, 128:]
    return jnp.concatenate([ar * br - ai * bi, ar * bi + ai * br], 1)


def product_conj(a, b):
    ar, ai, br, bi = a[:, :128], a[:, 128:], b[:, :128], b[:, 128:]
    return jnp.concatenate([ar * br + ai * bi, ar * bi - ai * br], 1)


def repeat_kernel(key_ref, value_ref, out_ref, held, arrived, done):
    loads = []
    for m, ref in enumerate((key_ref, value_ref)):
        loads.append(pltpu.make_async_copy(ref, held.at[m], arrived.at[m]))
        loads[m].start()
    copies = []
    for m in (0, 1):
        loads[m].wait()
        for n in range(SHARDS // ROW):
            copies.append(pltpu.make_async_copy(held.at[m], out_ref.at[n, m], done.at[n, m]))
            copies[-1].start()
    for copy in copies:
        copy.wait()


def pack_kernel(parts_ref, input_ref, gate_ref, taps_ref, out_ref, wide_ref):
    target = parts_ref[0].astype(jnp.float32)
    for n in range(1, 8):
        target += parts_ref[n].astype(jnp.float32)
    arrays = (target.T, input_ref[...], gate_ref[...], taps_ref[...])
    for n, array in enumerate(arrays):
        array = array.astype(jnp.float32)
        wide_ref[:, 2 * n, :] = array[:SHARDS]
        wide_ref[:, 2 * n + 1, :] = array[SHARDS:]
    out_ref[...] = wide_ref[...].astype(jnp.bfloat16)


def student_kernel(skip_ref, in_ref, tc, ts, first, last, forward, backward, out_ref, wide_in, wide_out):
    wide_in[...] = in_ref[...].astype(jnp.float32)
    rank = lax.axis_index("seq")
    skip = [skip_ref[rank], skip_ref[rank + SHARDS]]
    target, signal, gate, taps = [[wide_in[:, 2 * n + c, :] for c in (0, 1)] for n in range(4)]
    turn = tc[...], ts[...]
    ahead = first[...], *turn, forward[...]
    behind = last[...], *turn, backward[...]
    spectra = to_spectra(signal + taps, *ahead)
    conv = to_signals([product(spectra[c], spectra[2 + c]) for c in (0, 1)], *behind)
    back = []
    for c in (0, 1):
        output = gate[c] * (conv[:, c * 128 : (c + 1) * 128] + skip[c] * signal[c])
        back.append(gate[c] * (output - target[c]))
    gradient = to_spectra(back, *ahead)
    mixed = [product_conj(spectra[2 + c], gradient[c]) for c in (0, 1)]
    mixed += [product_conj(spectra[c], gradient[c]) for c in (0, 1)]
    signals = to_signals(mixed, *behind)
    scale = (SHARDS * SHARD) ** -0.5
    for c in (0, 1):
        wide_out[:, c, :] = skip[c] * back[c] + signals[:, c * 128 : (c + 1) * 128]
        wide_out[:, 2 + c, :] = scale * signals[:, (2 + c) * 128 : (3 + c) * 128]
    out_ref[...] = wide_out[...].astype(jnp.bfloat16)


def unpack_kernel(in_ref, grad_ref, step_ref, wide_ref):
    wide_ref[...] = in_ref[...].astype(jnp.float32)
    for c in (0, 1):
        grad_ref[c * SHARDS : (c + 1) * SHARDS, :] = wide_ref[:, c, :]
        step_ref[c * SHARDS : (c + 1) * SHARDS, :] = wide_ref[:, 2 + c, :]


def attend_kernel(q_ref, own_ref, sibling_ref, out_ref):
    rank = lax.axis_index("seq")
    row, mine, core = rank // ROW, rank % ROW // 2, rank % 2
    scale = 128 ** -0.5
    order = [row] + [jnp.maximum(row - BACK + r, 0) for r in range(BACK)]
    sources = (own_ref, sibling_ref)
    keys = jnp.concatenate([ref[n, 0] for ref in sources for n in order], 0)
    ones = jnp.ones((10 * SHARD, 128), jnp.bfloat16)
    values = jnp.concatenate([jnp.concatenate([ref[n, 1] for ref in sources for n in order], 0), ones], 1)
    rows = lax.broadcasted_iota(jnp.int32, (SHARD, SHARD), 0)
    columns = lax.broadcasted_iota(jnp.int32, (SHARD, SHARD), 1)
    diagonal = rows == columns
    zero = jnp.zeros((SHARD, SHARD), jnp.float32)
    for theirs in range(GROUP):
        ahead = 2 * (mine - theirs) * SHARD
        stats = []
        for half in (0, 1):
            lag = half * (SHARD // 2) + rows // 2 - columns
            newest = [lag >= ahead, lag >= ahead + (1 - 2 * core) * SHARD]
            scores = lax.dot_general(
                q_ref[theirs, half * SHARD : (half + 1) * SHARD, :],
                keys,
                (((1,), (1,)), ((), ())),
                preferred_element_type=jnp.float32,
            )
            parts = [scores[:, n * SHARD : (n + 1) * SHARD] for n in range(10)]
            blocks = []
            for source in (0, 1):
                part = parts[5 * source : 5 * source + 5]
                blocks.append(jnp.where(newest[source], part[0], jnp.where(row >= BACK, part[1], NEG)))
                blocks += [jnp.where(row >= BACK - r, part[1 + r], NEG) for r in (1, 2, 3)]
            top = blocks[0]
            for block in blocks[1:]:
                top = jnp.maximum(top, block)
            top = jnp.maximum(jnp.max(top, axis=1, keepdims=True), 0.5 * NEG)
            weights = [jnp.exp((b - top) * scale) for b in blocks]
            spread = []
            for source in (0, 1):
                part = weights[4 * source : 4 * source + 4]
                spread += [jnp.where(newest[source], part[0], zero), jnp.where(newest[source], zero, part[0])]
                spread += part[1:]
            spread = jnp.concatenate([w.astype(jnp.bfloat16) for w in spread], 1)
            sums = jnp.dot(spread, values, preferred_element_type=jnp.float32)
            total = sums[:, 128:]
            safe = jnp.maximum(total, 1e-30)
            out_ref[theirs, half * SHARD : (half + 1) * SHARD, :] = (sums[:, :128] / safe).astype(jnp.bfloat16)
            log_sum = jnp.where(total > 0.0, top * scale + jnp.log(safe), NEG)
            log_sum = jnp.sum(jnp.where(diagonal, log_sum, 0.0), axis=0, keepdims=True)
            high = log_sum.astype(jnp.bfloat16).astype(jnp.float32)
            rest = log_sum - high
            middle = rest.astype(jnp.bfloat16).astype(jnp.float32)
            stats += [high, middle, rest - middle]
        stats.append(jnp.zeros((10, 128), jnp.float32))
        out_ref[theirs, 256:272, :] = jnp.concatenate(stats, 0).astype(jnp.bfloat16)


def merge_kernel(parts_ref, proj_ref, out_ref, merged_ref):
    shares = []
    for half in (0, 1):
        sums = []
        for p in range(GROUP):
            stats = parts_ref[p, 256:272, :].astype(jnp.float32)
            sums.append(jnp.sum(stats[3 * half : 3 * half + 3], axis=0, keepdims=True))
        sums = jnp.concatenate(sums, 0)
        share = jnp.exp(sums - jnp.max(sums, axis=0, keepdims=True))
        shares.append(share / jnp.sum(share, axis=0, keepdims=True))
    shares.append(jnp.zeros((128 - 2 * GROUP, 128), jnp.float32))
    shares = jnp.concatenate(shares, 0).T
    for half in (0, 1):
        merged = None
        for p in range(GROUP):
            part = parts_ref[p, half * SHARD : (half + 1) * SHARD, :].astype(jnp.float32)
            part = shares[:, half * GROUP + p : half * GROUP + p + 1] * part
            merged = part if merged is None else merged + part
        merged_ref[half * SHARD : (half + 1) * SHARD, :] = merged
    attended = jnp.concatenate([merged_ref[pl.ds(h, SHARD, stride=2), :] for h in (0, 1)], 1)
    target = jnp.dot(attended.astype(jnp.bfloat16), proj_ref[...], preferred_element_type=jnp.float32)
    for n in range(8):
        out_ref[n] = target[:, n * 128 : (n + 1) * 128].astype(jnp.bfloat16)


VMEM = pl.BlockSpec(memory_space=pltpu.VMEM)
SMEM = pl.BlockSpec(memory_space=pltpu.SMEM)


def near(x):
    return pltpu.with_memory_space_constraint(x, pltpu.VMEM)


def call_repeat(key, value):
    anywhere = pl.BlockSpec(memory_space=pl.ANY)
    return pl.pallas_call(
        repeat_kernel,
        out_shape=jax.ShapeDtypeStruct((SHARDS // ROW, 2, SHARD, 128), jnp.bfloat16),
        in_specs=[anywhere] * 2,
        out_specs=anywhere,
        scratch_shapes=[
            pltpu.VMEM((2, SHARD, 128), jnp.bfloat16),
            pltpu.SemaphoreType.DMA((2,)),
            pltpu.SemaphoreType.DMA((SHARDS // ROW, 2)),
        ],
    )(key, value)


def call_pack(parts, *inputs):
    return pl.pallas_call(
        pack_kernel,
        out_shape=pltpu.VMEM((SHARDS, 8, 128), jnp.bfloat16),
        in_specs=[VMEM] * 4,
        out_specs=VMEM,
        scratch_shapes=[pltpu.VMEM((SHARDS, 8, 128), jnp.float32)],
    )(near(parts), *[near(x) for x in inputs])


def call_student(skip, packed, tables):
    return pl.pallas_call(
        student_kernel,
        out_shape=pltpu.VMEM((SHARDS, 4, 128), jnp.bfloat16),
        in_specs=[SMEM] + [VMEM] * 7,
        out_specs=VMEM,
        scratch_shapes=[pltpu.VMEM((SHARDS, 8, 128), jnp.float32), pltpu.VMEM((SHARDS, 4, 128), jnp.float32)],
    )(skip, near(packed), *tables)


def call_unpack(out):
    return pl.pallas_call(
        unpack_kernel,
        out_shape=(jax.ShapeDtypeStruct((128, 128), jnp.float32),) * 2,
        in_specs=[VMEM],
        out_specs=(VMEM,) * 2,
        scratch_shapes=[pltpu.VMEM((SHARDS, 4, 128), jnp.float32)],
    )(near(out))


def call_attend(queries, own, sibling):
    return pl.pallas_call(
        attend_kernel,
        out_shape=pltpu.VMEM((GROUP, 272, 128), jnp.bfloat16),
        in_specs=[VMEM] * 3,
        out_specs=VMEM,
    )(near(queries), near(own), near(sibling))


def call_merge(parts, proj):
    return pl.pallas_call(
        merge_kernel,
        out_shape=pltpu.VMEM((8, 128, 128), jnp.bfloat16),
        in_specs=[VMEM] * 2,
        out_specs=VMEM,
        scratch_shapes=[pltpu.VMEM((2 * SHARD, 128), jnp.float32)],
    )(near(parts), near(proj))


def body(
    query_heads,
    key_heads,
    value_heads,
    distill_proj,
    conv_input,
    gate_input,
    filter_taps,
    skip_gain,
):
    tables = [near(jnp.asarray(t)) for t in transform_tables()]
    lines = range(SHARDS // ROW)
    groups = [[y * ROW + 2 * x + core for x in range(GROUP)] for y in lines for core in (0, 1)]
    columns = [[y * ROW + p for y in lines] for p in range(ROW)]
    pairs = call_repeat(key_heads[:, 0], value_heads[:, 0])
    own = lax.all_to_all(pairs, "seq", 0, 0, axis_index_groups=columns)
    queries = lax.all_gather(query_heads.reshape(2 * SHARD, 128), "seq", axis_index_groups=groups)
    own, queries = lax.optimization_barrier((own, queries))
    sibling = lax.ppermute(own, "seq", [(i, i ^ 1) for i in range(SHARDS)])
    parts = call_attend(queries, own, sibling)
    parts = lax.all_to_all(parts, "seq", 0, 0, axis_index_groups=groups)
    target = call_merge(parts, distill_proj.reshape(256, 1024))
    target = lax.all_to_all(target, ("role", "head"), 0, 0)
    packed = call_pack(target, conv_input, gate_input, filter_taps)
    packed = lax.all_to_all(packed, "seq", 0, 0)
    out = call_student(skip_gain, packed, tables)
    out = lax.all_to_all(out, "seq", 0, 0)
    return call_unpack(out)


def solution(mesh):
    in_specs = (
        P("seq", ("role", "head"), None),
        P("seq", ("role", "head"), None),
        P("seq", ("role", "head"), None),
        P(("role", "head"), None, None),
        P(("role", "head"), "seq"),
        P(("role", "head"), "seq"),
        P(("role", "head"), "seq"),
        P(("role", "head")),
    )
    out_specs = (P(("role", "head"), "seq"), P(("role", "head"), "seq"))
    return jax.shard_map(body, mesh=mesh, in_specs=in_specs, out_specs=out_specs, check_vma=False)
```

```python
import jax
import jax.numpy as jnp
import ml_dtypes
import numpy as np
from jax import lax
from jax.experimental import pallas as pl
from jax.experimental.pallas import tpu as pltpu
from jax.sharding import PartitionSpec as P

WINDOW = 4096
SHARD = 128
ROW = 8
GROUP = 4
BACK = WINDOW // (ROW * SHARD)
SHARDS = 64
HALF = 72
NEG = -1e30
LOG2E = 1.4426950408889634


def transform_tables():
    length = 2 * SHARDS * SHARD
    k1 = np.arange(HALF)[:, None]
    live = (k1 <= SHARDS).astype(np.float64)
    a = np.arange(SHARDS)[None, :]
    angle = 2.0 * np.pi * ((k1 * a) % 128) / 128
    first = np.concatenate([live * np.cos(angle), -live * np.sin(angle)], 0)
    weight = live * np.where((k1 == 0) | (k1 == SHARDS), 1.0, 2.0) / length
    last = np.concatenate([weight * np.cos(angle), -weight * np.sin(angle)], 0).T
    b = np.arange(128)[None, :]
    turn = 2.0 * np.pi * (k1 * b) / length
    b2 = np.arange(128)[:, None]
    grid = 2.0 * np.pi * ((b2 * b) % 128) / 128
    cosine, sine = np.cos(grid), np.sin(grid)
    forward = np.block([[cosine, -sine], [sine, cosine]])
    backward = np.block([[cosine, sine], [-sine, cosine]])
    tables = [np.asarray(t, np.float32) for t in (np.cos(turn), np.sin(turn))]
    for table, axis in ((first, 1), (last, 1), (forward, 0), (backward, 0)):
        high = np.asarray(table, ml_dtypes.bfloat16)
        low = np.asarray(table - high.astype(np.float64), ml_dtypes.bfloat16)
        tables.append(np.concatenate([high, high, low], axis))
    return tables


def triple(x, axis):
    high = x.astype(jnp.bfloat16)
    low = (x - high.astype(jnp.float32)).astype(jnp.bfloat16)
    return jnp.concatenate([high, low, high], axis)


def table_times(table, x):
    return jnp.dot(table, triple(x, 0), preferred_element_type=jnp.float32)


def times_table(x, table):
    return jnp.dot(triple(x, 1), table, preferred_element_type=jnp.float32)


def to_spectra(signals, first, turn_cos, turn_sin, forward):
    stacked = table_times(first, jnp.concatenate(signals, 1))
    rows = []
    for n in range(len(signals)):
        re = stacked[:HALF, n * 128 : (n + 1) * 128]
        im = stacked[HALF:, n * 128 : (n + 1) * 128]
        rows.append(jnp.concatenate([re * turn_cos + im * turn_sin, im * turn_cos - re * turn_sin], 1))
    spectra = times_table(jnp.concatenate(rows, 0), forward)
    return [spectra[n * HALF : (n + 1) * HALF] for n in range(len(signals))]


def to_signals(spectra, last, turn_cos, turn_sin, backward):
    rows = times_table(jnp.concatenate(spectra, 0), backward)
    columns = []
    for n in range(len(spectra)):
        re = rows[n * HALF : (n + 1) * HALF, :128]
        im = rows[n * HALF : (n + 1) * HALF, 128:]
        columns.append(jnp.concatenate([re * turn_cos - im * turn_sin, re * turn_sin + im * turn_cos], 0))
    return table_times(last, jnp.concatenate(columns, 1))


def product(a, b):
    ar, ai, br, bi = a[:, :128], a[:, 128:], b[:, :128], b[:, 128:]
    return jnp.concatenate([ar * br - ai * bi, ar * bi + ai * br], 1)


def product_conj(a, b):
    ar, ai, br, bi = a[:, :128], a[:, 128:], b[:, :128], b[:, 128:]
    return jnp.concatenate([ar * br + ai * bi, ar * bi - ai * br], 1)


def repeat_kernel(key_ref, value_ref, out_ref, held, arrived, done):
    loads = []
    for m, ref in enumerate((key_ref, value_ref)):
        loads.append(pltpu.make_async_copy(ref, held.at[m], arrived.at[m]))
        loads[m].start()
    copies = []
    for m in (0, 1):
        loads[m].wait()
        for n in range(SHARDS // ROW):
            copies.append(pltpu.make_async_copy(held.at[m], out_ref.at[n, m], done.at[n, m]))
            copies[-1].start()
    for copy in copies:
        copy.wait()


def pack_kernel(parts_ref, input_ref, gate_ref, taps_ref, out_ref, wide_ref):
    target = parts_ref[0].astype(jnp.float32)
    for n in range(1, 8):
        target += parts_ref[n].astype(jnp.float32)
    arrays = (target.T, input_ref[...], gate_ref[...], taps_ref[...])
    for n, array in enumerate(arrays):
        array = array.astype(jnp.float32)
        wide_ref[:, 2 * n, :] = array[:SHARDS]
        wide_ref[:, 2 * n + 1, :] = array[SHARDS:]
    out_ref[...] = wide_ref[...].astype(jnp.bfloat16)


def student_kernel(skip_ref, in_ref, tc, ts, first, last, forward, backward, out_ref, wide_in, wide_out):
    wide_in[...] = in_ref[...].astype(jnp.float32)
    rank = lax.axis_index("seq")
    skip = [skip_ref[rank], skip_ref[rank + SHARDS]]
    target, signal, gate, taps = [[wide_in[:, 2 * n + c, :] for c in (0, 1)] for n in range(4)]
    turn = tc[...], ts[...]
    ahead = first[...], *turn, forward[...]
    behind = last[...], *turn, backward[...]
    spectra = to_spectra(signal + taps, *ahead)
    conv = to_signals([product(spectra[c], spectra[2 + c]) for c in (0, 1)], *behind)
    back = []
    for c in (0, 1):
        output = gate[c] * (conv[:, c * 128 : (c + 1) * 128] + skip[c] * signal[c])
        back.append(gate[c] * (output - target[c]))
    gradient = to_spectra(back, *ahead)
    mixed = [product_conj(spectra[2 + c], gradient[c]) for c in (0, 1)]
    mixed += [product_conj(spectra[c], gradient[c]) for c in (0, 1)]
    signals = to_signals(mixed, *behind)
    scale = (SHARDS * SHARD) ** -0.5
    for c in (0, 1):
        wide_out[:, c, :] = skip[c] * back[c] + signals[:, c * 128 : (c + 1) * 128]
        wide_out[:, 2 + c, :] = scale * signals[:, (2 + c) * 128 : (3 + c) * 128]
    out_ref[...] = wide_out[...].astype(jnp.bfloat16)


def unpack_kernel(in_ref, grad_ref, step_ref, wide_ref):
    wide_ref[...] = in_ref[...].astype(jnp.float32)
    for c in (0, 1):
        grad_ref[c * SHARDS : (c + 1) * SHARDS, :] = wide_ref[:, c, :]
        step_ref[c * SHARDS : (c + 1) * SHARDS, :] = wide_ref[:, 2 + c, :]


def attend_kernel(q_ref, own_ref, sibling_ref, out_ref):
    rank = lax.axis_index("seq")
    row, mine, core = rank // ROW, rank % ROW // 2, rank % 2
    scale = 128 ** -0.5
    oldest = jnp.maximum(row - BACK, 0)
    full = [(ref, jnp.maximum(row - BACK + r, 0)) for ref in (own_ref, sibling_ref) for r in (1, 2, 3)]
    full_live = [row >= BACK - r for r in (1, 2, 3)] * 2
    full_keys = jnp.concatenate([ref[n, 0] for ref, n in full], 0)
    full_values = jnp.concatenate([ref[n, 1] for ref, n in full], 0)
    rows = lax.broadcasted_iota(jnp.int32, (SHARD, SHARD), 0)
    columns = lax.broadcasted_iota(jnp.int32, (SHARD, SHARD), 1)
    diagonal = rows == columns
    zero = jnp.zeros((SHARD, SHARD), jnp.float32)
    for step in range(GROUP):
        theirs = (mine + step) % GROUP
        newer = core == 1 if step == 0 else theirs > mine
        edge = jnp.where(newer, row, oldest)
        edges = [(sibling_ref, edge)]
        edges = ([(own_ref, row), (own_ref, oldest)] if step == 0 else [(own_ref, edge)]) + edges
        live = jnp.logical_or(newer, row >= BACK)
        keys = jnp.concatenate([ref[n, 0] for ref, n in edges] + [full_keys], 0)
        values = jnp.concatenate([ref[n, 1] for ref, n in edges] + [full_values], 0)
        values = jnp.concatenate([values, jnp.ones(values.shape, jnp.bfloat16)], 1)
        scores = lax.dot_general(
            q_ref[theirs], keys, (((1,), (1,)), ((), ())), preferred_element_type=jnp.float32
        )
        spreads, tops = [], []
        for half in (0, 1):
            parts = scores[half * SHARD : (half + 1) * SHARD]
            parts = [parts[:, n * SHARD : (n + 1) * SHARD] for n in range(len(edges) + 6)]
            if step == 0:
                newest = half * (SHARD // 2) + rows // 2 >= columns
                blocks = [jnp.where(newest, parts[0], jnp.where(row >= BACK, parts[1], NEG))]
            else:
                blocks = [jnp.where(live, parts[0], NEG)]
            blocks.append(jnp.where(live, parts[len(edges) - 1], NEG))
            blocks += [jnp.where(ok, part, NEG) for ok, part in zip(full_live, parts[len(edges) :])]
            top = blocks[0]
            for block in blocks[1:]:
                top = jnp.maximum(top, block)
            top = jnp.maximum(jnp.max(top, axis=1, keepdims=True), 0.5 * NEG)
            tops.append(top)
            shift = top * (scale * LOG2E)
            weights = [jnp.exp2(b * (scale * LOG2E) - shift) for b in blocks]
            if step == 0:
                weights = [jnp.where(newest, weights[0], zero), jnp.where(newest, zero, weights[0])] + weights[1:]
            spreads.append(jnp.concatenate([w.astype(jnp.bfloat16) for w in weights], 1))
        sums = jnp.dot(jnp.concatenate(spreads, 0), values, preferred_element_type=jnp.float32)
        total = sums[:, 128:]
        safe = jnp.maximum(total, 1e-30)
        out_ref[theirs, :256, :] = (sums[:, :128] / safe).astype(jnp.bfloat16)
        log_sums = jnp.where(total > 0.0, jnp.concatenate(tops, 0) * scale + jnp.log(safe), NEG)
        stats = []
        for half in (0, 1):
            log_sum = log_sums[half * SHARD : (half + 1) * SHARD]
            log_sum = jnp.sum(jnp.where(diagonal, log_sum, 0.0), axis=0, keepdims=True)
            high = log_sum.astype(jnp.bfloat16).astype(jnp.float32)
            rest = log_sum - high
            middle = rest.astype(jnp.bfloat16).astype(jnp.float32)
            stats += [high, middle, rest - middle]
        stats.append(jnp.zeros((10, 128), jnp.float32))
        out_ref[theirs, 256:272, :] = jnp.concatenate(stats, 0).astype(jnp.bfloat16)


def merge_kernel(parts_ref, proj_ref, out_ref, merged_ref):
    shares = []
    for half in (0, 1):
        sums = []
        for p in range(GROUP):
            stats = parts_ref[p, 256:272, :].astype(jnp.float32)
            sums.append(jnp.sum(stats[3 * half : 3 * half + 3], axis=0, keepdims=True))
        sums = jnp.concatenate(sums, 0)
        share = jnp.exp(sums - jnp.max(sums, axis=0, keepdims=True))
        shares.append(share / jnp.sum(share, axis=0, keepdims=True))
    shares.append(jnp.zeros((128 - 2 * GROUP, 128), jnp.float32))
    shares = jnp.concatenate(shares, 0).T
    for half in (0, 1):
        merged = None
        for p in range(GROUP):
            part = parts_ref[p, half * SHARD : (half + 1) * SHARD, :].astype(jnp.float32)
            part = shares[:, half * GROUP + p : half * GROUP + p + 1] * part
            merged = part if merged is None else merged + part
        merged_ref[half * SHARD : (half + 1) * SHARD, :] = merged
    attended = jnp.concatenate([merged_ref[pl.ds(h, SHARD, stride=2), :] for h in (0, 1)], 1)
    target = jnp.dot(attended.astype(jnp.bfloat16), proj_ref[...], preferred_element_type=jnp.float32)
    for n in range(8):
        out_ref[n] = target[:, n * 128 : (n + 1) * 128].astype(jnp.bfloat16)


VMEM = pl.BlockSpec(memory_space=pltpu.VMEM)
SMEM = pl.BlockSpec(memory_space=pltpu.SMEM)


def near(x):
    return pltpu.with_memory_space_constraint(x, pltpu.VMEM)


def call_repeat(key, value):
    anywhere = pl.BlockSpec(memory_space=pl.ANY)
    return pl.pallas_call(
        repeat_kernel,
        out_shape=jax.ShapeDtypeStruct((SHARDS // ROW, 2, SHARD, 128), jnp.bfloat16),
        in_specs=[anywhere] * 2,
        out_specs=anywhere,
        scratch_shapes=[
            pltpu.VMEM((2, SHARD, 128), jnp.bfloat16),
            pltpu.SemaphoreType.DMA((2,)),
            pltpu.SemaphoreType.DMA((SHARDS // ROW, 2)),
        ],
    )(key, value)


def call_pack(parts, *inputs):
    return pl.pallas_call(
        pack_kernel,
        out_shape=pltpu.VMEM((SHARDS, 8, 128), jnp.bfloat16),
        in_specs=[VMEM] * 4,
        out_specs=VMEM,
        scratch_shapes=[pltpu.VMEM((SHARDS, 8, 128), jnp.float32)],
    )(near(parts), *[near(x) for x in inputs])


def call_student(skip, packed, tables):
    return pl.pallas_call(
        student_kernel,
        out_shape=pltpu.VMEM((SHARDS, 4, 128), jnp.bfloat16),
        in_specs=[SMEM] + [VMEM] * 7,
        out_specs=VMEM,
        scratch_shapes=[pltpu.VMEM((SHARDS, 8, 128), jnp.float32), pltpu.VMEM((SHARDS, 4, 128), jnp.float32)],
    )(skip, near(packed), *tables)


def call_unpack(out):
    return pl.pallas_call(
        unpack_kernel,
        out_shape=(jax.ShapeDtypeStruct((128, 128), jnp.float32),) * 2,
        in_specs=[VMEM],
        out_specs=(VMEM,) * 2,
        scratch_shapes=[pltpu.VMEM((SHARDS, 4, 128), jnp.float32)],
    )(near(out))


def call_attend(queries, own, sibling):
    return pl.pallas_call(
        attend_kernel,
        out_shape=pltpu.VMEM((GROUP, 272, 128), jnp.bfloat16),
        in_specs=[VMEM] * 3,
        out_specs=VMEM,
    )(near(queries), near(own), near(sibling))


def call_merge(parts, proj):
    return pl.pallas_call(
        merge_kernel,
        out_shape=pltpu.VMEM((8, 128, 128), jnp.bfloat16),
        in_specs=[VMEM] * 2,
        out_specs=VMEM,
        scratch_shapes=[pltpu.VMEM((2 * SHARD, 128), jnp.float32)],
    )(near(parts), near(proj))


def body(
    query_heads,
    key_heads,
    value_heads,
    distill_proj,
    conv_input,
    gate_input,
    filter_taps,
    skip_gain,
):
    tables = [near(jnp.asarray(t)) for t in transform_tables()]
    lines = range(SHARDS // ROW)
    groups = [[y * ROW + 2 * x + core for x in range(GROUP)] for y in lines for core in (0, 1)]
    columns = [[y * ROW + p for y in lines] for p in range(ROW)]
    pairs = call_repeat(key_heads[:, 0], value_heads[:, 0])
    own = lax.all_to_all(pairs, "seq", 0, 0, axis_index_groups=columns)
    queries = lax.all_gather(query_heads.reshape(2 * SHARD, 128), "seq", axis_index_groups=groups)
    own, queries = lax.optimization_barrier((own, queries))
    sibling = lax.ppermute(own, "seq", [(i, i ^ 1) for i in range(SHARDS)])
    parts = call_attend(queries, own, sibling)
    parts = lax.all_to_all(parts, "seq", 0, 0, axis_index_groups=groups)
    target = call_merge(parts, distill_proj.reshape(256, 1024))
    target = lax.all_to_all(target, ("role", "head"), 0, 0)
    packed = call_pack(target, conv_input, gate_input, filter_taps)
    packed = lax.all_to_all(packed, "seq", 0, 0)
    out = call_student(skip_gain, packed, tables)
    out = lax.all_to_all(out, "seq", 0, 0)
    return call_unpack(out)


def solution(mesh):
    in_specs = (
        P("seq", ("role", "head"), None),
        P("seq", ("role", "head"), None),
        P("seq", ("role", "head"), None),
        P(("role", "head"), None, None),
        P(("role", "head"), "seq"),
        P(("role", "head"), "seq"),
        P(("role", "head"), "seq"),
        P(("role", "head")),
    )
    out_specs = (P(("role", "head"), "seq"), P(("role", "head"), "seq"))
    return jax.shard_map(body, mesh=mesh, in_specs=in_specs, out_specs=out_specs, check_vma=False)
```

```python
import jax
import jax.numpy as jnp
import ml_dtypes
import numpy as np
from jax import lax
from jax.experimental import pallas as pl
from jax.experimental.pallas import tpu as pltpu
from jax.sharding import PartitionSpec as P

WINDOW = 4096
SHARD = 128
ROW = 8
BACK = WINDOW // (ROW * SHARD)
SHARDS = 64
HALF = 72
NEG = -1e30
LOG2E = 1.4426950408889634


def transform_tables():
    length = 2 * SHARDS * SHARD
    k1 = np.arange(HALF)[:, None]
    live = (k1 <= SHARDS).astype(np.float64)
    a = np.arange(SHARDS)[None, :]
    angle = 2.0 * np.pi * ((k1 * a) % 128) / 128
    first = np.concatenate([live * np.cos(angle), -live * np.sin(angle)], 0)
    weight = live * np.where((k1 == 0) | (k1 == SHARDS), 1.0, 2.0) / length
    last = np.concatenate([weight * np.cos(angle), -weight * np.sin(angle)], 0).T
    b = np.arange(128)[None, :]
    turn = 2.0 * np.pi * (k1 * b) / length
    b2 = np.arange(128)[:, None]
    grid = 2.0 * np.pi * ((b2 * b) % 128) / 128
    cosine, sine = np.cos(grid), np.sin(grid)
    forward = np.block([[cosine, -sine], [sine, cosine]])
    backward = np.block([[cosine, sine], [-sine, cosine]])
    tables = [np.asarray(t, np.float32) for t in (np.cos(turn), np.sin(turn))]
    for table, axis in ((first, 1), (last, 1), (forward, 0), (backward, 0)):
        high = np.asarray(table, ml_dtypes.bfloat16)
        low = np.asarray(table - high.astype(np.float64), ml_dtypes.bfloat16)
        tables.append(np.concatenate([high, high, low], axis))
    return tables


def triple(x, axis):
    high = x.astype(jnp.bfloat16)
    low = (x - high.astype(jnp.float32)).astype(jnp.bfloat16)
    return jnp.concatenate([high, low, high], axis)


def table_times(table, x):
    return jnp.dot(table, triple(x, 0), preferred_element_type=jnp.float32)


def times_table(x, table):
    return jnp.dot(triple(x, 1), table, preferred_element_type=jnp.float32)


def to_spectra(signals, first, turn_cos, turn_sin, forward):
    stacked = table_times(first, jnp.concatenate(signals, 1))
    rows = []
    for n in range(len(signals)):
        re = stacked[:HALF, n * 128 : (n + 1) * 128]
        im = stacked[HALF:, n * 128 : (n + 1) * 128]
        rows.append(jnp.concatenate([re * turn_cos + im * turn_sin, im * turn_cos - re * turn_sin], 1))
    spectra = times_table(jnp.concatenate(rows, 0), forward)
    return [spectra[n * HALF : (n + 1) * HALF] for n in range(len(signals))]


def to_signals(spectra, last, turn_cos, turn_sin, backward):
    rows = times_table(jnp.concatenate(spectra, 0), backward)
    columns = []
    for n in range(len(spectra)):
        re = rows[n * HALF : (n + 1) * HALF, :128]
        im = rows[n * HALF : (n + 1) * HALF, 128:]
        columns.append(jnp.concatenate([re * turn_cos - im * turn_sin, re * turn_sin + im * turn_cos], 0))
    return table_times(last, jnp.concatenate(columns, 1))


def product(a, b):
    ar, ai, br, bi = a[:, :128], a[:, 128:], b[:, :128], b[:, 128:]
    return jnp.concatenate([ar * br - ai * bi, ar * bi + ai * br], 1)


def product_conj(a, b):
    ar, ai, br, bi = a[:, :128], a[:, 128:], b[:, :128], b[:, 128:]
    return jnp.concatenate([ar * br + ai * bi, ar * bi - ai * br], 1)


def repeat_kernel(key_ref, value_ref, out_ref, held, arrived, done):
    loads = []
    for m, ref in enumerate((key_ref, value_ref)):
        loads.append(pltpu.make_async_copy(ref, held.at[m], arrived.at[m]))
        loads[m].start()
    copies = []
    for m in (0, 1):
        loads[m].wait()
        for n in range(SHARDS // ROW):
            copies.append(pltpu.make_async_copy(held.at[m], out_ref.at[n, m], done.at[n, m]))
            copies[-1].start()
    for copy in copies:
        copy.wait()


def pack_kernel(parts_ref, input_ref, gate_ref, taps_ref, out_ref, wide_ref):
    target = parts_ref[0].astype(jnp.float32)
    for n in range(1, 8):
        target += parts_ref[n].astype(jnp.float32)
    arrays = (target.T, input_ref[...], gate_ref[...], taps_ref[...])
    for n, array in enumerate(arrays):
        array = array.astype(jnp.float32)
        wide_ref[:, 2 * n, :] = array[:SHARDS]
        wide_ref[:, 2 * n + 1, :] = array[SHARDS:]
    out_ref[...] = wide_ref[...].astype(jnp.bfloat16)


def student_kernel(skip_ref, in_ref, tc, ts, first, last, forward, backward, out_ref, wide_in, wide_out):
    wide_in[...] = in_ref[...].astype(jnp.float32)
    rank = lax.axis_index("seq")
    skip = [skip_ref[rank], skip_ref[rank + SHARDS]]
    target, signal, gate, taps = [[wide_in[:, 2 * n + c, :] for c in (0, 1)] for n in range(4)]
    turn = tc[...], ts[...]
    ahead = first[...], *turn, forward[...]
    behind = last[...], *turn, backward[...]
    spectra = to_spectra(signal + taps, *ahead)
    conv = to_signals([product(spectra[c], spectra[2 + c]) for c in (0, 1)], *behind)
    back = []
    for c in (0, 1):
        output = gate[c] * (conv[:, c * 128 : (c + 1) * 128] + skip[c] * signal[c])
        back.append(gate[c] * (output - target[c]))
    gradient = to_spectra(back, *ahead)
    mixed = [product_conj(spectra[2 + c], gradient[c]) for c in (0, 1)]
    mixed += [product_conj(spectra[c], gradient[c]) for c in (0, 1)]
    signals = to_signals(mixed, *behind)
    scale = (SHARDS * SHARD) ** -0.5
    for c in (0, 1):
        wide_out[:, c, :] = skip[c] * back[c] + signals[:, c * 128 : (c + 1) * 128]
        wide_out[:, 2 + c, :] = scale * signals[:, (2 + c) * 128 : (3 + c) * 128]
    out_ref[...] = wide_out[...].astype(jnp.bfloat16)


def unpack_kernel(in_ref, grad_ref, step_ref, wide_ref):
    wide_ref[...] = in_ref[...].astype(jnp.float32)
    for c in (0, 1):
        grad_ref[c * SHARDS : (c + 1) * SHARDS, :] = wide_ref[:, c, :]
        step_ref[c * SHARDS : (c + 1) * SHARDS, :] = wide_ref[:, 2 + c, :]


def attend_kernel(q_ref, kv_ref, out_ref):
    rank = lax.axis_index("seq")
    row, mine = rank // ROW, rank % ROW
    scale = 128 ** -0.5
    oldest = jnp.maximum(row - BACK, 0)
    full = [jnp.maximum(row - BACK + r, 0) for r in (1, 2, 3)]
    full_live = [row >= BACK - r for r in (1, 2, 3)]
    full_keys = jnp.concatenate([kv_ref[n, 0] for n in full], 0)
    full_values = jnp.concatenate([kv_ref[n, 1] for n in full], 0)
    rows = lax.broadcasted_iota(jnp.int32, (SHARD, SHARD), 0)
    columns = lax.broadcasted_iota(jnp.int32, (SHARD, SHARD), 1)
    diagonal = rows == columns
    zero = jnp.zeros((SHARD, SHARD), jnp.float32)
    for step in range(ROW):
        theirs = (mine + step) % ROW
        newer = theirs > mine
        edges = [row, oldest] if step == 0 else [jnp.where(newer, row, oldest)]
        live = jnp.logical_or(newer, row >= BACK)
        keys = jnp.concatenate([kv_ref[n, 0] for n in edges] + [full_keys], 0)
        values = jnp.concatenate([kv_ref[n, 1] for n in edges] + [full_values], 0)
        values = jnp.concatenate([values, jnp.ones(values.shape, jnp.bfloat16)], 1)
        scores = lax.dot_general(
            q_ref[theirs], keys, (((1,), (1,)), ((), ())), preferred_element_type=jnp.float32
        )
        spreads, tops = [], []
        for half in (0, 1):
            parts = scores[half * SHARD : (half + 1) * SHARD]
            parts = [parts[:, n * SHARD : (n + 1) * SHARD] for n in range(len(edges) + 3)]
            if step == 0:
                newest = half * (SHARD // 2) + rows // 2 >= columns
                blocks = [jnp.where(newest, parts[0], jnp.where(row >= BACK, parts[1], NEG))]
            else:
                blocks = [jnp.where(live, parts[0], NEG)]
            blocks += [jnp.where(ok, part, NEG) for ok, part in zip(full_live, parts[len(edges) :])]
            top = blocks[0]
            for block in blocks[1:]:
                top = jnp.maximum(top, block)
            top = jnp.maximum(jnp.max(top, axis=1, keepdims=True), 0.5 * NEG)
            tops.append(top)
            shift = top * (scale * LOG2E)
            weights = [jnp.exp2(b * (scale * LOG2E) - shift) for b in blocks]
            if step == 0:
                weights = [jnp.where(newest, weights[0], zero), jnp.where(newest, zero, weights[0])] + weights[1:]
            spreads.append(jnp.concatenate([w.astype(jnp.bfloat16) for w in weights], 1))
        sums = jnp.dot(jnp.concatenate(spreads, 0), values, preferred_element_type=jnp.float32)
        total = sums[:, 128:]
        safe = jnp.maximum(total, 1e-30)
        out_ref[theirs, :256, :] = (sums[:, :128] / safe).astype(jnp.bfloat16)
        log_sums = jnp.where(total > 0.0, jnp.concatenate(tops, 0) * scale + jnp.log(safe), NEG)
        stats = []
        for half in (0, 1):
            log_sum = log_sums[half * SHARD : (half + 1) * SHARD]
            log_sum = jnp.sum(jnp.where(diagonal, log_sum, 0.0), axis=0, keepdims=True)
            high = log_sum.astype(jnp.bfloat16).astype(jnp.float32)
            rest = log_sum - high
            middle = rest.astype(jnp.bfloat16).astype(jnp.float32)
            stats += [high, middle, rest - middle]
        stats.append(jnp.zeros((10, 128), jnp.float32))
        out_ref[theirs, 256:272, :] = jnp.concatenate(stats, 0).astype(jnp.bfloat16)


def merge_kernel(parts_ref, proj_ref, out_ref, merged_ref):
    shares = []
    for half in (0, 1):
        sums = []
        for p in range(ROW):
            stats = parts_ref[p, 256:272, :].astype(jnp.float32)
            sums.append(jnp.sum(stats[3 * half : 3 * half + 3], axis=0, keepdims=True))
        sums = jnp.concatenate(sums, 0)
        share = jnp.exp(sums - jnp.max(sums, axis=0, keepdims=True))
        shares.append(share / jnp.sum(share, axis=0, keepdims=True))
    shares.append(jnp.zeros((128 - 2 * ROW, 128), jnp.float32))
    shares = jnp.concatenate(shares, 0).T
    for half in (0, 1):
        merged = None
        for p in range(ROW):
            part = parts_ref[p, half * SHARD : (half + 1) * SHARD, :].astype(jnp.float32)
            part = shares[:, half * ROW + p : half * ROW + p + 1] * part
            merged = part if merged is None else merged + part
        merged_ref[half * SHARD : (half + 1) * SHARD, :] = merged
    attended = jnp.concatenate([merged_ref[pl.ds(h, SHARD, stride=2), :] for h in (0, 1)], 1)
    target = jnp.dot(attended.astype(jnp.bfloat16), proj_ref[...], preferred_element_type=jnp.float32)
    for n in range(8):
        out_ref[n] = target[:, n * 128 : (n + 1) * 128].astype(jnp.bfloat16)


VMEM = pl.BlockSpec(memory_space=pltpu.VMEM)
SMEM = pl.BlockSpec(memory_space=pltpu.SMEM)


def near(x):
    return pltpu.with_memory_space_constraint(x, pltpu.VMEM)


def call_repeat(key, value):
    anywhere = pl.BlockSpec(memory_space=pl.ANY)
    return pl.pallas_call(
        repeat_kernel,
        out_shape=jax.ShapeDtypeStruct((SHARDS // ROW, 2, SHARD, 128), jnp.bfloat16),
        in_specs=[anywhere] * 2,
        out_specs=anywhere,
        scratch_shapes=[
            pltpu.VMEM((2, SHARD, 128), jnp.bfloat16),
            pltpu.SemaphoreType.DMA((2,)),
            pltpu.SemaphoreType.DMA((SHARDS // ROW, 2)),
        ],
    )(key, value)


def call_pack(parts, *inputs):
    return pl.pallas_call(
        pack_kernel,
        out_shape=pltpu.VMEM((SHARDS, 8, 128), jnp.bfloat16),
        in_specs=[VMEM] * 4,
        out_specs=VMEM,
        scratch_shapes=[pltpu.VMEM((SHARDS, 8, 128), jnp.float32)],
    )(near(parts), *[near(x) for x in inputs])


def call_student(skip, packed, tables):
    return pl.pallas_call(
        student_kernel,
        out_shape=pltpu.VMEM((SHARDS, 4, 128), jnp.bfloat16),
        in_specs=[SMEM] + [VMEM] * 7,
        out_specs=VMEM,
        scratch_shapes=[pltpu.VMEM((SHARDS, 8, 128), jnp.float32), pltpu.VMEM((SHARDS, 4, 128), jnp.float32)],
    )(skip, near(packed), *tables)


def call_unpack(out):
    return pl.pallas_call(
        unpack_kernel,
        out_shape=(jax.ShapeDtypeStruct((128, 128), jnp.float32),) * 2,
        in_specs=[VMEM],
        out_specs=(VMEM,) * 2,
        scratch_shapes=[pltpu.VMEM((SHARDS, 4, 128), jnp.float32)],
    )(near(out))


def call_attend(queries, pairs):
    return pl.pallas_call(
        attend_kernel,
        out_shape=pltpu.VMEM((ROW, 272, 128), jnp.bfloat16),
        in_specs=[VMEM] * 2,
        out_specs=VMEM,
    )(near(queries), near(pairs))


def call_merge(parts, proj):
    return pl.pallas_call(
        merge_kernel,
        out_shape=pltpu.VMEM((8, 128, 128), jnp.bfloat16),
        in_specs=[VMEM] * 2,
        out_specs=VMEM,
        scratch_shapes=[pltpu.VMEM((2 * SHARD, 128), jnp.float32)],
    )(near(parts), near(proj))


def body(
    query_heads,
    key_heads,
    value_heads,
    distill_proj,
    conv_input,
    gate_input,
    filter_taps,
    skip_gain,
):
    tables = [near(jnp.asarray(t)) for t in transform_tables()]
    lines = range(SHARDS // ROW)
    rows = [[y * ROW + p for p in range(ROW)] for y in lines]
    columns = [[y * ROW + p for y in lines] for p in range(ROW)]
    pairs = call_repeat(key_heads[:, 0], value_heads[:, 0])
    pairs = lax.all_to_all(pairs, "seq", 0, 0, axis_index_groups=columns)
    queries = lax.all_gather(query_heads.reshape(2 * SHARD, 128), "seq", axis_index_groups=rows)
    parts = call_attend(queries, pairs)
    parts = lax.all_to_all(parts, "seq", 0, 0, axis_index_groups=rows)
    target = call_merge(parts, distill_proj.reshape(256, 1024))
    target = lax.all_to_all(target, ("role", "head"), 0, 0)
    packed = call_pack(target, conv_input, gate_input, filter_taps)
    packed = lax.all_to_all(packed, "seq", 0, 0)
    out = call_student(skip_gain, packed, tables)
    out = lax.all_to_all(out, "seq", 0, 0)
    return call_unpack(out)


def solution(mesh):
    in_specs = (
        P("seq", ("role", "head"), None),
        P("seq", ("role", "head"), None),
        P("seq", ("role", "head"), None),
        P(("role", "head"), None, None),
        P(("role", "head"), "seq"),
        P(("role", "head"), "seq"),
        P(("role", "head"), "seq"),
        P(("role", "head")),
    )
    out_specs = (P(("role", "head"), "seq"), P(("role", "head"), "seq"))
    return jax.shard_map(body, mesh=mesh, in_specs=in_specs, out_specs=out_specs, check_vma=False)
```

```python
import jax
import jax.numpy as jnp
import ml_dtypes
import numpy as np
from jax import lax
from jax.experimental import pallas as pl
from jax.experimental.pallas import tpu as pltpu
from jax.sharding import PartitionSpec as P

WINDOW = 4096
SHARD = 128
ROW = 8
GROUP = 4
BACK = WINDOW // (ROW * SHARD)
SHARDS = 64
HALF = 72
NEG = -1e30
LOG2E = 1.4426950408889634


def transform_tables():
    length = 2 * SHARDS * SHARD
    k1 = np.arange(HALF)[:, None]
    live = (k1 <= SHARDS).astype(np.float64)
    a = np.arange(SHARDS)[None, :]
    angle = 2.0 * np.pi * ((k1 * a) % 128) / 128
    first = np.concatenate([live * np.cos(angle), -live * np.sin(angle)], 0)
    weight = live * np.where((k1 == 0) | (k1 == SHARDS), 1.0, 2.0) / length
    last = np.concatenate([weight * np.cos(angle), -weight * np.sin(angle)], 0).T
    b = np.arange(128)[None, :]
    turn = 2.0 * np.pi * (k1 * b) / length
    b2 = np.arange(128)[:, None]
    grid = 2.0 * np.pi * ((b2 * b) % 128) / 128
    cosine, sine = np.cos(grid), np.sin(grid)
    forward = np.block([[cosine, -sine], [sine, cosine]])
    backward = np.block([[cosine, sine], [-sine, cosine]])
    tables = [np.asarray(t, np.float32) for t in (np.cos(turn), np.sin(turn))]
    for table, axis in ((first, 1), (last, 1), (forward, 0), (backward, 0)):
        high = np.asarray(table, ml_dtypes.bfloat16)
        low = np.asarray(table - high.astype(np.float64), ml_dtypes.bfloat16)
        tables.append(np.concatenate([high, high, low], axis))
    return tables


def triple(x, axis):
    high = x.astype(jnp.bfloat16)
    low = (x - high.astype(jnp.float32)).astype(jnp.bfloat16)
    return jnp.concatenate([high, low, high], axis)


def table_times(table, x):
    return jnp.dot(table, triple(x, 0), preferred_element_type=jnp.float32)


def times_table(x, table):
    return jnp.dot(triple(x, 1), table, preferred_element_type=jnp.float32)


def to_spectra(signals, first, turn_cos, turn_sin, forward):
    stacked = table_times(first, jnp.concatenate(signals, 1))
    rows = []
    for n in range(len(signals)):
        re = stacked[:HALF, n * 128 : (n + 1) * 128]
        im = stacked[HALF:, n * 128 : (n + 1) * 128]
        rows.append(jnp.concatenate([re * turn_cos + im * turn_sin, im * turn_cos - re * turn_sin], 1))
    spectra = times_table(jnp.concatenate(rows, 0), forward)
    return [spectra[n * HALF : (n + 1) * HALF] for n in range(len(signals))]


def to_signals(spectra, last, turn_cos, turn_sin, backward):
    rows = times_table(jnp.concatenate(spectra, 0), backward)
    columns = []
    for n in range(len(spectra)):
        re = rows[n * HALF : (n + 1) * HALF, :128]
        im = rows[n * HALF : (n + 1) * HALF, 128:]
        columns.append(jnp.concatenate([re * turn_cos - im * turn_sin, re * turn_sin + im * turn_cos], 0))
    return table_times(last, jnp.concatenate(columns, 1))


def product(a, b):
    ar, ai, br, bi = a[:, :128], a[:, 128:], b[:, :128], b[:, 128:]
    return jnp.concatenate([ar * br - ai * bi, ar * bi + ai * br], 1)


def product_conj(a, b):
    ar, ai, br, bi = a[:, :128], a[:, 128:], b[:, :128], b[:, 128:]
    return jnp.concatenate([ar * br + ai * bi, ar * bi - ai * br], 1)


def repeat_kernel(key_ref, value_ref, out_ref, held, arrived, done):
    loads = []
    for m, ref in enumerate((key_ref, value_ref)):
        loads.append(pltpu.make_async_copy(ref, held.at[m], arrived.at[m]))
        loads[m].start()
    copies = []
    for m in (0, 1):
        loads[m].wait()
        for n in range(SHARDS // ROW):
            copies.append(pltpu.make_async_copy(held.at[m], out_ref.at[n, m], done.at[n, m]))
            copies[-1].start()
    for copy in copies:
        copy.wait()


def pack_kernel(parts_ref, input_ref, gate_ref, taps_ref, out_ref, wide_ref):
    target = parts_ref[0].astype(jnp.float32)
    for n in range(1, 8):
        target += parts_ref[n].astype(jnp.float32)
    arrays = (target.T, input_ref[...], gate_ref[...], taps_ref[...])
    for n, array in enumerate(arrays):
        array = array.astype(jnp.float32)
        wide_ref[:, 2 * n, :] = array[:SHARDS]
        wide_ref[:, 2 * n + 1, :] = array[SHARDS:]
    out_ref[...] = wide_ref[...].astype(jnp.bfloat16)


def student_kernel(skip_ref, in_ref, tc, ts, first, last, forward, backward, out_ref, wide_in, wide_out):
    wide_in[...] = in_ref[...].astype(jnp.float32)
    rank = lax.axis_index("seq")
    skip = [skip_ref[rank], skip_ref[rank + SHARDS]]
    target, signal, gate, taps = [[wide_in[:, 2 * n + c, :] for c in (0, 1)] for n in range(4)]
    turn = tc[...], ts[...]
    ahead = first[...], *turn, forward[...]
    behind = last[...], *turn, backward[...]
    spectra = to_spectra(signal + taps, *ahead)
    conv = to_signals([product(spectra[c], spectra[2 + c]) for c in (0, 1)], *behind)
    back = []
    for c in (0, 1):
        output = gate[c] * (conv[:, c * 128 : (c + 1) * 128] + skip[c] * signal[c])
        back.append(gate[c] * (output - target[c]))
    gradient = to_spectra(back, *ahead)
    mixed = [product_conj(spectra[2 + c], gradient[c]) for c in (0, 1)]
    mixed += [product_conj(spectra[c], gradient[c]) for c in (0, 1)]
    signals = to_signals(mixed, *behind)
    scale = (SHARDS * SHARD) ** -0.5
    for c in (0, 1):
        wide_out[:, c, :] = skip[c] * back[c] + signals[:, c * 128 : (c + 1) * 128]
        wide_out[:, 2 + c, :] = scale * signals[:, (2 + c) * 128 : (3 + c) * 128]
    out_ref[...] = wide_out[...].astype(jnp.bfloat16)


def unpack_kernel(in_ref, grad_ref, step_ref, wide_ref):
    wide_ref[...] = in_ref[...].astype(jnp.float32)
    for c in (0, 1):
        grad_ref[c * SHARDS : (c + 1) * SHARDS, :] = wide_ref[:, c, :]
        step_ref[c * SHARDS : (c + 1) * SHARDS, :] = wide_ref[:, 2 + c, :]


def attend_part(query, kv_ref, row, edges, live, diagonal, before):
    scale = 128 ** -0.5
    full = [jnp.maximum(row - BACK + r, 0) for r in (1, 2, 3)]
    order = edges + full
    keys = jnp.concatenate([kv_ref[n, 0] for n in order], 0)
    values = jnp.concatenate([kv_ref[n, 1] for n in order], 0)
    values = jnp.concatenate([values, jnp.ones(values.shape, jnp.bfloat16)], 1)
    scores = lax.dot_general(query, keys, (((1,), (1,)), ((), ())), preferred_element_type=jnp.float32)
    rows = lax.broadcasted_iota(jnp.int32, (SHARD, SHARD), 0)
    columns = lax.broadcasted_iota(jnp.int32, (SHARD, SHARD), 1)
    zero = jnp.zeros((SHARD, SHARD), jnp.float32)
    spreads, tops = [], []
    for half in (0, 1):
        parts = scores[half * SHARD : (half + 1) * SHARD]
        parts = [parts[:, n * SHARD : (n + 1) * SHARD] for n in range(len(order))]
        if diagonal:
            newest = half * (SHARD // 2) + rows // 2 >= columns
            blocks = [jnp.where(newest, parts[0], jnp.where(row >= BACK, parts[1], NEG))]
        else:
            blocks = [jnp.where(live, parts[0], NEG)]
        blocks += [jnp.where(row >= BACK - r, parts[len(edges) + r - 1], NEG) for r in (1, 2, 3)]
        top = jnp.maximum(jnp.maximum(blocks[0], blocks[1]), jnp.maximum(blocks[2], blocks[3]))
        top = jnp.max(top, axis=1, keepdims=True)
        top = jnp.maximum(top, 0.5 * NEG if before is None else before[half * SHARD : (half + 1) * SHARD])
        tops.append(top)
        shift = top * (scale * LOG2E)
        weights = [jnp.exp2(b * (scale * LOG2E) - shift) for b in blocks]
        if diagonal:
            weights = [jnp.where(newest, weights[0], zero), jnp.where(newest, zero, weights[0])] + weights[1:]
        spreads.append(jnp.concatenate([w.astype(jnp.bfloat16) for w in weights], 1))
    sums = jnp.dot(jnp.concatenate(spreads, 0), values, preferred_element_type=jnp.float32)
    return jnp.concatenate(tops, 0), sums[:, :128], sums[:, 128:]


def low_lanes():
    return lax.broadcasted_iota(jnp.int32, (2 * SHARD, 128), 1) < 64


def attend_own_kernel(q_ref, kv_ref, sums_ref, stats_ref):
    rank = lax.axis_index("seq")
    row, mine = rank // ROW, rank % ROW // 2
    oldest = jnp.maximum(row - BACK, 0)
    for step in range(GROUP):
        theirs = (mine + step) % GROUP
        newer = theirs > mine
        edges = [row, oldest] if step == 0 else [jnp.where(newer, row, oldest)]
        live = jnp.logical_or(newer, row >= BACK)
        top, sums, total = attend_part(q_ref[theirs], kv_ref, row, edges, live, step == 0, None)
        sums_ref[step] = sums
        stats_ref[step] = jnp.where(low_lanes(), top, total)


def attend_sibling_kernel(q_ref, kv_ref, sums_ref, stats_ref, out_ref):
    rank = lax.axis_index("seq")
    row, mine, core = rank // ROW, rank % ROW // 2, rank % 2
    scale = 128 ** -0.5
    oldest = jnp.maximum(row - BACK, 0)
    rows = lax.broadcasted_iota(jnp.int32, (SHARD, SHARD), 0)
    columns = lax.broadcasted_iota(jnp.int32, (SHARD, SHARD), 1)
    for step in range(GROUP):
        theirs = (mine + step) % GROUP
        newer = core == 1 if step == 0 else theirs > mine
        live = jnp.logical_or(newer, row >= BACK)
        stats = stats_ref[step]
        before, total_before = stats[:, :1], stats[:, 127:]
        edges = [jnp.where(newer, row, oldest)]
        top, sums, total = attend_part(q_ref[theirs], kv_ref, row, edges, live, False, before)
        share = jnp.exp2((before - top) * (scale * LOG2E))
        total = total + share * total_before
        safe = jnp.maximum(total, 1e-30)
        out_ref[theirs, :256, :] = ((sums + share * sums_ref[step]) / safe).astype(jnp.bfloat16)
        log_sums = jnp.where(total > 0.0, top * scale + jnp.log(safe), NEG)
        stats = []
        for half in (0, 1):
            log_sum = log_sums[half * SHARD : (half + 1) * SHARD]
            log_sum = jnp.sum(jnp.where(rows == columns, log_sum, 0.0), axis=0, keepdims=True)
            high = log_sum.astype(jnp.bfloat16).astype(jnp.float32)
            rest = log_sum - high
            middle = rest.astype(jnp.bfloat16).astype(jnp.float32)
            stats += [high, middle, rest - middle]
        stats.append(jnp.zeros((10, 128), jnp.float32))
        out_ref[theirs, 256:272, :] = jnp.concatenate(stats, 0).astype(jnp.bfloat16)


def merge_kernel(parts_ref, proj_ref, out_ref, merged_ref):
    shares = []
    for half in (0, 1):
        sums = []
        for p in range(GROUP):
            stats = parts_ref[p, 256:272, :].astype(jnp.float32)
            sums.append(jnp.sum(stats[3 * half : 3 * half + 3], axis=0, keepdims=True))
        sums = jnp.concatenate(sums, 0)
        share = jnp.exp(sums - jnp.max(sums, axis=0, keepdims=True))
        shares.append(share / jnp.sum(share, axis=0, keepdims=True))
    shares.append(jnp.zeros((128 - 2 * GROUP, 128), jnp.float32))
    shares = jnp.concatenate(shares, 0).T
    for half in (0, 1):
        merged = None
        for p in range(GROUP):
            part = parts_ref[p, half * SHARD : (half + 1) * SHARD, :].astype(jnp.float32)
            part = shares[:, half * GROUP + p : half * GROUP + p + 1] * part
            merged = part if merged is None else merged + part
        merged_ref[half * SHARD : (half + 1) * SHARD, :] = merged
    attended = jnp.concatenate([merged_ref[pl.ds(h, SHARD, stride=2), :] for h in (0, 1)], 1)
    target = jnp.dot(attended.astype(jnp.bfloat16), proj_ref[...], preferred_element_type=jnp.float32)
    for n in range(8):
        out_ref[n] = target[:, n * 128 : (n + 1) * 128].astype(jnp.bfloat16)


VMEM = pl.BlockSpec(memory_space=pltpu.VMEM)
SMEM = pl.BlockSpec(memory_space=pltpu.SMEM)


def near(x):
    return pltpu.with_memory_space_constraint(x, pltpu.VMEM)


def call_repeat(key, value):
    anywhere = pl.BlockSpec(memory_space=pl.ANY)
    return pl.pallas_call(
        repeat_kernel,
        out_shape=jax.ShapeDtypeStruct((SHARDS // ROW, 2, SHARD, 128), jnp.bfloat16),
        in_specs=[anywhere] * 2,
        out_specs=anywhere,
        scratch_shapes=[
            pltpu.VMEM((2, SHARD, 128), jnp.bfloat16),
            pltpu.SemaphoreType.DMA((2,)),
            pltpu.SemaphoreType.DMA((SHARDS // ROW, 2)),
        ],
    )(key, value)


def call_pack(parts, *inputs):
    return pl.pallas_call(
        pack_kernel,
        out_shape=pltpu.VMEM((SHARDS, 8, 128), jnp.bfloat16),
        in_specs=[VMEM] * 4,
        out_specs=VMEM,
        scratch_shapes=[pltpu.VMEM((SHARDS, 8, 128), jnp.float32)],
    )(near(parts), *[near(x) for x in inputs])


def call_student(skip, packed, tables):
    return pl.pallas_call(
        student_kernel,
        out_shape=pltpu.VMEM((SHARDS, 4, 128), jnp.bfloat16),
        in_specs=[SMEM] + [VMEM] * 7,
        out_specs=VMEM,
        scratch_shapes=[pltpu.VMEM((SHARDS, 8, 128), jnp.float32), pltpu.VMEM((SHARDS, 4, 128), jnp.float32)],
    )(skip, near(packed), *tables)


def call_unpack(out):
    return pl.pallas_call(
        unpack_kernel,
        out_shape=(jax.ShapeDtypeStruct((128, 128), jnp.float32),) * 2,
        in_specs=[VMEM],
        out_specs=(VMEM,) * 2,
        scratch_shapes=[pltpu.VMEM((SHARDS, 4, 128), jnp.float32)],
    )(near(out))


def call_attend(queries, own, sibling):
    queries = near(queries)
    held = pltpu.VMEM((GROUP, 2 * SHARD, 128), jnp.float32)
    sums, stats = pl.pallas_call(
        attend_own_kernel,
        out_shape=(held, held),
        in_specs=[VMEM] * 2,
        out_specs=(VMEM,) * 2,
    )(queries, near(own))
    return pl.pallas_call(
        attend_sibling_kernel,
        out_shape=pltpu.VMEM((GROUP, 272, 128), jnp.bfloat16),
        in_specs=[VMEM] * 4,
        out_specs=VMEM,
    )(queries, near(sibling), near(sums), near(stats))


def call_merge(parts, proj):
    return pl.pallas_call(
        merge_kernel,
        out_shape=pltpu.VMEM((8, 128, 128), jnp.bfloat16),
        in_specs=[VMEM] * 2,
        out_specs=VMEM,
        scratch_shapes=[pltpu.VMEM((2 * SHARD, 128), jnp.float32)],
    )(near(parts), near(proj))


def body(
    query_heads,
    key_heads,
    value_heads,
    distill_proj,
    conv_input,
    gate_input,
    filter_taps,
    skip_gain,
):
    tables = [near(jnp.asarray(t)) for t in transform_tables()]
    lines = range(SHARDS // ROW)
    groups = [[y * ROW + 2 * x + core for x in range(GROUP)] for y in lines for core in (0, 1)]
    columns = [[y * ROW + p for y in lines] for p in range(ROW)]
    pairs = call_repeat(key_heads[:, 0], value_heads[:, 0])
    own = lax.all_to_all(pairs, "seq", 0, 0, axis_index_groups=columns)
    queries = lax.all_gather(query_heads.reshape(2 * SHARD, 128), "seq", axis_index_groups=groups)
    own, queries = lax.optimization_barrier((own, queries))
    sibling = lax.ppermute(own, "seq", [(i, i ^ 1) for i in range(SHARDS)])
    parts = call_attend(queries, own, sibling)
    parts = lax.all_to_all(parts, "seq", 0, 0, axis_index_groups=groups)
    target = call_merge(parts, distill_proj.reshape(256, 1024))
    target = lax.all_to_all(target, ("role", "head"), 0, 0)
    packed = call_pack(target, conv_input, gate_input, filter_taps)
    packed = lax.all_to_all(packed, "seq", 0, 0)
    out = call_student(skip_gain, packed, tables)
    out = lax.all_to_all(out, "seq", 0, 0)
    return call_unpack(out)


def solution(mesh):
    in_specs = (
        P("seq", ("role", "head"), None),
        P("seq", ("role", "head"), None),
        P("seq", ("role", "head"), None),
        P(("role", "head"), None, None),
        P(("role", "head"), "seq"),
        P(("role", "head"), "seq"),
        P(("role", "head"), "seq"),
        P(("role", "head")),
    )
    out_specs = (P(("role", "head"), "seq"), P(("role", "head"), "seq"))
    return jax.shard_map(body, mesh=mesh, in_specs=in_specs, out_specs=out_specs, check_vma=False)
```

```python
import jax
import jax.numpy as jnp
import ml_dtypes
import numpy as np
from jax import lax
from jax.experimental import pallas as pl
from jax.experimental.pallas import tpu as pltpu
from jax.sharding import PartitionSpec as P

WINDOW = 4096
SHARD = 128
ROW = 8
GROUP = 4
BACK = WINDOW // (ROW * SHARD)
SHARDS = 64
HALF = 72
NEG = -1e30
LOG2E = 1.4426950408889634


def transform_tables():
    length = 2 * SHARDS * SHARD
    k1 = np.arange(HALF)[:, None]
    live = (k1 <= SHARDS).astype(np.float64)
    a = np.arange(SHARDS)[None, :]
    angle = 2.0 * np.pi * ((k1 * a) % 128) / 128
    first = np.concatenate([live * np.cos(angle), -live * np.sin(angle)], 0)
    weight = live * np.where((k1 == 0) | (k1 == SHARDS), 1.0, 2.0) / length
    last = np.concatenate([weight * np.cos(angle), -weight * np.sin(angle)], 0).T
    b = np.arange(128)[None, :]
    turn = 2.0 * np.pi * (k1 * b) / length
    b2 = np.arange(128)[:, None]
    grid = 2.0 * np.pi * ((b2 * b) % 128) / 128
    cosine, sine = np.cos(grid), np.sin(grid)
    forward = np.block([[cosine, -sine], [sine, cosine]])
    backward = np.block([[cosine, sine], [-sine, cosine]])
    tables = [np.asarray(t, np.float32) for t in (np.cos(turn), np.sin(turn))]
    for table, axis in ((first, 1), (last, 1), (forward, 0), (backward, 0)):
        high = np.asarray(table, ml_dtypes.bfloat16)
        low = np.asarray(table - high.astype(np.float64), ml_dtypes.bfloat16)
        tables.append(np.concatenate([high, low, high], axis))
    return tables


def triple(x, axis):
    high = x.astype(jnp.bfloat16)
    low = (x - high.astype(jnp.float32)).astype(jnp.bfloat16)
    return jnp.concatenate([high, high, low], axis)


def table_times(table, x):
    return jnp.dot(table, triple(x, 0), preferred_element_type=jnp.float32)


def times_table(x, table):
    return jnp.dot(triple(x, 1), table, preferred_element_type=jnp.float32)


def to_spectra(signals, first, turn_cos, turn_sin, forward, exact=False):
    joined = jnp.concatenate(signals, 1)
    if exact:
        joined = joined.astype(jnp.bfloat16)
        joined = jnp.concatenate([joined, joined], 0)
        stacked = jnp.dot(first[:, : 2 * SHARDS], joined, preferred_element_type=jnp.float32)
    else:
        stacked = table_times(first, joined)
    rows = []
    for n in range(len(signals)):
        re = stacked[:HALF, n * 128 : (n + 1) * 128]
        im = stacked[HALF:, n * 128 : (n + 1) * 128]
        rows.append(jnp.concatenate([re * turn_cos + im * turn_sin, im * turn_cos - re * turn_sin], 1))
    spectra = times_table(jnp.concatenate(rows, 0), forward)
    return [spectra[n * HALF : (n + 1) * HALF] for n in range(len(signals))]


def to_signals(spectra, last, turn_cos, turn_sin, backward):
    rows = times_table(jnp.concatenate(spectra, 0), backward)
    columns = []
    for n in range(len(spectra)):
        re = rows[n * HALF : (n + 1) * HALF, :128]
        im = rows[n * HALF : (n + 1) * HALF, 128:]
        columns.append(jnp.concatenate([re * turn_cos - im * turn_sin, re * turn_sin + im * turn_cos], 0))
    return table_times(last, jnp.concatenate(columns, 1))


def product(a, b):
    ar, ai, br, bi = a[:, :128], a[:, 128:], b[:, :128], b[:, 128:]
    return jnp.concatenate([ar * br - ai * bi, ar * bi + ai * br], 1)


def product_conj(a, b):
    ar, ai, br, bi = a[:, :128], a[:, 128:], b[:, :128], b[:, 128:]
    return jnp.concatenate([ar * br + ai * bi, ar * bi - ai * br], 1)


def repeat_kernel(key_ref, value_ref, out_ref, held, arrived, done):
    loads = []
    for m, ref in enumerate((key_ref, value_ref)):
        loads.append(pltpu.make_async_copy(ref, held.at[m], arrived.at[m]))
        loads[m].start()
    copies = []
    for m in (0, 1):
        loads[m].wait()
        for n in range(SHARDS // ROW):
            copies.append(pltpu.make_async_copy(held.at[m], out_ref.at[n, m], done.at[n, m]))
            copies[-1].start()
    for copy in copies:
        copy.wait()


def pack_kernel(parts_ref, input_ref, gate_ref, taps_ref, out_ref, wide_ref):
    target = parts_ref[0].astype(jnp.float32)
    for n in range(1, 8):
        target += parts_ref[n].astype(jnp.float32)
    arrays = (target.T, input_ref[...], gate_ref[...], taps_ref[...])
    for n, array in enumerate(arrays):
        array = array.astype(jnp.float32)
        wide_ref[:, 2 * n, :] = array[:SHARDS]
        wide_ref[:, 2 * n + 1, :] = array[SHARDS:]
    out_ref[...] = wide_ref[...].astype(jnp.bfloat16)


def student_kernel(skip_ref, in_ref, tc, ts, first, last, forward, backward, out_ref, wide_out):
    wide = in_ref[...].astype(jnp.float32)
    rank = lax.axis_index("seq")
    skip = [skip_ref[rank], skip_ref[rank + SHARDS]]
    target, signal, gate, taps = [[wide[:, 2 * n + c, :] for c in (0, 1)] for n in range(4)]
    turn = tc[...], ts[...]
    ahead = first[...], *turn, forward[...]
    behind = last[...], *turn, backward[...]
    spectra = to_spectra(signal + taps, *ahead, exact=True)
    conv = to_signals([product(spectra[c], spectra[2 + c]) for c in (0, 1)], *behind)
    back = []
    for c in (0, 1):
        output = gate[c] * (conv[:, c * 128 : (c + 1) * 128] + skip[c] * signal[c])
        back.append(gate[c] * (output - target[c]))
    gradient = to_spectra(back, *ahead)
    mixed = [product_conj(spectra[2 + c], gradient[c]) for c in (0, 1)]
    mixed += [product_conj(spectra[c], gradient[c]) for c in (0, 1)]
    signals = to_signals(mixed, *behind)
    scale = (SHARDS * SHARD) ** -0.5
    for c in (0, 1):
        wide_out[:, c, :] = skip[c] * back[c] + signals[:, c * 128 : (c + 1) * 128]
        wide_out[:, 2 + c, :] = scale * signals[:, (2 + c) * 128 : (3 + c) * 128]
    out_ref[...] = wide_out[...].astype(jnp.bfloat16)


def unpack_kernel(in_ref, grad_ref, step_ref):
    wide = in_ref[...].astype(jnp.float32)
    for c in (0, 1):
        grad_ref[c * SHARDS : (c + 1) * SHARDS, :] = wide[:, c, :]
        step_ref[c * SHARDS : (c + 1) * SHARDS, :] = wide[:, 2 + c, :]


def attend_part(query, kv_ref, row, edges, live, diagonal, before):
    scale = 128 ** -0.5
    full = [jnp.maximum(row - BACK + r, 0) for r in (1, 2, 3)]
    order = edges + full
    keys = jnp.concatenate([kv_ref[n, 0] for n in order], 0)
    values = jnp.concatenate([kv_ref[n, 1] for n in order], 0)
    values = jnp.concatenate([values, jnp.ones(values.shape, jnp.bfloat16)], 1)
    scores = lax.dot_general(query, keys, (((1,), (1,)), ((), ())), preferred_element_type=jnp.float32)
    rows = lax.broadcasted_iota(jnp.int32, (SHARD, SHARD), 0)
    columns = lax.broadcasted_iota(jnp.int32, (SHARD, SHARD), 1)
    zero = jnp.zeros((SHARD, SHARD), jnp.float32)
    spreads, tops = [], []
    for half in (0, 1):
        parts = scores[half * SHARD : (half + 1) * SHARD]
        parts = [parts[:, n * SHARD : (n + 1) * SHARD] for n in range(len(order))]
        if diagonal:
            newest = half * (SHARD // 2) + rows // 2 >= columns
            blocks = [jnp.where(newest, parts[0], jnp.where(row >= BACK, parts[1], NEG))]
        else:
            blocks = [jnp.where(live, parts[0], NEG)]
        blocks += [jnp.where(row >= BACK - r, parts[len(edges) + r - 1], NEG) for r in (1, 2, 3)]
        top = jnp.maximum(jnp.maximum(blocks[0], blocks[1]), jnp.maximum(blocks[2], blocks[3]))
        top = jnp.max(top, axis=1, keepdims=True)
        top = jnp.maximum(top, 0.5 * NEG if before is None else before[half * SHARD : (half + 1) * SHARD])
        tops.append(top)
        shift = top * (scale * LOG2E)
        weights = [jnp.exp2(b * (scale * LOG2E) - shift) for b in blocks]
        if diagonal:
            weights = [jnp.where(newest, weights[0], zero), jnp.where(newest, zero, weights[0])] + weights[1:]
        spreads.append(jnp.concatenate([w.astype(jnp.bfloat16) for w in weights], 1))
    sums = jnp.dot(jnp.concatenate(spreads, 0), values, preferred_element_type=jnp.float32)
    return jnp.concatenate(tops, 0), sums[:, :128], sums[:, 128:]


def low_lanes():
    return lax.broadcasted_iota(jnp.int32, (2 * SHARD, 128), 1) < 64


def attend_own_kernel(q_ref, kv_ref, sums_ref, stats_ref):
    rank = lax.axis_index("seq")
    row, mine = rank // ROW, rank % ROW // 2
    oldest = jnp.maximum(row - BACK, 0)
    for step in range(GROUP):
        theirs = (mine + step) % GROUP
        newer = theirs > mine
        edges = [row, oldest] if step == 0 else [jnp.where(newer, row, oldest)]
        live = jnp.logical_or(newer, row >= BACK)
        top, sums, total = attend_part(q_ref[theirs], kv_ref, row, edges, live, step == 0, None)
        sums_ref[step] = sums
        stats_ref[step] = jnp.where(low_lanes(), top, total)


def attend_sibling_kernel(q_ref, kv_ref, sums_ref, stats_ref, out_ref):
    rank = lax.axis_index("seq")
    row, mine, core = rank // ROW, rank % ROW // 2, rank % 2
    scale = 128 ** -0.5
    oldest = jnp.maximum(row - BACK, 0)
    rows = lax.broadcasted_iota(jnp.int32, (SHARD, SHARD), 0)
    columns = lax.broadcasted_iota(jnp.int32, (SHARD, SHARD), 1)
    for step in range(GROUP):
        theirs = (mine + step) % GROUP
        newer = core == 1 if step == 0 else theirs > mine
        live = jnp.logical_or(newer, row >= BACK)
        stats = stats_ref[step]
        before, total_before = stats[:, :1], stats[:, 127:]
        edges = [jnp.where(newer, row, oldest)]
        top, sums, total = attend_part(q_ref[theirs], kv_ref, row, edges, live, False, before)
        share = jnp.exp2((before - top) * (scale * LOG2E))
        total = total + share * total_before
        safe = jnp.maximum(total, 1e-30)
        out_ref[theirs, :256, :] = ((sums + share * sums_ref[step]) / safe).astype(jnp.bfloat16)
        log_sums = jnp.where(total > 0.0, top * scale + jnp.log(safe), NEG)
        stats = []
        for half in (0, 1):
            log_sum = log_sums[half * SHARD : (half + 1) * SHARD]
            log_sum = jnp.sum(jnp.where(rows == columns, log_sum, 0.0), axis=0, keepdims=True)
            high = log_sum.astype(jnp.bfloat16).astype(jnp.float32)
            rest = log_sum - high
            middle = rest.astype(jnp.bfloat16).astype(jnp.float32)
            stats += [high, middle, rest - middle]
        stats.append(jnp.zeros((2, 128), jnp.float32))
        out_ref[theirs, 256:264, :] = jnp.concatenate(stats, 0).astype(jnp.bfloat16)


def merge_kernel(parts_ref, proj_ref, out_ref, merged_ref):
    shares = []
    for half in (0, 1):
        sums = []
        for p in range(GROUP):
            stats = parts_ref[p, 256:264, :].astype(jnp.float32)
            sums.append(jnp.sum(stats[3 * half : 3 * half + 3], axis=0, keepdims=True))
        sums = jnp.concatenate(sums, 0)
        share = jnp.exp(sums - jnp.max(sums, axis=0, keepdims=True))
        shares.append(share / jnp.sum(share, axis=0, keepdims=True))
    shares.append(jnp.zeros((128 - 2 * GROUP, 128), jnp.float32))
    shares = jnp.concatenate(shares, 0).T
    for half in (0, 1):
        merged = None
        for p in range(GROUP):
            part = parts_ref[p, half * SHARD : (half + 1) * SHARD, :].astype(jnp.float32)
            part = shares[:, half * GROUP + p : half * GROUP + p + 1] * part
            merged = part if merged is None else merged + part
        merged_ref[half * SHARD : (half + 1) * SHARD, :] = merged
    attended = jnp.concatenate([merged_ref[pl.ds(h, SHARD, stride=2), :] for h in (0, 1)], 1)
    target = jnp.dot(attended.astype(jnp.bfloat16), proj_ref[...], preferred_element_type=jnp.float32)
    for n in range(8):
        out_ref[n] = target[:, n * 128 : (n + 1) * 128].astype(jnp.bfloat16)


VMEM = pl.BlockSpec(memory_space=pltpu.VMEM)
SMEM = pl.BlockSpec(memory_space=pltpu.SMEM)


def near(x):
    return pltpu.with_memory_space_constraint(x, pltpu.VMEM)


def call_repeat(key, value):
    anywhere = pl.BlockSpec(memory_space=pl.ANY)
    return pl.pallas_call(
        repeat_kernel,
        out_shape=jax.ShapeDtypeStruct((SHARDS // ROW, 2, SHARD, 128), jnp.bfloat16),
        in_specs=[anywhere] * 2,
        out_specs=anywhere,
        scratch_shapes=[
            pltpu.VMEM((2, SHARD, 128), jnp.bfloat16),
            pltpu.SemaphoreType.DMA((2,)),
            pltpu.SemaphoreType.DMA((SHARDS // ROW, 2)),
        ],
    )(key, value)


def call_pack(parts, *inputs):
    return pl.pallas_call(
        pack_kernel,
        out_shape=pltpu.VMEM((SHARDS, 8, 128), jnp.bfloat16),
        in_specs=[VMEM] * 4,
        out_specs=VMEM,
        scratch_shapes=[pltpu.VMEM((SHARDS, 8, 128), jnp.float32)],
    )(near(parts), *[near(x) for x in inputs])


def call_student(skip, packed, tables):
    return pl.pallas_call(
        student_kernel,
        out_shape=pltpu.VMEM((SHARDS, 4, 128), jnp.bfloat16),
        in_specs=[SMEM] + [VMEM] * 7,
        out_specs=VMEM,
        scratch_shapes=[pltpu.VMEM((SHARDS, 4, 128), jnp.float32)],
    )(skip, near(packed), *tables)


def call_unpack(out):
    return pl.pallas_call(
        unpack_kernel,
        out_shape=(jax.ShapeDtypeStruct((128, 128), jnp.float32),) * 2,
        in_specs=[VMEM],
        out_specs=(VMEM,) * 2,
    )(near(out))


def call_attend(queries, own, sibling):
    queries = near(queries)
    held = pltpu.VMEM((GROUP, 2 * SHARD, 128), jnp.float32)
    sums, stats = pl.pallas_call(
        attend_own_kernel,
        out_shape=(held, held),
        in_specs=[VMEM] * 2,
        out_specs=(VMEM,) * 2,
    )(queries, near(own))
    return pl.pallas_call(
        attend_sibling_kernel,
        out_shape=pltpu.VMEM((GROUP, 264, 128), jnp.bfloat16),
        in_specs=[VMEM] * 4,
        out_specs=VMEM,
    )(queries, near(sibling), near(sums), near(stats))


def call_merge(parts, proj):
    return pl.pallas_call(
        merge_kernel,
        out_shape=pltpu.VMEM((8, 128, 128), jnp.bfloat16),
        in_specs=[VMEM] * 2,
        out_specs=VMEM,
        scratch_shapes=[pltpu.VMEM((2 * SHARD, 128), jnp.float32)],
    )(near(parts), near(proj))


def body(
    query_heads,
    key_heads,
    value_heads,
    distill_proj,
    conv_input,
    gate_input,
    filter_taps,
    skip_gain,
):
    tables = [near(jnp.asarray(t)) for t in transform_tables()]
    lines = range(SHARDS // ROW)
    groups = [[y * ROW + 2 * x + core for x in range(GROUP)] for y in lines for core in (0, 1)]
    columns = [[y * ROW + p for y in lines] for p in range(ROW)]
    pairs = call_repeat(key_heads[:, 0], value_heads[:, 0])
    own = lax.all_to_all(pairs, "seq", 0, 0, axis_index_groups=columns)
    queries = lax.all_gather(query_heads.reshape(2 * SHARD, 128), "seq", axis_index_groups=groups)
    own, queries = lax.optimization_barrier((own, queries))
    sibling = lax.ppermute(own, "seq", [(i, i ^ 1) for i in range(SHARDS)])
    parts = call_attend(queries, own, sibling)
    parts = lax.all_to_all(parts, "seq", 0, 0, axis_index_groups=groups)
    target = call_merge(parts, distill_proj.reshape(256, 1024))
    target = lax.all_to_all(target, ("role", "head"), 0, 0)
    packed = call_pack(target, conv_input, gate_input, filter_taps)
    packed = lax.all_to_all(packed, "seq", 0, 0)
    out = call_student(skip_gain, packed, tables)
    out = lax.all_to_all(out, "seq", 0, 0)
    return call_unpack(out)


def solution(mesh):
    in_specs = (
        P("seq", ("role", "head"), None),
        P("seq", ("role", "head"), None),
        P("seq", ("role", "head"), None),
        P(("role", "head"), None, None),
        P(("role", "head"), "seq"),
        P(("role", "head"), "seq"),
        P(("role", "head"), "seq"),
        P(("role", "head")),
    )
    out_specs = (P(("role", "head"), "seq"), P(("role", "head"), "seq"))
    return jax.shard_map(body, mesh=mesh, in_specs=in_specs, out_specs=out_specs, check_vma=False)
```

```python
import jax
import jax.numpy as jnp
import ml_dtypes
import numpy as np
from jax import lax
from jax.experimental import pallas as pl
from jax.experimental.pallas import tpu as pltpu
from jax.sharding import PartitionSpec as P

WINDOW = 4096
SHARD = 128
ROW = 8
GROUP = 4
BACK = WINDOW // (ROW * SHARD)
SHARDS = 64
HALF = 72
NEG = -1e30
LOG2E = 1.4426950408889634


def transform_tables():
    length = 2 * SHARDS * SHARD
    k1 = np.arange(HALF)[:, None]
    live = (k1 <= SHARDS).astype(np.float64)
    a = np.arange(SHARDS)[None, :]
    angle = 2.0 * np.pi * ((k1 * a) % 128) / 128
    first = np.concatenate([live * np.cos(angle), -live * np.sin(angle)], 0)
    weight = live * np.where((k1 == 0) | (k1 == SHARDS), 1.0, 2.0) / length
    last = np.concatenate([weight * np.cos(angle), -weight * np.sin(angle)], 0).T
    b = np.arange(128)[None, :]
    turn = 2.0 * np.pi * (k1 * b) / length
    b2 = np.arange(128)[:, None]
    grid = 2.0 * np.pi * ((b2 * b) % 128) / 128
    cosine, sine = np.cos(grid), np.sin(grid)
    forward = np.block([[cosine, -sine], [sine, cosine]])
    backward = np.block([[cosine, sine], [-sine, cosine]])
    tables = [np.asarray(t, np.float32) for t in (np.cos(turn), np.sin(turn))]
    for table, axis in ((first, 1), (last, 1), (forward, 0), (backward, 0)):
        high = np.asarray(table, ml_dtypes.bfloat16)
        low = np.asarray(table - high.astype(np.float64), ml_dtypes.bfloat16)
        tables.append(np.concatenate([high, low, high], axis))
    return tables


def triple(x, axis):
    high = x.astype(jnp.bfloat16)
    low = (x - high.astype(jnp.float32)).astype(jnp.bfloat16)
    return jnp.concatenate([high, high, low], axis)


def table_times(table, x):
    return jnp.dot(table, triple(x, 0), preferred_element_type=jnp.float32)


def times_table(x, table):
    return jnp.dot(triple(x, 1), table, preferred_element_type=jnp.float32)


def to_spectra(signals, first, turn_cos, turn_sin, forward, exact=False):
    joined = jnp.concatenate(signals, 1)
    if exact:
        joined = joined.astype(jnp.bfloat16)
        joined = jnp.concatenate([joined, joined], 0)
        stacked = jnp.dot(first[:, : 2 * SHARDS], joined, preferred_element_type=jnp.float32)
    else:
        stacked = table_times(first, joined)
    rows = []
    for n in range(len(signals)):
        re = stacked[:HALF, n * 128 : (n + 1) * 128]
        im = stacked[HALF:, n * 128 : (n + 1) * 128]
        rows.append(jnp.concatenate([re * turn_cos + im * turn_sin, im * turn_cos - re * turn_sin], 1))
    spectra = times_table(jnp.concatenate(rows, 0), forward)
    return [spectra[n * HALF : (n + 1) * HALF] for n in range(len(signals))]


def to_signals(spectra, last, turn_cos, turn_sin, backward):
    rows = times_table(jnp.concatenate(spectra, 0), backward)
    columns = []
    for n in range(len(spectra)):
        re = rows[n * HALF : (n + 1) * HALF, :128]
        im = rows[n * HALF : (n + 1) * HALF, 128:]
        columns.append(jnp.concatenate([re * turn_cos - im * turn_sin, re * turn_sin + im * turn_cos], 0))
    return table_times(last, jnp.concatenate(columns, 1))


def product(a, b):
    ar, ai, br, bi = a[:, :128], a[:, 128:], b[:, :128], b[:, 128:]
    return jnp.concatenate([ar * br - ai * bi, ar * bi + ai * br], 1)


def product_conj(a, b):
    ar, ai, br, bi = a[:, :128], a[:, 128:], b[:, :128], b[:, 128:]
    return jnp.concatenate([ar * br + ai * bi, ar * bi - ai * br], 1)


def repeat_kernel(key_ref, value_ref, out_ref, held, arrived, done):
    loads = []
    for m, ref in enumerate((key_ref, value_ref)):
        loads.append(pltpu.make_async_copy(ref, held.at[m], arrived.at[m]))
        loads[m].start()
    copies = []
    for m in (0, 1):
        loads[m].wait()
        for n in range(SHARDS // ROW):
            copies.append(pltpu.make_async_copy(held.at[m], out_ref.at[n, m], done.at[n, m]))
            copies[-1].start()
    for copy in copies:
        copy.wait()


def pack_kernel(parts_ref, input_ref, gate_ref, taps_ref, out_ref, wide_ref):
    target = parts_ref[0].astype(jnp.float32)
    for n in range(1, 8):
        target += parts_ref[n].astype(jnp.float32)
    arrays = (target.T, input_ref[...], gate_ref[...], taps_ref[...])
    for n, array in enumerate(arrays):
        array = array.astype(jnp.float32)
        wide_ref[:, 2 * n, :] = array[:SHARDS]
        wide_ref[:, 2 * n + 1, :] = array[SHARDS:]
    out_ref[...] = wide_ref[...].astype(jnp.bfloat16)


def student_kernel(skip_ref, in_ref, tc, ts, first, last, forward, backward, out_ref, wide_out):
    wide = in_ref[...].astype(jnp.float32)
    rank = lax.axis_index("seq")
    skip = [skip_ref[rank], skip_ref[rank + SHARDS]]
    target, signal, gate, taps = [[wide[:, 2 * n + c, :] for c in (0, 1)] for n in range(4)]
    turn = tc[...], ts[...]
    ahead = first[...], *turn, forward[...]
    behind = last[...], *turn, backward[...]
    spectra = to_spectra(signal + taps, *ahead, exact=True)
    conv = to_signals([product(spectra[c], spectra[2 + c]) for c in (0, 1)], *behind)
    back = []
    for c in (0, 1):
        output = gate[c] * (conv[:, c * 128 : (c + 1) * 128] + skip[c] * signal[c])
        back.append(gate[c] * (output - target[c]))
    gradient = to_spectra(back, *ahead)
    mixed = [product_conj(spectra[2 + c], gradient[c]) for c in (0, 1)]
    mixed += [product_conj(spectra[c], gradient[c]) for c in (0, 1)]
    signals = to_signals(mixed, *behind)
    scale = (SHARDS * SHARD) ** -0.5
    for c in (0, 1):
        wide_out[:, c, :] = skip[c] * back[c] + signals[:, c * 128 : (c + 1) * 128]
        wide_out[:, 2 + c, :] = scale * signals[:, (2 + c) * 128 : (3 + c) * 128]
    out_ref[...] = wide_out[...].astype(jnp.bfloat16)


def unpack_kernel(in_ref, grad_ref, step_ref):
    wide = in_ref[...].astype(jnp.float32)
    for c in (0, 1):
        grad_ref[c * SHARDS : (c + 1) * SHARDS, :] = wide[:, c, :]
        step_ref[c * SHARDS : (c + 1) * SHARDS, :] = wide[:, 2 + c, :]


def attend_part(query, kv_ref, row, edges, live, diagonal, before):
    scale = 128 ** -0.5
    full = [jnp.maximum(row - BACK + r, 0) for r in (1, 2, 3)]
    order = edges + full
    keys = jnp.concatenate([kv_ref[n, 0] for n in order], 0)
    values = jnp.concatenate([kv_ref[n, 1] for n in order], 0)
    values = jnp.concatenate([values, jnp.ones(values.shape, jnp.bfloat16)], 1)
    scores = lax.dot_general(query, keys, (((1,), (1,)), ((), ())), preferred_element_type=jnp.float32)
    rows = lax.broadcasted_iota(jnp.int32, (SHARD, SHARD), 0)
    columns = lax.broadcasted_iota(jnp.int32, (SHARD, SHARD), 1)
    zero = jnp.zeros((SHARD, SHARD), jnp.float32)
    spreads, tops = [], []
    for half in (0, 1):
        parts = scores[half * SHARD : (half + 1) * SHARD]
        parts = [parts[:, n * SHARD : (n + 1) * SHARD] for n in range(len(order))]
        if diagonal:
            newest = half * (SHARD // 2) + rows // 2 >= columns
            blocks = [jnp.where(newest, parts[0], jnp.where(row >= BACK, parts[1], NEG))]
        else:
            blocks = [jnp.where(live, parts[0], NEG)]
        blocks += [jnp.where(row >= BACK - r, parts[len(edges) + r - 1], NEG) for r in (1, 2, 3)]
        top = jnp.maximum(jnp.maximum(blocks[0], blocks[1]), jnp.maximum(blocks[2], blocks[3]))
        top = jnp.max(top, axis=1, keepdims=True)
        top = jnp.maximum(top, 0.5 * NEG if before is None else before[half * SHARD : (half + 1) * SHARD])
        tops.append(top)
        shift = top * (scale * LOG2E)
        weights = [jnp.exp2(b * (scale * LOG2E) - shift) for b in blocks]
        if diagonal:
            weights = [jnp.where(newest, weights[0], zero), jnp.where(newest, zero, weights[0])] + weights[1:]
        spreads.append(jnp.concatenate([w.astype(jnp.bfloat16) for w in weights], 1))
    sums = jnp.dot(jnp.concatenate(spreads, 0), values, preferred_element_type=jnp.float32)
    return jnp.concatenate(tops, 0), sums[:, :128], sums[:, 128:]


def low_lanes():
    return lax.broadcasted_iota(jnp.int32, (2 * SHARD, 128), 1) < 64


def attend_own_kernel(q_ref, kv_ref, sums_ref, stats_ref):
    rank = lax.axis_index("seq")
    row, mine = rank // ROW, rank % ROW // 2
    oldest = jnp.maximum(row - BACK, 0)
    for step in range(GROUP):
        theirs = (mine + step) % GROUP
        newer = theirs > mine
        edges = [row, oldest] if step == 0 else [jnp.where(newer, row, oldest)]
        live = jnp.logical_or(newer, row >= BACK)
        top, sums, total = attend_part(q_ref[theirs], kv_ref, row, edges, live, step == 0, None)
        sums_ref[theirs] = sums
        stats_ref[theirs] = jnp.where(low_lanes(), top, total)


def attend_sibling_kernel(q_ref, kv_ref, sums_ref, stats_ref, out_ref):
    rank = lax.axis_index("seq")
    row, mine, core = rank // ROW, rank % ROW // 2, rank % 2
    scale = 128 ** -0.5
    oldest = jnp.maximum(row - BACK, 0)
    rows = lax.broadcasted_iota(jnp.int32, (SHARD, SHARD), 0)
    columns = lax.broadcasted_iota(jnp.int32, (SHARD, SHARD), 1)
    full = [jnp.maximum(row - BACK + r, 0) for r in (1, 2, 3)]
    ones = jnp.ones((SHARD, 128), jnp.bfloat16)
    keys = jnp.concatenate([kv_ref[n, 0] for n in full], 0)
    values = jnp.concatenate([jnp.concatenate([kv_ref[n, 1], ones], 1) for n in full], 0)
    contract = (((1,), (1,)), ((), ()))
    queries = q_ref[...].reshape(GROUP * 2 * SHARD, 128)
    scores = lax.dot_general(queries, keys, contract, preferred_element_type=jnp.float32)
    tops, edge_sums, spreads = [], [], []
    for theirs in range(GROUP):
        newer = jnp.where(mine == theirs, core, (mine < theirs).astype(jnp.int32)) == 1
        edge = jnp.where(newer, row, oldest)
        block = lax.dot_general(q_ref[theirs], kv_ref[edge, 0], contract, preferred_element_type=jnp.float32)
        blocks = [jnp.where(jnp.logical_or(newer, row >= BACK), block, NEG)]
        part = scores[theirs * 2 * SHARD : (theirs + 1) * 2 * SHARD]
        for r in (1, 2, 3):
            blocks.append(jnp.where(row >= BACK - r, part[:, (r - 1) * SHARD : r * SHARD], NEG))
        top = jnp.maximum(jnp.maximum(blocks[0], blocks[1]), jnp.maximum(blocks[2], blocks[3]))
        top = jnp.maximum(jnp.max(top, axis=1, keepdims=True), stats_ref[theirs, :, :1])
        tops.append(top)
        shift = top * (scale * LOG2E)
        weights = [jnp.exp2(b * (scale * LOG2E) - shift).astype(jnp.bfloat16) for b in blocks]
        edge_values = jnp.concatenate([kv_ref[edge, 1], ones], 1)
        edge_sums.append(jnp.dot(weights[0], edge_values, preferred_element_type=jnp.float32))
        spreads.append(jnp.concatenate(weights[1:], 1))
    all_sums = jnp.dot(jnp.concatenate(spreads, 0), values, preferred_element_type=jnp.float32)
    for theirs in range(GROUP):
        top = tops[theirs]
        sums = all_sums[theirs * 2 * SHARD : (theirs + 1) * 2 * SHARD] + edge_sums[theirs]
        share = jnp.exp2((stats_ref[theirs, :, :1] - top) * (scale * LOG2E))
        total = sums[:, 128:] + share * stats_ref[theirs, :, 127:]
        merged = sums[:, :128] + share * sums_ref[theirs]
        out_ref[theirs, :256, :] = (merged / jnp.maximum(total, 1e-30)).astype(jnp.bfloat16)
        stats = []
        for half in (0, 1):
            part = slice(half * SHARD, (half + 1) * SHARD)
            total_row = jnp.sum(jnp.where(rows == columns, total[part], 0.0), axis=0, keepdims=True)
            top_row = jnp.sum(jnp.where(rows == columns, top[part], 0.0), axis=0, keepdims=True)
            log_sum = top_row * scale + jnp.log(jnp.maximum(total_row, 1e-30))
            log_sum = jnp.where(total_row > 0.0, log_sum, NEG)
            high = log_sum.astype(jnp.bfloat16).astype(jnp.float32)
            rest = log_sum - high
            middle = rest.astype(jnp.bfloat16).astype(jnp.float32)
            stats += [high, middle, rest - middle]
        stats.append(jnp.zeros((2, 128), jnp.float32))
        out_ref[theirs, 256:264, :] = jnp.concatenate(stats, 0).astype(jnp.bfloat16)


def merge_kernel(parts_ref, proj_ref, out_ref, merged_ref):
    shares = []
    for half in (0, 1):
        sums = []
        for p in range(GROUP):
            stats = parts_ref[p, 256:264, :].astype(jnp.float32)
            sums.append(jnp.sum(stats[3 * half : 3 * half + 3], axis=0, keepdims=True))
        sums = jnp.concatenate(sums, 0)
        share = jnp.exp(sums - jnp.max(sums, axis=0, keepdims=True))
        shares.append(share / jnp.sum(share, axis=0, keepdims=True))
    shares.append(jnp.zeros((128 - 2 * GROUP, 128), jnp.float32))
    shares = jnp.concatenate(shares, 0).T
    for half in (0, 1):
        merged = None
        for p in range(GROUP):
            part = parts_ref[p, half * SHARD : (half + 1) * SHARD, :].astype(jnp.float32)
            part = shares[:, half * GROUP + p : half * GROUP + p + 1] * part
            merged = part if merged is None else merged + part
        merged_ref[half * SHARD : (half + 1) * SHARD, :] = merged
    attended = jnp.concatenate([merged_ref[pl.ds(h, SHARD, stride=2), :] for h in (0, 1)], 1)
    target = jnp.dot(attended.astype(jnp.bfloat16), proj_ref[...], preferred_element_type=jnp.float32)
    for n in range(8):
        out_ref[n] = target[:, n * 128 : (n + 1) * 128].astype(jnp.bfloat16)


VMEM = pl.BlockSpec(memory_space=pltpu.VMEM)
SMEM = pl.BlockSpec(memory_space=pltpu.SMEM)


def near(x):
    return pltpu.with_memory_space_constraint(x, pltpu.VMEM)


def call_repeat(key, value):
    anywhere = pl.BlockSpec(memory_space=pl.ANY)
    return pl.pallas_call(
        repeat_kernel,
        out_shape=jax.ShapeDtypeStruct((SHARDS // ROW, 2, SHARD, 128), jnp.bfloat16),
        in_specs=[anywhere] * 2,
        out_specs=anywhere,
        scratch_shapes=[
            pltpu.VMEM((2, SHARD, 128), jnp.bfloat16),
            pltpu.SemaphoreType.DMA((2,)),
            pltpu.SemaphoreType.DMA((SHARDS // ROW, 2)),
        ],
    )(key, value)


def call_pack(parts, *inputs):
    return pl.pallas_call(
        pack_kernel,
        out_shape=pltpu.VMEM((SHARDS, 8, 128), jnp.bfloat16),
        in_specs=[VMEM] * 4,
        out_specs=VMEM,
        scratch_shapes=[pltpu.VMEM((SHARDS, 8, 128), jnp.float32)],
    )(near(parts), *[near(x) for x in inputs])


def call_student(skip, packed, tables):
    return pl.pallas_call(
        student_kernel,
        out_shape=pltpu.VMEM((SHARDS, 4, 128), jnp.bfloat16),
        in_specs=[SMEM] + [VMEM] * 7,
        out_specs=VMEM,
        scratch_shapes=[pltpu.VMEM((SHARDS, 4, 128), jnp.float32)],
    )(skip, near(packed), *tables)


def call_unpack(out):
    return pl.pallas_call(
        unpack_kernel,
        out_shape=(jax.ShapeDtypeStruct((128, 128), jnp.float32),) * 2,
        in_specs=[VMEM],
        out_specs=(VMEM,) * 2,
    )(near(out))


def call_attend(queries, own, sibling):
    queries = near(queries)
    held = pltpu.VMEM((GROUP, 2 * SHARD, 128), jnp.float32)
    sums, stats = pl.pallas_call(
        attend_own_kernel,
        out_shape=(held, held),
        in_specs=[VMEM] * 2,
        out_specs=(VMEM,) * 2,
    )(queries, near(own))
    return pl.pallas_call(
        attend_sibling_kernel,
        out_shape=pltpu.VMEM((GROUP, 264, 128), jnp.bfloat16),
        in_specs=[VMEM] * 4,
        out_specs=VMEM,
    )(queries, near(sibling), near(sums), near(stats))


def call_merge(parts, proj):
    return pl.pallas_call(
        merge_kernel,
        out_shape=pltpu.VMEM((8, 128, 128), jnp.bfloat16),
        in_specs=[VMEM] * 2,
        out_specs=VMEM,
        scratch_shapes=[pltpu.VMEM((2 * SHARD, 128), jnp.float32)],
    )(near(parts), near(proj))


def body(
    query_heads,
    key_heads,
    value_heads,
    distill_proj,
    conv_input,
    gate_input,
    filter_taps,
    skip_gain,
):
    tables = [near(jnp.asarray(t)) for t in transform_tables()]
    lines = range(SHARDS // ROW)
    groups = [[y * ROW + 2 * x + core for x in range(GROUP)] for y in lines for core in (0, 1)]
    columns = [[y * ROW + p for y in lines] for p in range(ROW)]
    pairs = call_repeat(key_heads[:, 0], value_heads[:, 0])
    own = lax.all_to_all(pairs, "seq", 0, 0, axis_index_groups=columns)
    queries = lax.all_gather(query_heads.reshape(2 * SHARD, 128), "seq", axis_index_groups=groups)
    own, queries = lax.optimization_barrier((own, queries))
    sibling = lax.ppermute(own, "seq", [(i, i ^ 1) for i in range(SHARDS)])
    parts = call_attend(queries, own, sibling)
    parts = lax.all_to_all(parts, "seq", 0, 0, axis_index_groups=groups)
    target = call_merge(parts, distill_proj.reshape(256, 1024))
    target = lax.all_to_all(target, ("role", "head"), 0, 0)
    packed = call_pack(target, conv_input, gate_input, filter_taps)
    packed = lax.all_to_all(packed, "seq", 0, 0)
    out = call_student(skip_gain, packed, tables)
    out = lax.all_to_all(out, "seq", 0, 0)
    return call_unpack(out)


def solution(mesh):
    in_specs = (
        P("seq", ("role", "head"), None),
        P("seq", ("role", "head"), None),
        P("seq", ("role", "head"), None),
        P(("role", "head"), None, None),
        P(("role", "head"), "seq"),
        P(("role", "head"), "seq"),
        P(("role", "head"), "seq"),
        P(("role", "head")),
    )
    out_specs = (P(("role", "head"), "seq"), P(("role", "head"), "seq"))
    return jax.shard_map(body, mesh=mesh, in_specs=in_specs, out_specs=out_specs, check_vma=False)
```

```python
import jax
import jax.numpy as jnp
import ml_dtypes
import numpy as np
from jax import lax
from jax.experimental import pallas as pl
from jax.experimental.pallas import tpu as pltpu
from jax.sharding import PartitionSpec as P

WINDOW = 4096
SHARD = 128
ROW = 8
GROUP = 4
BACK = WINDOW // (ROW * SHARD)
SHARDS = 64
HALF = 72
NEG = -1e30
LOG2E = 1.4426950408889634


def transform_tables():
    length = 2 * SHARDS * SHARD
    k1 = np.arange(HALF)[:, None]
    live = (k1 <= SHARDS).astype(np.float64)
    a = np.arange(SHARDS)[None, :]
    angle = 2.0 * np.pi * ((k1 * a) % 128) / 128
    first = np.concatenate([live * np.cos(angle), -live * np.sin(angle)], 0)
    weight = live * np.where((k1 == 0) | (k1 == SHARDS), 1.0, 2.0) / length
    last = np.concatenate([weight * np.cos(angle), -weight * np.sin(angle)], 0).T
    b = np.arange(128)[None, :]
    turn = 2.0 * np.pi * (k1 * b) / length
    b2 = np.arange(128)[:, None]
    grid = 2.0 * np.pi * ((b2 * b) % 128) / 128
    cosine, sine = np.cos(grid), np.sin(grid)
    forward = np.block([[cosine, -sine], [sine, cosine]])
    backward = np.block([[cosine, sine], [-sine, cosine]])
    tables = [np.asarray(t, np.float32) for t in (np.cos(turn), np.sin(turn))]
    for table, axis in ((first, 1), (last, 1), (forward, 0), (backward, 0)):
        high = np.asarray(table, ml_dtypes.bfloat16)
        low = np.asarray(table - high.astype(np.float64), ml_dtypes.bfloat16)
        tables.append(np.concatenate([high, low, high], axis))
    return tables


def triple(x, axis):
    high = x.astype(jnp.bfloat16)
    low = (x - high.astype(jnp.float32)).astype(jnp.bfloat16)
    return jnp.concatenate([high, high, low], axis)


def table_times(table, x):
    return jnp.dot(table, triple(x, 0), preferred_element_type=jnp.float32)


def times_table(x, table):
    return jnp.dot(triple(x, 1), table, preferred_element_type=jnp.float32)


def to_spectra(signals, first, turn_cos, turn_sin, forward, exact=False):
    joined = jnp.concatenate(signals, 1)
    if exact:
        joined = joined.astype(jnp.bfloat16)
        joined = jnp.concatenate([joined, joined], 0)
        stacked = jnp.dot(first[:, : 2 * SHARDS], joined, preferred_element_type=jnp.float32)
    else:
        stacked = table_times(first, joined)
    rows = []
    for n in range(len(signals)):
        re = stacked[:HALF, n * 128 : (n + 1) * 128]
        im = stacked[HALF:, n * 128 : (n + 1) * 128]
        rows.append(jnp.concatenate([re * turn_cos + im * turn_sin, im * turn_cos - re * turn_sin], 1))
    spectra = times_table(jnp.concatenate(rows, 0), forward)
    return [spectra[n * HALF : (n + 1) * HALF] for n in range(len(signals))]


def to_signals(spectra, last, turn_cos, turn_sin, backward):
    rows = times_table(jnp.concatenate(spectra, 0), backward)
    columns = []
    for n in range(len(spectra)):
        re = rows[n * HALF : (n + 1) * HALF, :128]
        im = rows[n * HALF : (n + 1) * HALF, 128:]
        columns.append(jnp.concatenate([re * turn_cos - im * turn_sin, re * turn_sin + im * turn_cos], 0))
    return table_times(last, jnp.concatenate(columns, 1))


def product(a, b):
    ar, ai, br, bi = a[:, :128], a[:, 128:], b[:, :128], b[:, 128:]
    return jnp.concatenate([ar * br - ai * bi, ar * bi + ai * br], 1)


def product_conj(a, b):
    ar, ai, br, bi = a[:, :128], a[:, 128:], b[:, :128], b[:, 128:]
    return jnp.concatenate([ar * br + ai * bi, ar * bi - ai * br], 1)


def repeat_kernel(key_ref, value_ref, out_ref, held, arrived, done):
    loads = []
    for m, ref in enumerate((key_ref, value_ref)):
        loads.append(pltpu.make_async_copy(ref, held.at[m], arrived.at[m]))
        loads[m].start()
    copies = []
    for m in (0, 1):
        loads[m].wait()
        for n in range(SHARDS // ROW):
            copies.append(pltpu.make_async_copy(held.at[m], out_ref.at[n, m], done.at[n, m]))
            copies[-1].start()
    for copy in copies:
        copy.wait()


def pack_kernel(parts_ref, input_ref, gate_ref, taps_ref, out_ref, wide_ref):
    target = parts_ref[0].astype(jnp.float32)
    for n in range(1, 8):
        target += parts_ref[n].astype(jnp.float32)
    arrays = (target.T, input_ref[...], gate_ref[...], taps_ref[...])
    for n, array in enumerate(arrays):
        array = array.astype(jnp.float32)
        wide_ref[:, 2 * n, :] = array[:SHARDS]
        wide_ref[:, 2 * n + 1, :] = array[SHARDS:]
    out_ref[...] = wide_ref[...].astype(jnp.bfloat16)


def student_kernel(skip_ref, in_ref, tc, ts, first, last, forward, backward, out_ref, wide_out):
    wide = in_ref[...].astype(jnp.float32)
    rank = lax.axis_index("seq")
    skip = [skip_ref[rank], skip_ref[rank + SHARDS]]
    target, signal, gate, taps = [[wide[:, 2 * n + c, :] for c in (0, 1)] for n in range(4)]
    turn = tc[...], ts[...]
    ahead = first[...], *turn, forward[...]
    behind = last[...], *turn, backward[...]
    spectra = to_spectra(signal + taps, *ahead, exact=True)
    conv = to_signals([product(spectra[c], spectra[2 + c]) for c in (0, 1)], *behind)
    back = []
    for c in (0, 1):
        output = gate[c] * (conv[:, c * 128 : (c + 1) * 128] + skip[c] * signal[c])
        back.append(gate[c] * (output - target[c]))
    gradient = to_spectra(back, *ahead)
    mixed = [product_conj(spectra[2 + c], gradient[c]) for c in (0, 1)]
    mixed += [product_conj(spectra[c], gradient[c]) for c in (0, 1)]
    signals = to_signals(mixed, *behind)
    scale = (SHARDS * SHARD) ** -0.5
    for c in (0, 1):
        wide_out[:, c, :] = skip[c] * back[c] + signals[:, c * 128 : (c + 1) * 128]
        wide_out[:, 2 + c, :] = scale * signals[:, (2 + c) * 128 : (3 + c) * 128]
    out_ref[...] = wide_out[...].astype(jnp.bfloat16)


def unpack_kernel(in_ref, grad_ref, step_ref):
    wide = in_ref[...].astype(jnp.float32)
    for c in (0, 1):
        grad_ref[c * SHARDS : (c + 1) * SHARDS, :] = wide[:, c, :]
        step_ref[c * SHARDS : (c + 1) * SHARDS, :] = wide[:, 2 + c, :]


def attend_part(query, kv_ref, row, edges, live, diagonal, before):
    scale = 128 ** -0.5
    full = [jnp.maximum(row - BACK + r, 0) for r in (1, 2, 3)]
    order = edges + full
    keys = jnp.concatenate([kv_ref[n, 0] for n in order], 0)
    values = jnp.concatenate([kv_ref[n, 1] for n in order], 0)
    values = jnp.concatenate([values, jnp.ones(values.shape, jnp.bfloat16)], 1)
    scores = lax.dot_general(query, keys, (((1,), (1,)), ((), ())), preferred_element_type=jnp.float32)
    rows = lax.broadcasted_iota(jnp.int32, (SHARD, SHARD), 0)
    columns = lax.broadcasted_iota(jnp.int32, (SHARD, SHARD), 1)
    zero = jnp.zeros((SHARD, SHARD), jnp.float32)
    spreads, tops = [], []
    for half in (0, 1):
        parts = scores[half * SHARD : (half + 1) * SHARD]
        parts = [parts[:, n * SHARD : (n + 1) * SHARD] for n in range(len(order))]
        if diagonal:
            newest = half * (SHARD // 2) + rows // 2 >= columns
            blocks = [jnp.where(newest, parts[0], jnp.where(row >= BACK, parts[1], NEG))]
        else:
            blocks = [jnp.where(live, parts[0], NEG)]
        blocks += [jnp.where(row >= BACK - r, parts[len(edges) + r - 1], NEG) for r in (1, 2, 3)]
        top = jnp.maximum(jnp.maximum(blocks[0], blocks[1]), jnp.maximum(blocks[2], blocks[3]))
        top = jnp.max(top, axis=1, keepdims=True)
        top = jnp.maximum(top, 0.5 * NEG if before is None else before[half * SHARD : (half + 1) * SHARD])
        tops.append(top)
        shift = top * (scale * LOG2E)
        weights = [jnp.exp2(b * (scale * LOG2E) - shift) for b in blocks]
        if diagonal:
            weights = [jnp.where(newest, weights[0], zero), jnp.where(newest, zero, weights[0])] + weights[1:]
        spreads.append(jnp.concatenate([w.astype(jnp.bfloat16) for w in weights], 1))
    sums = jnp.dot(jnp.concatenate(spreads, 0), values, preferred_element_type=jnp.float32)
    return jnp.concatenate(tops, 0), sums[:, :128], sums[:, 128:]


def low_lanes():
    return lax.broadcasted_iota(jnp.int32, (2 * SHARD, 128), 1) < 64


def attend_own_kernel(q_ref, kv_ref, sums_ref, stats_ref):
    rank = lax.axis_index("seq")
    row, mine = rank // ROW, rank % ROW // 2
    oldest = jnp.maximum(row - BACK, 0)
    for step in range(GROUP):
        theirs = (mine + step) % GROUP
        newer = theirs > mine
        edges = [row, oldest] if step == 0 else [jnp.where(newer, row, oldest)]
        live = jnp.logical_or(newer, row >= BACK)
        top, sums, total = attend_part(q_ref[theirs], kv_ref, row, edges, live, step == 0, None)
        sums_ref[step] = sums
        stats_ref[step] = jnp.where(low_lanes(), top, total)


def attend_sibling_kernel(q_ref, kv_ref, sums_ref, stats_ref, out_ref):
    rank = lax.axis_index("seq")
    row, mine, core = rank // ROW, rank % ROW // 2, rank % 2
    scale = 128 ** -0.5
    oldest = jnp.maximum(row - BACK, 0)
    rows = lax.broadcasted_iota(jnp.int32, (SHARD, SHARD), 0)
    columns = lax.broadcasted_iota(jnp.int32, (SHARD, SHARD), 1)

    @pl.loop(0, GROUP)
    def _(step):
        theirs = (mine + step) % GROUP
        newer = jnp.where(step == 0, core, (theirs > mine).astype(jnp.int32)) == 1
        live = jnp.logical_or(newer, row >= BACK)
        stats = stats_ref[step]
        before, total_before = stats[:, :1], stats[:, 127:]
        edges = [jnp.where(newer, row, oldest)]
        top, sums, total = attend_part(q_ref[theirs], kv_ref, row, edges, live, False, before)
        share = jnp.exp2((before - top) * (scale * LOG2E))
        total = total + share * total_before
        safe = jnp.maximum(total, 1e-30)
        out_ref[theirs, :256, :] = ((sums + share * sums_ref[step]) / safe).astype(jnp.bfloat16)
        log_sums = jnp.where(total > 0.0, top * scale + jnp.log(safe), NEG)
        stats = []
        for half in (0, 1):
            log_sum = log_sums[half * SHARD : (half + 1) * SHARD]
            log_sum = jnp.sum(jnp.where(rows == columns, log_sum, 0.0), axis=0, keepdims=True)
            high = log_sum.astype(jnp.bfloat16).astype(jnp.float32)
            rest = log_sum - high
            middle = rest.astype(jnp.bfloat16).astype(jnp.float32)
            stats += [high, middle, rest - middle]
        stats.append(jnp.zeros((2, 128), jnp.float32))
        out_ref[theirs, 256:264, :] = jnp.concatenate(stats, 0).astype(jnp.bfloat16)


def merge_kernel(parts_ref, proj_ref, out_ref, merged_ref):
    shares = []
    for half in (0, 1):
        sums = []
        for p in range(GROUP):
            stats = parts_ref[p, 256:264, :].astype(jnp.float32)
            sums.append(jnp.sum(stats[3 * half : 3 * half + 3], axis=0, keepdims=True))
        sums = jnp.concatenate(sums, 0)
        share = jnp.exp(sums - jnp.max(sums, axis=0, keepdims=True))
        shares.append(share / jnp.sum(share, axis=0, keepdims=True))
    shares.append(jnp.zeros((128 - 2 * GROUP, 128), jnp.float32))
    shares = jnp.concatenate(shares, 0).T
    for half in (0, 1):
        merged = None
        for p in range(GROUP):
            part = parts_ref[p, half * SHARD : (half + 1) * SHARD, :].astype(jnp.float32)
            part = shares[:, half * GROUP + p : half * GROUP + p + 1] * part
            merged = part if merged is None else merged + part
        merged_ref[half * SHARD : (half + 1) * SHARD, :] = merged
    attended = jnp.concatenate([merged_ref[pl.ds(h, SHARD, stride=2), :] for h in (0, 1)], 1)
    target = jnp.dot(attended.astype(jnp.bfloat16), proj_ref[...], preferred_element_type=jnp.float32)
    for n in range(8):
        out_ref[n] = target[:, n * 128 : (n + 1) * 128].astype(jnp.bfloat16)


VMEM = pl.BlockSpec(memory_space=pltpu.VMEM)
SMEM = pl.BlockSpec(memory_space=pltpu.SMEM)


def near(x):
    return pltpu.with_memory_space_constraint(x, pltpu.VMEM)


def call_repeat(key, value):
    anywhere = pl.BlockSpec(memory_space=pl.ANY)
    return pl.pallas_call(
        repeat_kernel,
        out_shape=jax.ShapeDtypeStruct((SHARDS // ROW, 2, SHARD, 128), jnp.bfloat16),
        in_specs=[anywhere] * 2,
        out_specs=anywhere,
        scratch_shapes=[
            pltpu.VMEM((2, SHARD, 128), jnp.bfloat16),
            pltpu.SemaphoreType.DMA((2,)),
            pltpu.SemaphoreType.DMA((SHARDS // ROW, 2)),
        ],
    )(key, value)


def call_pack(parts, *inputs):
    return pl.pallas_call(
        pack_kernel,
        out_shape=pltpu.VMEM((SHARDS, 8, 128), jnp.bfloat16),
        in_specs=[VMEM] * 4,
        out_specs=VMEM,
        scratch_shapes=[pltpu.VMEM((SHARDS, 8, 128), jnp.float32)],
    )(near(parts), *[near(x) for x in inputs])


def call_student(skip, packed, tables):
    return pl.pallas_call(
        student_kernel,
        out_shape=pltpu.VMEM((SHARDS, 4, 128), jnp.bfloat16),
        in_specs=[SMEM] + [VMEM] * 7,
        out_specs=VMEM,
        scratch_shapes=[pltpu.VMEM((SHARDS, 4, 128), jnp.float32)],
    )(skip, near(packed), *tables)


def call_unpack(out):
    return pl.pallas_call(
        unpack_kernel,
        out_shape=(jax.ShapeDtypeStruct((128, 128), jnp.float32),) * 2,
        in_specs=[VMEM],
        out_specs=(VMEM,) * 2,
    )(near(out))


def call_attend(queries, own, sibling):
    queries = near(queries)
    held = pltpu.VMEM((GROUP, 2 * SHARD, 128), jnp.float32)
    sums, stats = pl.pallas_call(
        attend_own_kernel,
        out_shape=(held, held),
        in_specs=[VMEM] * 2,
        out_specs=(VMEM,) * 2,
    )(queries, near(own))
    return pl.pallas_call(
        attend_sibling_kernel,
        out_shape=pltpu.VMEM((GROUP, 264, 128), jnp.bfloat16),
        in_specs=[VMEM] * 4,
        out_specs=VMEM,
    )(queries, near(sibling), near(sums), near(stats))


def call_merge(parts, proj):
    return pl.pallas_call(
        merge_kernel,
        out_shape=pltpu.VMEM((8, 128, 128), jnp.bfloat16),
        in_specs=[VMEM] * 2,
        out_specs=VMEM,
        scratch_shapes=[pltpu.VMEM((2 * SHARD, 128), jnp.float32)],
    )(near(parts), near(proj))


def body(
    query_heads,
    key_heads,
    value_heads,
    distill_proj,
    conv_input,
    gate_input,
    filter_taps,
    skip_gain,
):
    tables = [near(jnp.asarray(t)) for t in transform_tables()]
    lines = range(SHARDS // ROW)
    groups = [[y * ROW + 2 * x + core for x in range(GROUP)] for y in lines for core in (0, 1)]
    columns = [[y * ROW + p for y in lines] for p in range(ROW)]
    pairs = call_repeat(key_heads[:, 0], value_heads[:, 0])
    own = lax.all_to_all(pairs, "seq", 0, 0, axis_index_groups=columns)
    queries = lax.all_gather(query_heads.reshape(2 * SHARD, 128), "seq", axis_index_groups=groups)
    own, queries = lax.optimization_barrier((own, queries))
    sibling = lax.ppermute(own, "seq", [(i, i ^ 1) for i in range(SHARDS)])
    parts = call_attend(queries, own, sibling)
    parts = lax.all_to_all(parts, "seq", 0, 0, axis_index_groups=groups)
    target = call_merge(parts, distill_proj.reshape(256, 1024))
    target = lax.all_to_all(target, ("role", "head"), 0, 0)
    packed = call_pack(target, conv_input, gate_input, filter_taps)
    packed = lax.all_to_all(packed, "seq", 0, 0)
    out = call_student(skip_gain, packed, tables)
    out = lax.all_to_all(out, "seq", 0, 0)
    return call_unpack(out)


def solution(mesh):
    in_specs = (
        P("seq", ("role", "head"), None),
        P("seq", ("role", "head"), None),
        P("seq", ("role", "head"), None),
        P(("role", "head"), None, None),
        P(("role", "head"), "seq"),
        P(("role", "head"), "seq"),
        P(("role", "head"), "seq"),
        P(("role", "head")),
    )
    out_specs = (P(("role", "head"), "seq"), P(("role", "head"), "seq"))
    return jax.shard_map(body, mesh=mesh, in_specs=in_specs, out_specs=out_specs, check_vma=False)
```

```python
import jax
import jax.numpy as jnp
import ml_dtypes
import numpy as np
from jax import lax
from jax.experimental import pallas as pl
from jax.experimental.pallas import tpu as pltpu
from jax.sharding import PartitionSpec as P

WINDOW = 4096
SHARD = 128
ROW = 8
GROUP = 4
BACK = WINDOW // (ROW * SHARD)
SHARDS = 64
HALF = 72
NEG = -1e30
LOG2E = 1.4426950408889634


def transform_tables():
    length = 2 * SHARDS * SHARD
    k1 = np.arange(HALF)[:, None]
    live = (k1 <= SHARDS).astype(np.float64)
    a = np.arange(SHARDS)[None, :]
    angle = 2.0 * np.pi * ((k1 * a) % 128) / 128
    first = np.concatenate([live * np.cos(angle), -live * np.sin(angle)], 0)
    weight = live * np.where((k1 == 0) | (k1 == SHARDS), 1.0, 2.0) / length
    last = np.concatenate([weight * np.cos(angle), -weight * np.sin(angle)], 0).T
    b = np.arange(128)[None, :]
    turn = 2.0 * np.pi * (k1 * b) / length
    b2 = np.arange(128)[:, None]
    grid = 2.0 * np.pi * ((b2 * b) % 128) / 128
    cosine, sine = np.cos(grid), np.sin(grid)
    forward = np.block([[cosine, -sine], [sine, cosine]])
    backward = np.block([[cosine, sine], [-sine, cosine]])
    tables = [np.asarray(t, np.float32) for t in (np.cos(turn), np.sin(turn))]
    for table, axis in ((first, 1), (last, 1), (forward, 0), (backward, 0)):
        high = np.asarray(table, ml_dtypes.bfloat16)
        low = np.asarray(table - high.astype(np.float64), ml_dtypes.bfloat16)
        tables.append(np.concatenate([high, low, high], axis))
    return tables


def triple(x, axis):
    high = x.astype(jnp.bfloat16)
    low = (x - high.astype(jnp.float32)).astype(jnp.bfloat16)
    return jnp.concatenate([high, high, low], axis)


def table_times(table, x):
    return jnp.dot(table, triple(x, 0), preferred_element_type=jnp.float32)


def times_table(x, table):
    return jnp.dot(triple(x, 1), table, preferred_element_type=jnp.float32)


def to_spectra(signals, first, turn_cos, turn_sin, forward, exact=False):
    joined = jnp.concatenate(signals, 1)
    if exact:
        joined = joined.astype(jnp.bfloat16)
        joined = jnp.concatenate([joined, joined], 0)
        stacked = jnp.dot(first[:, : 2 * SHARDS], joined, preferred_element_type=jnp.float32)
    else:
        stacked = table_times(first, joined)
    rows = []
    for n in range(len(signals)):
        re = stacked[:HALF, n * 128 : (n + 1) * 128]
        im = stacked[HALF:, n * 128 : (n + 1) * 128]
        rows.append(jnp.concatenate([re * turn_cos + im * turn_sin, im * turn_cos - re * turn_sin], 1))
    spectra = times_table(jnp.concatenate(rows, 0), forward)
    return [spectra[n * HALF : (n + 1) * HALF] for n in range(len(signals))]


def to_signals(spectra, last, turn_cos, turn_sin, backward):
    rows = times_table(jnp.concatenate(spectra, 0), backward)
    columns = []
    for n in range(len(spectra)):
        re = rows[n * HALF : (n + 1) * HALF, :128]
        im = rows[n * HALF : (n + 1) * HALF, 128:]
        columns.append(jnp.concatenate([re * turn_cos - im * turn_sin, re * turn_sin + im * turn_cos], 0))
    return table_times(last, jnp.concatenate(columns, 1))


def product(a, b):
    ar, ai, br, bi = a[:, :128], a[:, 128:], b[:, :128], b[:, 128:]
    return jnp.concatenate([ar * br - ai * bi, ar * bi + ai * br], 1)


def product_conj(a, b):
    ar, ai, br, bi = a[:, :128], a[:, 128:], b[:, :128], b[:, 128:]
    return jnp.concatenate([ar * br + ai * bi, ar * bi - ai * br], 1)


def repeat_kernel(key_ref, value_ref, out_ref, held, arrived, done):
    loads = []
    for m, ref in enumerate((key_ref, value_ref)):
        loads.append(pltpu.make_async_copy(ref, held.at[m], arrived.at[m]))
        loads[m].start()
    copies = []
    for m in (0, 1):
        loads[m].wait()
        for n in range(SHARDS // ROW):
            copies.append(pltpu.make_async_copy(held.at[m], out_ref.at[n, m], done.at[n, m]))
            copies[-1].start()
    for copy in copies:
        copy.wait()


def pack_kernel(parts_ref, input_ref, gate_ref, taps_ref, out_ref, wide_ref):
    target = parts_ref[0].astype(jnp.float32)
    for n in range(1, 8):
        target += parts_ref[n].astype(jnp.float32)
    arrays = (target.T, input_ref[...], gate_ref[...], taps_ref[...])
    for n, array in enumerate(arrays):
        array = array.astype(jnp.float32)
        wide_ref[:, 2 * n, :] = array[:SHARDS]
        wide_ref[:, 2 * n + 1, :] = array[SHARDS:]
    out_ref[...] = wide_ref[...].astype(jnp.bfloat16)


def student_kernel(skip_ref, in_ref, tc, ts, first, last, forward, backward, out_ref, wide_out):
    wide = in_ref[...].astype(jnp.float32)
    rank = lax.axis_index("seq")
    skip = [skip_ref[rank], skip_ref[rank + SHARDS]]
    target, signal, gate, taps = [[wide[:, 2 * n + c, :] for c in (0, 1)] for n in range(4)]
    turn = tc[...], ts[...]
    ahead = first[...], *turn, forward[...]
    behind = last[...], *turn, backward[...]
    spectra = to_spectra(signal + taps, *ahead, exact=True)
    conv = to_signals([product(spectra[c], spectra[2 + c]) for c in (0, 1)], *behind)
    back = []
    for c in (0, 1):
        output = gate[c] * (conv[:, c * 128 : (c + 1) * 128] + skip[c] * signal[c])
        back.append(gate[c] * (output - target[c]))
    gradient = to_spectra(back, *ahead)
    mixed = [product_conj(spectra[2 + c], gradient[c]) for c in (0, 1)]
    mixed += [product_conj(spectra[c], gradient[c]) for c in (0, 1)]
    signals = to_signals(mixed, *behind)
    scale = (SHARDS * SHARD) ** -0.5
    for c in (0, 1):
        wide_out[:, c, :] = skip[c] * back[c] + signals[:, c * 128 : (c + 1) * 128]
        wide_out[:, 2 + c, :] = scale * signals[:, (2 + c) * 128 : (3 + c) * 128]
    out_ref[...] = wide_out[...].astype(jnp.bfloat16)


def unpack_kernel(in_ref, grad_ref, step_ref):
    wide = in_ref[...].astype(jnp.float32)
    for c in (0, 1):
        grad_ref[c * SHARDS : (c + 1) * SHARDS, :] = wide[:, c, :]
        step_ref[c * SHARDS : (c + 1) * SHARDS, :] = wide[:, 2 + c, :]


def attend_part(query, kv_ref, row, edges, live, diagonal, before):
    scale = 128 ** -0.5
    full = [jnp.maximum(row - BACK + r, 0) for r in (1, 2, 3)]
    order = edges + full
    keys = jnp.concatenate([kv_ref[n, 0] for n in order], 0)
    values = jnp.concatenate([kv_ref[n, 1] for n in order], 0)
    values = jnp.concatenate([values, jnp.ones(values.shape, jnp.bfloat16)], 1)
    scores = lax.dot_general(query, keys, (((1,), (1,)), ((), ())), preferred_element_type=jnp.float32)
    rows = lax.broadcasted_iota(jnp.int32, (SHARD, SHARD), 0)
    columns = lax.broadcasted_iota(jnp.int32, (SHARD, SHARD), 1)
    zero = jnp.zeros((SHARD, SHARD), jnp.float32)
    spreads, tops = [], []
    for half in (0, 1):
        parts = scores[half * SHARD : (half + 1) * SHARD]
        parts = [parts[:, n * SHARD : (n + 1) * SHARD] for n in range(len(order))]
        if diagonal:
            newest = half * (SHARD // 2) + rows // 2 >= columns
            blocks = [jnp.where(newest, parts[0], jnp.where(row >= BACK, parts[1], NEG))]
        else:
            blocks = [jnp.where(live, parts[0], NEG)]
        blocks += [jnp.where(row >= BACK - r, parts[len(edges) + r - 1], NEG) for r in (1, 2, 3)]
        top = jnp.maximum(jnp.maximum(blocks[0], blocks[1]), jnp.maximum(blocks[2], blocks[3]))
        top = jnp.max(top, axis=1, keepdims=True)
        top = jnp.maximum(top, 0.5 * NEG if before is None else before[half * SHARD : (half + 1) * SHARD])
        tops.append(top)
        shift = top * (scale * LOG2E)
        weights = [jnp.exp2(b * (scale * LOG2E) - shift) for b in blocks]
        if diagonal:
            weights = [jnp.where(newest, weights[0], zero), jnp.where(newest, zero, weights[0])] + weights[1:]
        spreads.append(jnp.concatenate([w.astype(jnp.bfloat16) for w in weights], 1))
    sums = jnp.dot(jnp.concatenate(spreads, 0), values, preferred_element_type=jnp.float32)
    return jnp.concatenate(tops, 0), sums[:, :128], sums[:, 128:]


def low_lanes():
    return lax.broadcasted_iota(jnp.int32, (2 * SHARD, 128), 1) < 64


def attend_own_kernel(q_ref, kv_ref, sums_ref, stats_ref):
    rank = lax.axis_index("seq")
    row, mine = rank // ROW, rank % ROW // 2
    oldest = jnp.maximum(row - BACK, 0)
    for step in range(GROUP):
        theirs = (mine + step) % GROUP
        newer = theirs > mine
        edges = [row, oldest] if step == 0 else [jnp.where(newer, row, oldest)]
        live = jnp.logical_or(newer, row >= BACK)
        top, sums, total = attend_part(q_ref[theirs], kv_ref, row, edges, live, step == 0, None)
        sums_ref[step] = sums
        stats_ref[step] = jnp.where(low_lanes(), top, total)


def attend_sibling_kernel(q_ref, kv_ref, sums_ref, stats_ref, out_ref):
    rank = lax.axis_index("seq")
    row, mine, core = rank // ROW, rank % ROW // 2, rank % 2
    scale = 128 ** -0.5
    oldest = jnp.maximum(row - BACK, 0)
    rows = lax.broadcasted_iota(jnp.int32, (SHARD, SHARD), 0)
    columns = lax.broadcasted_iota(jnp.int32, (SHARD, SHARD), 1)
    for step in range(GROUP):
        theirs = (mine + step) % GROUP
        newer = core == 1 if step == 0 else theirs > mine
        live = jnp.logical_or(newer, row >= BACK)
        stats = stats_ref[step]
        before, total_before = stats[:, :1], stats[:, 127:]
        edges = [jnp.where(newer, row, oldest)]
        top, sums, total = attend_part(q_ref[theirs], kv_ref, row, edges, live, False, before)
        share = jnp.exp2((before - top) * (scale * LOG2E))
        total = total + share * total_before
        safe = jnp.maximum(total, 1e-30)
        out_ref[theirs, :256, :] = ((sums + share * sums_ref[step]) / safe).astype(jnp.bfloat16)
        stats = []
        for half in (0, 1):
            part = slice(half * SHARD, (half + 1) * SHARD)
            total_row = jnp.sum(jnp.where(rows == columns, total[part], 0.0), axis=0, keepdims=True)
            top_row = jnp.sum(jnp.where(rows == columns, top[part], 0.0), axis=0, keepdims=True)
            log_sum = top_row * scale + jnp.log(jnp.maximum(total_row, 1e-30))
            log_sum = jnp.where(total_row > 0.0, log_sum, NEG)
            high = log_sum.astype(jnp.bfloat16).astype(jnp.float32)
            rest = log_sum - high
            middle = rest.astype(jnp.bfloat16).astype(jnp.float32)
            stats += [high, middle, rest - middle]
        stats.append(jnp.zeros((2, 128), jnp.float32))
        out_ref[theirs, 256:264, :] = jnp.concatenate(stats, 0).astype(jnp.bfloat16)


def merge_kernel(parts_ref, proj_ref, out_ref, merged_ref):
    shares = []
    for half in (0, 1):
        sums = []
        for p in range(GROUP):
            stats = parts_ref[p, 256:264, :].astype(jnp.float32)
            sums.append(jnp.sum(stats[3 * half : 3 * half + 3], axis=0, keepdims=True))
        sums = jnp.concatenate(sums, 0)
        share = jnp.exp(sums - jnp.max(sums, axis=0, keepdims=True))
        shares.append(share / jnp.sum(share, axis=0, keepdims=True))
    shares.append(jnp.zeros((128 - 2 * GROUP, 128), jnp.float32))
    shares = jnp.concatenate(shares, 0).T
    for half in (0, 1):
        merged = None
        for p in range(GROUP):
            part = parts_ref[p, half * SHARD : (half + 1) * SHARD, :].astype(jnp.float32)
            part = shares[:, half * GROUP + p : half * GROUP + p + 1] * part
            merged = part if merged is None else merged + part
        merged_ref[half * SHARD : (half + 1) * SHARD, :] = merged
    attended = jnp.concatenate([merged_ref[pl.ds(h, SHARD, stride=2), :] for h in (0, 1)], 1)
    target = jnp.dot(attended.astype(jnp.bfloat16), proj_ref[...], preferred_element_type=jnp.float32)
    for n in range(8):
        out_ref[n] = target[:, n * 128 : (n + 1) * 128].astype(jnp.bfloat16)


VMEM = pl.BlockSpec(memory_space=pltpu.VMEM)
SMEM = pl.BlockSpec(memory_space=pltpu.SMEM)


def near(x):
    return pltpu.with_memory_space_constraint(x, pltpu.VMEM)


def call_repeat(key, value):
    anywhere = pl.BlockSpec(memory_space=pl.ANY)
    return pl.pallas_call(
        repeat_kernel,
        out_shape=jax.ShapeDtypeStruct((SHARDS // ROW, 2, SHARD, 128), jnp.bfloat16),
        in_specs=[anywhere] * 2,
        out_specs=anywhere,
        scratch_shapes=[
            pltpu.VMEM((2, SHARD, 128), jnp.bfloat16),
            pltpu.SemaphoreType.DMA((2,)),
            pltpu.SemaphoreType.DMA((SHARDS // ROW, 2)),
        ],
    )(key, value)


def call_pack(parts, *inputs):
    return pl.pallas_call(
        pack_kernel,
        out_shape=pltpu.VMEM((SHARDS, 8, 128), jnp.bfloat16),
        in_specs=[VMEM] * 4,
        out_specs=VMEM,
        scratch_shapes=[pltpu.VMEM((SHARDS, 8, 128), jnp.float32)],
    )(near(parts), *[near(x) for x in inputs])


def call_student(skip, packed, tables):
    return pl.pallas_call(
        student_kernel,
        out_shape=pltpu.VMEM((SHARDS, 4, 128), jnp.bfloat16),
        in_specs=[SMEM] + [VMEM] * 7,
        out_specs=VMEM,
        scratch_shapes=[pltpu.VMEM((SHARDS, 4, 128), jnp.float32)],
    )(skip, near(packed), *tables)


def call_unpack(out):
    return pl.pallas_call(
        unpack_kernel,
        out_shape=(jax.ShapeDtypeStruct((128, 128), jnp.float32),) * 2,
        in_specs=[VMEM],
        out_specs=(VMEM,) * 2,
    )(near(out))


def call_attend(queries, own, sibling):
    queries = near(queries)
    held = pltpu.VMEM((GROUP, 2 * SHARD, 128), jnp.float32)
    sums, stats = pl.pallas_call(
        attend_own_kernel,
        out_shape=(held, held),
        in_specs=[VMEM] * 2,
        out_specs=(VMEM,) * 2,
    )(queries, near(own))
    return pl.pallas_call(
        attend_sibling_kernel,
        out_shape=pltpu.VMEM((GROUP, 264, 128), jnp.bfloat16),
        in_specs=[VMEM] * 4,
        out_specs=VMEM,
    )(queries, near(sibling), near(sums), near(stats))


def call_merge(parts, proj):
    return pl.pallas_call(
        merge_kernel,
        out_shape=pltpu.VMEM((8, 128, 128), jnp.bfloat16),
        in_specs=[VMEM] * 2,
        out_specs=VMEM,
        scratch_shapes=[pltpu.VMEM((2 * SHARD, 128), jnp.float32)],
    )(near(parts), near(proj))


def body(
    query_heads,
    key_heads,
    value_heads,
    distill_proj,
    conv_input,
    gate_input,
    filter_taps,
    skip_gain,
):
    tables = [near(jnp.asarray(t)) for t in transform_tables()]
    lines = range(SHARDS // ROW)
    groups = [[y * ROW + 2 * x + core for x in range(GROUP)] for y in lines for core in (0, 1)]
    columns = [[y * ROW + p for y in lines] for p in range(ROW)]
    pairs = call_repeat(key_heads[:, 0], value_heads[:, 0])
    own = lax.all_to_all(pairs, "seq", 0, 0, axis_index_groups=columns)
    queries = lax.all_gather(query_heads.reshape(2 * SHARD, 128), "seq", axis_index_groups=groups)
    own, queries = lax.optimization_barrier((own, queries))
    sibling = lax.ppermute(own, "seq", [(i, i ^ 1) for i in range(SHARDS)])
    parts = call_attend(queries, own, sibling)
    parts = lax.all_to_all(parts, "seq", 0, 0, axis_index_groups=groups)
    target = call_merge(parts, distill_proj.reshape(256, 1024))
    target = lax.all_to_all(target, ("role", "head"), 0, 0)
    packed = call_pack(target, conv_input, gate_input, filter_taps)
    packed = lax.all_to_all(packed, "seq", 0, 0)
    out = call_student(skip_gain, packed, tables)
    out = lax.all_to_all(out, "seq", 0, 0)
    return call_unpack(out)


def solution(mesh):
    in_specs = (
        P("seq", ("role", "head"), None),
        P("seq", ("role", "head"), None),
        P("seq", ("role", "head"), None),
        P(("role", "head"), None, None),
        P(("role", "head"), "seq"),
        P(("role", "head"), "seq"),
        P(("role", "head"), "seq"),
        P(("role", "head")),
    )
    out_specs = (P(("role", "head"), "seq"), P(("role", "head"), "seq"))
    return jax.shard_map(body, mesh=mesh, in_specs=in_specs, out_specs=out_specs, check_vma=False)
```
